128 devices in a mesh: rows: 32 (over x, z, core), cols: 4 (over y).
Axes of the slice: x: 4, y: 4, z: 4, core: 2. Of those that a mesh axis runs over, the one named last changes fastest.
Arguments:
- table: bfloat16 [262144, 512], P('rows', 'cols'), may hold values from -6 to 6
- item_ids: int32 [256, 256], P(('rows', 'cols')), may hold values from 0 to 262143, as said below
- cotangent: bfloat16 [256, 256, 512], P(('rows', 'cols')), may hold values from -6 to 6
- norm_gain: float32 [512], replicated, may hold values from 0.25 to 1.75
- w_in: bfloat16 [512, 2048], replicated, may hold values from -0.25 to 0.25
- bias_in: float32 [2048], replicated, may hold values from -3 to 3
- w_out: bfloat16 [2048, 512], replicated, may hold values from -0.125 to 0.125
Outputs:
- table_grad: float32 [262144, 512], P('rows', 'cols')
- w_in_grad: float32 [512, 2048], replicated
- bias_grad: float32 [2048], replicated
- w_out_grad: float32 [2048, 512], replicated
- gain_grad: float32 [512], replicated
The draws below stay inside these ranges and needn't reach their ends.
Inputs may be any that keep to these rules, and one draw needn't show every extreme that they name: `item_ids`: within each device's 512 positions (aligned blocks of 2 sequences), at most 32 name rows of one range k * 8192 to (k + 1) * 8192 - 1; one range is named by exactly 32 positions of every device.
All inputs are finite; a program needn't handle non-finite values.
Results may differ from the reference program's by a relative error of at most 0.0051.
Values may be sent and summed in bfloat16 or wider, within the bound.
No kernel may reach another device: no remote copies, remote signals or barrier semaphores. Data moves between devices by JAX's collectives and lax.ppermute only.
A program may use at most 128 MiB of HBM per device.

```python
import math
import jax
import jax.numpy as jnp
from jax import lax

D = 512
FF = 2048
ROWS_DEV = 8192
SEQ = 256
SEQS_DEV = 2
TOK_DEV = 512
BATCH = 256
TOKENS = 65536
SHARDS = 32
VOCAB = 262144
CAP = 32


def draw_item_ids(key, part):
    key_hot = jax.random.fold_in(key, 11)
    key_blocks = jax.random.fold_in(key, 12)
    hot_range = jax.random.randint(key_hot, (), 0, SHARDS)
    n_blocks = BATCH // SEQS_DEV

    def one_block(block_key):
        key_one, key_two, key_three, key_four = jax.random.split(block_key, 4)
        others = jax.random.permutation(key_one, (SHARDS - 1) * CAP)[:TOK_DEV - CAP] // CAP
        others = others + (others >= hot_range).astype(jnp.int32)
        ranges = jnp.concatenate([jnp.full((CAP,), hot_range, jnp.int32), others.astype(jnp.int32)])
        ranges = ranges[jax.random.permutation(key_two, TOK_DEV)]
        shifts = jax.random.randint(key_three, (TOK_DEV,), 0, 5)
        offsets = jnp.right_shift(jax.random.randint(key_four, (TOK_DEV,), 0, ROWS_DEV), shifts)
        return ranges * ROWS_DEV + offsets
    keys = jax.random.split(key_blocks, n_blocks)
    return jax.vmap(one_block)(keys).reshape(BATCH, SEQ).astype(jnp.int32)


def shard_levels(stream_key, shape, pieces, least, top_value):
    level, own = 1.0, jax.random.fold_in(stream_key, 6)
    for position, parts in pieces:
        steps = jnp.exp(jax.random.uniform(jax.random.fold_in(own, position), (parts,), jnp.float32, least / len(pieces), top_value / len(pieces)))
        level = level * jnp.repeat(steps, shape[position] // parts).reshape([-1 if axis == position else 1 for axis in range(len(shape))])
    return level


def centred(stream_key, extent, spread, reach, cuts=(), kind=jnp.bfloat16):
    result = jax.random.normal(stream_key, extent, jnp.float32) * spread
    if len(cuts) > 0:
        result = shard_levels(stream_key, extent, cuts, -0.22, 0.18) * result
    return jnp.clip(result, min=-reach, max=reach).astype(kind)


def setup_inputs(seed: int = 0) -> dict:
    seeds = jax.random.split(jax.random.key(seed), 8)
    table = centred(seeds[0], (VOCAB, D), 1.0, 6.0, ((0, 32), (1, 4)))
    item_ids = draw_item_ids(jax.random.fold_in(seeds[7], 71), 0)
    cotangent = centred(seeds[2], (BATCH, SEQ, D), 1.0, 6.0, ((0, 128),))
    norm_gain = jnp.clip(1.0 + 0.15 * jax.random.normal(seeds[3], (D,), jnp.float32), 0.25, 1.75)
    w_in = centred(seeds[4], (D, FF), D ** -0.5, 0.25)
    bias_in = centred(seeds[5], (FF,), 0.5, 3.0, (), jnp.float32)
    w_out = centred(seeds[6], (FF, D), FF ** -0.5, 0.125)
    return {"table": table, "item_ids": item_ids, "cotangent": cotangent, "norm_gain": norm_gain, "w_in": w_in, "bias_in": bias_in, "w_out": w_out}


norm_eps = 1e-06
gelu_coef = 0.7978845608

def local_pass(embedded, d_out, norm_gain, w_in, bias_in, w_out):
    x_float = embedded.astype(jnp.float32)
    inv_rms = lax.rsqrt(lax.optimization_barrier(jnp.mean(x_float * x_float, axis=-1, keepdims=True)) + norm_eps)
    x_hat = x_float * inv_rms
    normed = (x_hat * norm_gain).astype(jnp.bfloat16)
    pre_act = jnp.dot(normed, w_in, preferred_element_type=jnp.float32) + bias_in
    tanh_part = jnp.tanh(gelu_coef * (pre_act + 0.044715 * pre_act * pre_act * pre_act))
    hidden = (0.5 * pre_act * (1.0 + tanh_part)).astype(jnp.bfloat16)
    d_act = lax.dot_general(d_out, w_out, (((1,), (1,)), ((), ())), preferred_element_type=jnp.float32)
    slope = 0.5 * (1.0 + tanh_part) + 0.5 * pre_act * (1.0 - tanh_part * tanh_part) * gelu_coef * (1.0 + 3.0 * 0.044715 * pre_act * pre_act)
    d_pre = d_act * slope
    d_pre_bf = d_pre.astype(jnp.bfloat16)
    g_out = lax.dot_general(hidden, d_out, (((0,), (0,)), ((), ())), preferred_element_type=jnp.float32)
    g_in = lax.dot_general(normed, d_pre_bf, (((0,), (0,)), ((), ())), preferred_element_type=jnp.float32)
    g_bias = lax.optimization_barrier(jnp.sum(d_pre, axis=0))
    d_norm = lax.dot_general(d_pre_bf, w_in, (((1,), (1,)), ((), ())), preferred_element_type=jnp.float32)
    g_gain = lax.optimization_barrier(jnp.sum(d_norm * x_hat, axis=0))
    scaled = d_norm * norm_gain
    d_embed = inv_rms * (scaled - x_hat * lax.optimization_barrier(jnp.mean(scaled * x_hat, axis=-1, keepdims=True))) + d_out.astype(jnp.float32)
    return (d_embed, g_in, g_bias, g_out, g_gain)

def reference(table, item_ids, cotangent, norm_gain, w_in, bias_in, w_out):
    block_ids = item_ids.reshape(-1, TOK_DEV).astype(jnp.int32)
    block_cot = cotangent.reshape(-1, TOK_DEV, D)

    def one_block(carry, block):
        table_acc, acc_in, acc_bias, acc_out, acc_gain = carry
        these_ids, these_cot = block
        embedded = jnp.take(table, these_ids, axis=0)
        d_embed, g_in, g_bias, g_out, g_gain = local_pass(embedded, these_cot, norm_gain, w_in, bias_in, w_out)
        table_acc = table_acc.at[these_ids].add(d_embed)
        return ((table_acc, acc_in + g_in, acc_bias + g_bias, acc_out + g_out, acc_gain + g_gain), None)
    start = (jnp.zeros((VOCAB, D), jnp.float32), jnp.zeros((D, FF), jnp.float32), jnp.zeros((FF,), jnp.float32), jnp.zeros((FF, D), jnp.float32), jnp.zeros((D,), jnp.float32))
    final, unused = lax.scan(one_block, start, (block_ids, block_cot))
    scale = 1.0 / math.sqrt(TOKENS)
    return (final[0], final[1] * scale, final[2] * scale, final[3] * scale, final[4] * scale)
```

```python
import math

import jax
import jax.numpy as jnp
from jax import lax
from jax.experimental import pallas as pl
from jax.experimental.pallas import tpu as pltpu
from jax.sharding import Mesh
from jax.sharding import PartitionSpec as P

norm_eps = 1e-06
gelu_coef = 0.7978845608
bf16 = jnp.bfloat16
f32 = jnp.float32

N_X, N_Z, N_CORE, N_Y = 4, 4, 2, 4
N_XZ = N_X * N_Z
PEERS = ("x", "z", "y")
N_PEERS = N_XZ * N_Y
EVERY = ("x", "z", "core", "y")


def swap(a):
    return lax.ppermute(a, "core", [(0, 1), (1, 0)])


def exchange(a):
    return lax.all_to_all(a, PEERS, split_axis=0, concat_axis=0, tiled=True)


def by_core(core, own, other):
    return jnp.where(core == 0, jnp.stack([own, other]), jnp.stack([other, own]))


def finish_kernel(scale, core_ref, own_ref, other_ref, out_ref, in_ref):
    step = pl.program_id(0)

    def write(ref):
        for y in range(N_Y):
            out_ref[:, y * 128 : (y + 1) * 128] = ref[0, y, :64, :].astype(f32) * scale
            for part in range(2):
                lane = (y * 2 + part) * 128
                in_ref[:, lane : lane + 128] = (
                    ref[0, y, 64 + part * 32 : 96 + part * 32, :].astype(f32) * scale
                )

    @pl.when(step == 0)
    def _():
        write(own_ref)

    @pl.when(step == 1)
    def _():
        write(other_ref)


def finish(core, own, other, scale):
    n = N_XZ
    grid_spec = pltpu.PrefetchScalarGridSpec(
        num_scalar_prefetch=1,
        grid=(2, n),
        in_specs=[
            pl.BlockSpec((1, N_Y, 128, 128), lambda s, i, c: (jnp.where(s == 0, i, n - 1), 0, 0, 0)),
            pl.BlockSpec((1, N_Y, 128, 128), lambda s, i, c: (jnp.where(s == 0, 0, i), 0, 0, 0)),
        ],
        out_specs=[
            pl.BlockSpec((64, 512), lambda s, i, c: (jnp.where(s == 0, c[0], 1 - c[0]) * n + i, 0)),
            pl.BlockSpec((32, 1024), lambda s, i, c: (i, jnp.where(s == 0, c[0], 1 - c[0]))),
        ],
    )
    return pl.pallas_call(
        lambda *refs: finish_kernel(scale, *refs),
        grid_spec=grid_spec,
        out_shape=[
            jax.ShapeDtypeStruct((2048, 512), f32),
            jax.ShapeDtypeStruct((512, 2048), f32),
        ],
        name="finish",
    )(core.reshape(1), own, other)


def local(table, item_ids, cotangent, norm_gain, w_in, bias_in, w_out):
    core = lax.axis_index("core")
    rows_dev, col_width = table.shape
    width = N_Y * col_width
    own_ids = item_ids.reshape(-1)
    n_tok = own_ids.shape[0]
    n_ranges = N_XZ * N_CORE
    capacity = max(2, 2 * n_tok // n_ranges)
    n_slots = N_XZ * capacity
    half = w_in.shape[1] // 2

    ids = by_core(core, own_ids, swap(own_ids))
    own_cot = cotangent.reshape(n_tok, width)
    d_out = by_core(core, own_cot, swap(own_cot)).reshape(2 * n_tok, width)

    owners = ids // rows_dev
    offsets = ids - owners * rows_dev
    range_ids = jnp.arange(n_ranges, dtype=jnp.int32)
    onehot = (owners[:, :, None] == range_ids).astype(bf16)
    tok_ids = jnp.arange(n_tok, dtype=jnp.int32)
    lower = (tok_ids[:, None] >= tok_ids[None, :]).astype(bf16)
    running = jnp.einsum("ts,jsr->jtr", lower, onehot, preferred_element_type=f32)
    rank = (jnp.sum(running * onehot.astype(f32), axis=2) - 1.0).astype(jnp.int32)
    slot_of = jnp.where(owners % 2 == core, (owners // 2) * capacity + rank, -1)
    slot_ids = jnp.arange(n_slots, dtype=jnp.int32)
    slot_hit = slot_of[:, :, None] == slot_ids
    wanted = jnp.sum(jnp.where(slot_hit, offsets[:, :, None], 0), axis=1)
    wanted = jnp.transpose(wanted.reshape(2, N_XZ, capacity), (1, 0, 2))
    requests = jnp.broadcast_to(
        wanted.reshape(N_XZ, 1, 2 * capacity), (N_XZ, N_Y, 2 * capacity)
    ).reshape(N_PEERS, 2 * capacity)
    asked = exchange(requests)
    looked = jnp.take(table, asked, axis=0)
    fetched = exchange(looked)
    by_slot = jnp.transpose(
        fetched.reshape(N_XZ, N_Y, 2, capacity, col_width), (2, 0, 3, 1, 4)
    ).reshape(2, n_slots, width)
    hit = slot_hit.astype(bf16)
    part = (
        jnp.einsum("jts,jsw->jtw", hit, by_slot, preferred_element_type=f32)
        .astype(bf16)
        .reshape(2 * n_tok, width)
    )
    embedded = part + swap(part)

    w_in_half = lax.dynamic_slice_in_dim(w_in, core * half, half, axis=1)
    w_out_half = lax.dynamic_slice_in_dim(w_out, core * half, half, axis=0)
    bias_half = lax.dynamic_slice_in_dim(bias_in, core * half, half, axis=0)

    x_float = embedded.astype(f32)
    inv_rms = lax.rsqrt(jnp.mean(x_float * x_float, axis=-1, keepdims=True) + norm_eps)
    x_hat = x_float * inv_rms
    normed = (x_hat * norm_gain).astype(bf16)
    pre_act = jnp.dot(normed, w_in_half, preferred_element_type=f32) + bias_half
    tanh_part = jnp.tanh(gelu_coef * (pre_act + 0.044715 * pre_act * pre_act * pre_act))
    hidden = (0.5 * pre_act * (1.0 + tanh_part)).astype(bf16)
    d_act = lax.dot_general(
        d_out, w_out_half, (((1,), (1,)), ((), ())), preferred_element_type=f32
    )
    slope = 0.5 * (1.0 + tanh_part) + 0.5 * pre_act * (1.0 - tanh_part * tanh_part) * gelu_coef * (
        1.0 + 3.0 * 0.044715 * pre_act * pre_act
    )
    d_pre = d_act * slope
    d_pre_bf = d_pre.astype(bf16)
    part_norm = lax.dot_general(
        d_pre_bf, w_in_half, (((1,), (1,)), ((), ())), preferred_element_type=f32
    )
    other_norm = swap(part_norm.astype(bf16))
    g_out = lax.dot_general(hidden, d_out, (((0,), (0,)), ((), ())), preferred_element_type=f32)
    g_in = lax.dot_general(normed, d_pre_bf, (((0,), (0,)), ((), ())), preferred_element_type=f32)
    g_bias = jnp.sum(d_pre, axis=0)
    g_gain = jnp.sum(part_norm * x_hat, axis=0)
    d_norm = part_norm + other_norm.astype(f32)
    scaled = d_norm * norm_gain
    d_embed = inv_rms * (
        scaled - x_hat * jnp.mean(scaled * x_hat, axis=-1, keepdims=True)
    ) + d_out.astype(f32)

    slot_grad = jnp.einsum(
        "jts,jtw->jsw",
        hit,
        d_embed.astype(bf16).reshape(2, n_tok, width),
        preferred_element_type=f32,
    ).astype(bf16)
    to_slots = jnp.transpose(
        slot_grad.reshape(2, N_XZ, capacity, N_Y, col_width), (1, 3, 0, 2, 4)
    ).reshape(N_PEERS, 2 * capacity, col_width)
    to_out = jnp.transpose(g_out.astype(bf16).reshape(N_XZ, 64, N_Y, 128), (0, 2, 1, 3)).reshape(
        N_PEERS, 64, 128
    )
    to_in = jnp.transpose(
        g_in.astype(bf16).reshape(N_XZ, 32, N_Y, 2, 128), (0, 2, 3, 1, 4)
    ).reshape(N_PEERS, 64, 128)
    vec = jnp.concatenate([g_bias, g_gain]).astype(bf16).reshape(1, 12, 128)
    to_vec = jnp.broadcast_to(jnp.pad(vec, ((0, 0), (0, 4), (0, 0))), (N_PEERS, 16, 128))
    arrived = exchange(jnp.concatenate([to_slots, to_out, to_in, to_vec], axis=1))

    n_grad = 2 * capacity
    summed = jnp.sum(arrived[:, n_grad:].astype(f32), axis=0)
    share = summed[:128].astype(bf16)
    gathered = exchange(jnp.broadcast_to(share[None], (N_PEERS, 128, 128)))
    table_grad = (
        jnp.zeros((rows_dev, col_width), f32)
        .at[asked.reshape(-1)]
        .add(arrived[:, :n_grad].reshape(-1, col_width).astype(f32))
    )
    scale = 1.0 / math.sqrt(n_tok * N_PEERS * N_CORE)
    vec_sum = summed[128:140].reshape(-1)
    vec_other = swap(vec_sum)
    g_bias = by_core(core, vec_sum[:half], vec_other[:half]).reshape(-1)
    g_gain = vec_sum[half:] + vec_other[half:]
    own = gathered.reshape(N_XZ, N_Y, 128, 128)
    g_out, g_in = finish(core, own, swap(own), scale)
    return (table_grad, g_in, g_bias * scale, g_out, g_gain * scale)


def solution(mesh):
    pairs = Mesh(mesh.devices.reshape(N_X, N_Z, N_CORE, N_Y), EVERY)
    rows = ("x", "z", "core")
    return jax.shard_map(
        local,
        mesh=pairs,
        in_specs=(
            P(rows, "y"),
            P(EVERY, None),
            P(EVERY, None, None),
            P(),
            P(),
            P(),
            P(),
        ),
        out_specs=(P(rows, "y"), P(), P(), P(), P()),
        check_vma=False,
    )
```

```python
import math

import jax
import jax.numpy as jnp
from jax import lax
from jax.experimental import pallas as pl
from jax.experimental.pallas import tpu as pltpu
from jax.sharding import Mesh
from jax.sharding import PartitionSpec as P

norm_eps = 1e-06
gelu_coef = 0.7978845608
bf16 = jnp.bfloat16
f32 = jnp.float32
i32 = jnp.int32

N_X, N_Z, N_CORE, N_Y = 4, 4, 2, 4
N_XZ = N_X * N_Z
PEERS = ("x", "z", "y")
N_PEERS = N_XZ * N_Y
EVERY = ("x", "z", "core", "y")

TOK = 512
D = 512
HALF = 1024
LANES = 128
CAP = 32
PAIR_CAP = 2 * CAP
N_SLOTS = N_XZ * CAP
ROWS = 8192
N_REQ = N_PEERS * PAIR_CAP
N_W = 144


def swap(a):
    return lax.ppermute(a, "core", [(0, 1), (1, 0)])


def exchange(a):
    return lax.all_to_all(a, PEERS, split_axis=0, concat_axis=0, tiled=True)


def params(mib):
    return pltpu.CompilerParams(vmem_limit_bytes=mib << 20)


def whole(shape, space=pltpu.VMEM):
    return pl.BlockSpec(shape, lambda *_: (0,) * len(shape), memory_space=space)


def gather_kernel(asked, table_ref, out_ref, wide, picked):
    step = 1024

    def widen(i, carry):
        rows = pl.ds(pl.multiple_of(i * step, step), step)
        wide[rows, :] = table_ref[rows, :].astype(f32)
        return carry

    lax.fori_loop(0, ROWS // step, widen, 0)
    unroll = 16

    def pick(i, carry):
        base = pl.multiple_of(i * unroll, unroll)
        for u in range(unroll):
            picked[pl.ds(base + u, 1), :] = wide[pl.ds(asked[base + u], 1), :]
        return carry

    lax.fori_loop(0, N_REQ // unroll, pick, 0)

    def narrow(i, carry):
        rows = pl.ds(pl.multiple_of(i * 512, 512), 512)
        out_ref[pl.ds(i * 8, 8)] = picked[rows, :].astype(bf16).reshape(8, PAIR_CAP, LANES)
        return carry

    lax.fori_loop(0, N_REQ // 512, narrow, 0)


def gather_rows(asked, table):
    return pl.pallas_call(
        gather_kernel,
        grid_spec=pltpu.PrefetchScalarGridSpec(
            num_scalar_prefetch=1,
            grid=(1,),
            in_specs=[whole((ROWS, LANES))],
            out_specs=whole((N_PEERS, PAIR_CAP, LANES)),
            scratch_shapes=[pltpu.VMEM((ROWS, LANES), f32), pltpu.VMEM((N_REQ, LANES), f32)],
        ),
        out_shape=jax.ShapeDtypeStruct((N_PEERS, PAIR_CAP, LANES), bf16),
        compiler_params=params(24),
        name="gather_rows",
    )(asked, table)


def block_kernel(
    core,
    slot_own,
    slot_other,
    got_own,
    got_other,
    cot_own,
    cot_other,
    gain_ref,
    w_in,
    bias_ref,
    w_out,
    emb_ref,
    part_ref,
    send_ref,
    w_ref,
    by_slot,
    normed_s,
    hidden_s,
    d_pre_s,
    bias_acc,
    gain_acc,
    d_out_s,
):
    for j in range(2):
        for y in range(N_Y):
            lanes = slice(y * LANES, (y + 1) * LANES)
            by_slot[j, :N_SLOTS, lanes] = got_own[:, y, j * CAP : (j + 1) * CAP, :].reshape(
                N_SLOTS, LANES
            )
            k = 1 - j
            by_slot[j, N_SLOTS:, lanes] = got_other[:, y, k * CAP : (k + 1) * CAP, :].reshape(
                N_SLOTS, LANES
            )
    d_out_s[:TOK, :] = cot_own[...]
    d_out_s[TOK:, :] = cot_other[...]
    bias_acc[...] = jnp.zeros_like(bias_acc)
    gain_acc[...] = jnp.zeros_like(gain_acc)
    gain = gain_ref[...]
    bias = bias_ref[...]
    chunk = 256
    nt = (((1,), (1,)), ((), ()))
    tn = (((0,), (0,)), ((), ()))
    slot_ids = lax.broadcasted_iota(i32, (chunk, N_SLOTS), 1)

    def one_chunk(i, carry):
        rows = pl.ds(pl.multiple_of(i * chunk, chunk), chunk)
        hit_own = (slot_own[rows, :] == slot_ids).astype(f32).astype(bf16)
        hit_other = (slot_other[rows, :] == slot_ids).astype(f32).astype(bf16)
        j = i // (TOK // chunk)
        emb = jnp.dot(hit_own, by_slot[j, :N_SLOTS, :], preferred_element_type=f32) + jnp.dot(
            hit_other, by_slot[j, N_SLOTS:, :], preferred_element_type=f32
        )
        emb_ref[rows, :] = emb.astype(bf16)
        inv_rms = lax.rsqrt(jnp.mean(emb * emb, axis=-1, keepdims=True) + norm_eps)
        x_hat = emb * inv_rms
        normed = (x_hat * gain).astype(bf16)
        normed_s[rows, :] = normed
        pre = jnp.dot(normed, w_in[...], preferred_element_type=f32) + bias
        square = pre * pre
        tanh_part = jnp.tanh(gelu_coef * (pre + 0.044715 * (square * pre)))
        gate = 0.5 * (1.0 + tanh_part)
        hidden_s[rows, :] = (pre * gate).astype(bf16)
        slope = gate + 0.5 * pre * (1.0 - tanh_part * tanh_part) * (
            gelu_coef + (gelu_coef * 3.0 * 0.044715) * square
        )
        d_act = lax.dot_general(d_out_s[rows, :], w_out[...], nt, preferred_element_type=f32)
        d_pre = d_act * slope
        d_pre_bf = d_pre.astype(bf16)
        d_pre_s[rows, :] = d_pre_bf
        bias_acc[...] += jnp.sum(d_pre.reshape(chunk // 8, 8, HALF), axis=0)
        part = lax.dot_general(d_pre_bf, w_in[...], nt, preferred_element_type=f32)
        part_ref[rows, :] = part
        send_ref[rows, :] = part.astype(bf16)
        gain_acc[...] += jnp.sum((part * x_hat).reshape(chunk // 8, 8, D), axis=0)
        return carry

    lax.fori_loop(0, 2 * TOK // chunk, one_chunk, 0)

    def one_tile(i, carry):
        cols = pl.ds(pl.multiple_of(i * 256, 256), 256)
        g_out = lax.dot_general(
            hidden_s[:, cols], d_out_s[...], tn, preferred_element_type=f32
        ).astype(bf16)
        for y in range(N_Y):
            w_ref[pl.ds(i * 4, 4), y, 0:64, :] = g_out[:, y * LANES : (y + 1) * LANES].reshape(
                4, 64, LANES
            )
        g_in = lax.dot_general(
            normed_s[...], d_pre_s[:, cols], tn, preferred_element_type=f32
        ).astype(bf16)
        for p in range(2):
            w_ref[:, i, 64 + p * 32 : 96 + p * 32, :] = g_in[
                :, p * LANES : (p + 1) * LANES
            ].reshape(N_XZ, 32, LANES)
        return carry

    lax.fori_loop(0, HALF // 256, one_tile, 0)
    g_bias = jnp.sum(bias_acc[...], axis=0, keepdims=True)
    g_gain = jnp.sum(gain_acc[...], axis=0, keepdims=True)
    pieces = [g_bias[:, r * LANES : (r + 1) * LANES] for r in range(HALF // LANES)]
    pieces += [g_gain[:, r * LANES : (r + 1) * LANES] for r in range(D // LANES)]
    pieces += [jnp.zeros((4, LANES), f32)]
    vec = jnp.concatenate(pieces, axis=0).astype(bf16)

    def one_peer(i, carry):
        for y in range(N_Y):
            w_ref[i, y, 128:144, :] = vec
        return carry

    lax.fori_loop(0, N_XZ, one_peer, 0)


def block(core, slot_own, slot_other, got_own, got_other, cot_own, cot_other, gain, w_in, bias, w_out):
    got = (N_XZ, N_Y, PAIR_CAP, LANES)
    return pl.pallas_call(
        block_kernel,
        grid_spec=pltpu.PrefetchScalarGridSpec(
            num_scalar_prefetch=1,
            grid=(1,),
            in_specs=[
                whole((2 * TOK, 1)),
                whole((2 * TOK, 1)),
                whole(got),
                whole(got),
                whole((TOK, D)),
                whole((TOK, D)),
                whole((1, D)),
                pl.BlockSpec((D, HALF), lambda i, c: (0, c[0])),
                pl.BlockSpec((1, HALF), lambda i, c: (0, c[0])),
                pl.BlockSpec((HALF, D), lambda i, c: (c[0], 0)),
            ],
            out_specs=[
                whole((2 * TOK, D)),
                whole((2 * TOK, D)),
                whole((2 * TOK, D)),
                whole((N_XZ, N_Y, N_W, LANES)),
            ],
            scratch_shapes=[
                pltpu.VMEM((2, 2 * N_SLOTS, D), bf16),
                pltpu.VMEM((2 * TOK, D), bf16),
                pltpu.VMEM((2 * TOK, HALF), bf16),
                pltpu.VMEM((2 * TOK, HALF), bf16),
                pltpu.VMEM((8, HALF), f32),
                pltpu.VMEM((8, D), f32),
                pltpu.VMEM((2 * TOK, D), bf16),
            ],
        ),
        out_shape=[
            jax.ShapeDtypeStruct((2 * TOK, D), bf16),
            jax.ShapeDtypeStruct((2 * TOK, D), f32),
            jax.ShapeDtypeStruct((2 * TOK, D), bf16),
            jax.ShapeDtypeStruct((N_XZ, N_Y, N_W, LANES), bf16),
        ],
        compiler_params=params(48),
        name="block",
    )(core, slot_own, slot_other, got_own, got_other, cot_own, cot_other, gain, w_in, bias, w_out)


def pack_kernel(slot_ref, part_ref, other_ref, emb_ref, gain_ref, cot_own, cot_other, w_ref, out_ref):
    out_ref[:, :, PAIR_CAP:, :] = w_ref[...]
    gain = gain_ref[...]
    slot_ids = lax.broadcasted_iota(i32, (N_SLOTS, TOK), 0)
    for j in range(2):
        rows = slice(j * TOK, (j + 1) * TOK)
        theirs = slice((1 - j) * TOK, (2 - j) * TOK)
        emb = emb_ref[rows, :].astype(f32)
        inv_rms = lax.rsqrt(jnp.mean(emb * emb, axis=-1, keepdims=True) + norm_eps)
        x_hat = emb * inv_rms
        scaled = (part_ref[rows, :] + other_ref[theirs, :].astype(f32)) * gain
        d_out = (cot_own if j == 0 else cot_other)[...].astype(f32)
        d_embed = (
            inv_rms * (scaled - x_hat * jnp.mean(scaled * x_hat, axis=-1, keepdims=True)) + d_out
        ).astype(bf16)
        hit = (slot_ids == slot_ref[j : j + 1, :]).astype(f32).astype(bf16)
        grads = jnp.dot(hit, d_embed, preferred_element_type=f32).astype(bf16)
        for y in range(N_Y):
            out_ref[:, y, j * CAP : (j + 1) * CAP, :] = grads[
                :, y * LANES : (y + 1) * LANES
            ].reshape(N_XZ, CAP, LANES)


def pack(slot_row, part, other, emb, gain, cot_own, cot_other, w_part):
    return pl.pallas_call(
        pack_kernel,
        out_shape=jax.ShapeDtypeStruct((N_XZ, N_Y, PAIR_CAP + N_W, LANES), bf16),
        compiler_params=params(40),
        name="pack",
    )(slot_row, part, other, emb, gain, cot_own, cot_other, w_part)


N_ACC = 2


def scatter_kernel(asked, arrived_ref, out_ref, grads, *accs):
    zero = jnp.zeros((512, LANES), f32)

    def clear(i, carry):
        rows = pl.ds(pl.multiple_of(i * 512, 512), 512)
        for acc in (out_ref,) + accs:
            acc[rows, :] = zero
        return carry

    lax.fori_loop(0, ROWS // 512, clear, 0)

    def widen(i, carry):
        rows = pl.ds(pl.multiple_of(i * 512, 512), 512)
        grads[rows, :] = arrived_ref[pl.ds(i * 8, 8)].astype(f32).reshape(512, LANES)
        return carry

    lax.fori_loop(0, N_REQ // 512, widen, 0)
    unroll = 8
    share = N_REQ // N_ACC

    def add(i, carry):
        base = pl.multiple_of(i * unroll, unroll)
        for u in range(unroll):
            for a, acc in enumerate((out_ref,) + accs):
                row = base + (a * share + u)
                at = pl.ds(asked[row], 1)
                acc[at, :] = acc[at, :] + grads[pl.ds(row, 1), :]
        return carry

    lax.fori_loop(0, share // unroll, add, 0)

    def merge(i, carry):
        rows = pl.ds(pl.multiple_of(i * 512, 512), 512)
        total = out_ref[rows, :]
        for acc in accs:
            total = total + acc[rows, :]
        out_ref[rows, :] = total
        return carry

    lax.fori_loop(0, ROWS // 512, merge, 0)


def scatter_rows(asked, arrived):
    return pl.pallas_call(
        scatter_kernel,
        grid_spec=pltpu.PrefetchScalarGridSpec(
            num_scalar_prefetch=1,
            grid=(1,),
            in_specs=[whole((N_PEERS, PAIR_CAP, LANES))],
            out_specs=whole((ROWS, LANES)),
            scratch_shapes=[pltpu.VMEM((N_REQ, LANES), f32)]
            + [pltpu.VMEM((ROWS, LANES), f32)] * (N_ACC - 1),
        ),
        out_shape=jax.ShapeDtypeStruct((ROWS, LANES), f32),
        compiler_params=params(28),
        cost_estimate=pl.CostEstimate(flops=10**10, bytes_accessed=10**7, transcendentals=0),
        name="scatter_rows",
    )(asked, arrived)


def finish_kernel(scale, core_ref, own_ref, other_ref, out_ref, in_ref):
    n = own_ref.shape[0]

    def write(ref):
        for y in range(N_Y):
            out_ref[:, y * LANES : (y + 1) * LANES] = (
                ref[:, y, :64, :].astype(f32) * scale
            ).reshape(n * 64, LANES)
            for p in range(2):
                lane = (y * 2 + p) * LANES
                in_ref[:, lane : lane + LANES] = (
                    ref[:, y, 64 + p * 32 : 96 + p * 32, :].astype(f32) * scale
                ).reshape(n * 32, LANES)

    @pl.when(pl.program_id(0) == 0)
    def _():
        write(own_ref)

    @pl.when(pl.program_id(0) == 1)
    def _():
        write(other_ref)


def finish(core, own, other, scale):
    n, wide = 4, 4

    def half_of(s, c):
        return jnp.where(s == 0, c[0], 1 - c[0])

    return pl.pallas_call(
        lambda *refs: finish_kernel(scale, *refs),
        grid_spec=pltpu.PrefetchScalarGridSpec(
            num_scalar_prefetch=1,
            grid=(2, n),
            in_specs=[
                pl.BlockSpec(
                    (wide, N_Y, 128, LANES), lambda s, i, c: (jnp.where(s == 0, i, n - 1), 0, 0, 0)
                ),
                pl.BlockSpec(
                    (wide, N_Y, 128, LANES), lambda s, i, c: (jnp.where(s == 0, 0, i), 0, 0, 0)
                ),
            ],
            out_specs=[
                pl.BlockSpec((64 * wide, D), lambda s, i, c: (half_of(s, c) * n + i, 0)),
                pl.BlockSpec((32 * wide, HALF), lambda s, i, c: (i, half_of(s, c))),
            ],
        ),
        out_shape=[
            jax.ShapeDtypeStruct((2 * HALF, D), f32),
            jax.ShapeDtypeStruct((D, 2 * HALF), f32),
        ],
        compiler_params=params(16),
        name="finish",
    )(core, own, other)


def local(table, item_ids, cotangent, norm_gain, w_in, bias_in, w_out):
    core = lax.axis_index("core").astype(i32)
    core_arr = core.reshape(1)
    own_ids = item_ids.reshape(-1)
    cot_own = cotangent.reshape(TOK, D)
    cot_other = swap(cot_own)
    ids = jnp.stack([own_ids, swap(own_ids)])

    owners = ids // ROWS
    offsets = ids - owners * ROWS
    range_ids = jnp.arange(N_XZ * N_CORE, dtype=i32)
    onehot = (owners[:, :, None] == range_ids).astype(bf16)
    tok_ids = jnp.arange(TOK, dtype=i32)
    lower = (tok_ids[:, None] >= tok_ids[None, :]).astype(bf16)
    running = jnp.einsum("ts,jsr->jtr", lower, onehot, preferred_element_type=f32)
    rank = (jnp.sum(running * onehot.astype(f32), axis=2) - 1.0).astype(i32)
    slot = (owners // 2) * CAP + rank
    is_own = owners % 2 == core
    slot_own = jnp.where(is_own, slot, -1)
    slot_other = jnp.where(is_own, -1, slot)
    slot_ids = jnp.arange(N_SLOTS, dtype=i32)
    wanted = jnp.sum(
        jnp.where(slot_own[:, :, None] == slot_ids, offsets[:, :, None], 0), axis=1
    )
    wanted = jnp.transpose(wanted.reshape(2, N_XZ, CAP), (1, 0, 2))
    requests = jnp.broadcast_to(
        wanted.reshape(N_XZ, 1, PAIR_CAP), (N_XZ, N_Y, PAIR_CAP)
    ).reshape(N_PEERS, PAIR_CAP)
    requests, cot_other, slot_own, slot_other = lax.optimization_barrier(
        (requests, cot_other, slot_own, slot_other)
    )
    asked = exchange(requests).reshape(-1)
    fetched = exchange(gather_rows(asked, table)).reshape(N_XZ, N_Y, PAIR_CAP, LANES)
    gain_row = norm_gain.reshape(1, D)
    emb, part, send, w_part = block(
        core_arr,
        slot_own.reshape(2 * TOK, 1),
        slot_other.reshape(2 * TOK, 1),
        fetched,
        swap(fetched),
        cot_own,
        cot_other,
        gain_row,
        w_in,
        bias_in.reshape(1, 2 * HALF),
        w_out,
    )
    payload = pack(slot_own, part, swap(send), emb, gain_row, cot_own, cot_other, w_part)
    arrived = exchange(payload.reshape(N_PEERS, PAIR_CAP + N_W, LANES))

    summed = jnp.sum(arrived[:, PAIR_CAP:].astype(f32), axis=0)
    share = summed[:128].astype(bf16)
    gathered = exchange(jnp.broadcast_to(share[None], (N_PEERS, 128, LANES)))
    table_grad = scatter_rows(asked, arrived)
    scale = 1.0 / math.sqrt(TOK * N_PEERS * N_CORE)
    vec_own = summed[128:140].reshape(-1)
    vec_other = swap(vec_own)
    bias_own, bias_other = vec_own[:HALF], vec_other[:HALF]
    g_bias = jnp.where(
        core == 0, jnp.stack([bias_own, bias_other]), jnp.stack([bias_other, bias_own])
    ).reshape(-1)
    g_gain = vec_own[HALF:] + vec_other[HALF:]
    own = gathered.reshape(N_XZ, N_Y, 128, LANES)
    g_out, g_in = finish(core_arr, own, swap(own), scale)
    return (table_grad, g_in, g_bias * scale, g_out, g_gain * scale)


def solution(mesh):
    pairs = Mesh(mesh.devices.reshape(N_X, N_Z, N_CORE, N_Y), EVERY)
    rows = ("x", "z", "core")
    return jax.shard_map(
        local,
        mesh=pairs,
        in_specs=(
            P(rows, "y"),
            P(EVERY, None),
            P(EVERY, None, None),
            P(),
            P(),
            P(),
            P(),
        ),
        out_specs=(P(rows, "y"), P(), P(), P(), P()),
        check_vma=False,
    )
```

```python
import math

import jax
import jax.numpy as jnp
from jax import lax
from jax.experimental import pallas as pl
from jax.experimental.pallas import tpu as pltpu
from jax.sharding import Mesh
from jax.sharding import PartitionSpec as P

norm_eps = 1e-06
gelu_coef = 0.7978845608
bf16 = jnp.bfloat16
f32 = jnp.float32
i32 = jnp.int32

N_X, N_Z, N_CORE, N_Y = 4, 4, 2, 4
N_XZ = N_X * N_Z
PEERS = ("x", "z", "y")
N_PEERS = N_XZ * N_Y
EVERY = ("x", "z", "core", "y")

TOK = 512
D = 512
HALF = 1024
LANES = 128
CAP = 32
PAIR_CAP = 2 * CAP
N_SLOTS = N_XZ * CAP
ROWS = 8192
N_REQ = N_PEERS * PAIR_CAP
N_BLOCK = 512
N_VEC = 16
N_RING = 4 * N_BLOCK + N_VEC


def swap(a):
    return lax.ppermute(a, "core", [(0, 1), (1, 0)])


def exchange(a):
    return lax.all_to_all(a, PEERS, split_axis=0, concat_axis=0, tiled=True)


def device(x, z, core, y):
    return ((x * N_Z + z) * N_CORE + core) * N_Y + y


def rings(of_core):
    found = []
    for core in range(N_CORE):
        for i in range(4):
            for j in range(4):
                at = [{"x": (k, i, j), "y": (i, k, j), "z": (i, j, k)}[of_core[core]] for k in range(4)]
                found.append([device(x, z, core, y) for x, y, z in at])
    return found


RING = (rings("xy"), rings("yz"), rings("zx"))


def along(stage, a, shift):
    pairs = [(ring[i], ring[(i + shift) % 4]) for ring in RING[stage] for i in range(4)]
    return lax.ppermute(a, EVERY, pairs)


def params(mib):
    return pltpu.CompilerParams(vmem_limit_bytes=mib << 20)


def whole(shape, space=pltpu.VMEM):
    return pl.BlockSpec(shape, lambda *_: (0,) * len(shape), memory_space=space)


def request_at(row):
    return (row // PAIR_CAP) * LANES + row % PAIR_CAP


def gather_kernel(asked, table_ref, out_ref, wide, picked):
    step = 1024

    def widen(i, carry):
        rows = pl.ds(pl.multiple_of(i * step, step), step)
        wide[rows, :] = table_ref[rows, :].astype(f32)
        return carry

    lax.fori_loop(0, ROWS // step, widen, 0)
    unroll = 16

    def pick(i, carry):
        base = pl.multiple_of(i * unroll, unroll)
        at = request_at(base)
        for u in range(unroll):
            picked[pl.ds(base + u, 1), :] = wide[pl.ds(asked[at + u], 1), :]
        return carry

    lax.fori_loop(0, N_REQ // unroll, pick, 0)

    def narrow(i, carry):
        rows = pl.ds(pl.multiple_of(i * 512, 512), 512)
        out_ref[pl.ds(i * 8, 8)] = picked[rows, :].astype(bf16).reshape(8, PAIR_CAP, LANES)
        return carry

    lax.fori_loop(0, N_REQ // 512, narrow, 0)


def gather_rows(asked, table):
    return pl.pallas_call(
        gather_kernel,
        grid_spec=pltpu.PrefetchScalarGridSpec(
            num_scalar_prefetch=1,
            grid=(1,),
            in_specs=[whole((ROWS, LANES))],
            out_specs=whole((N_PEERS, PAIR_CAP, LANES)),
            scratch_shapes=[pltpu.VMEM((ROWS, LANES), f32), pltpu.VMEM((N_REQ, LANES), f32)],
        ),
        out_shape=jax.ShapeDtypeStruct((N_PEERS, PAIR_CAP, LANES), bf16),
        compiler_params=params(24),
        name="gather_rows",
    )(asked, table)


def block_kernel(
    place,
    slot_own,
    slot_other,
    got_own,
    got_other,
    cot_own,
    cot_other,
    gain_ref,
    w_in,
    bias_ref,
    w_out,
    emb_ref,
    part_ref,
    send_ref,
    ring_0,
    ring_1,
    ring_2,
    ring_3,
    by_slot,
    normed_s,
    hidden_s,
    d_pre_s,
    bias_acc,
    gain_acc,
    d_out_s,
    gin_s,
    vec_s,
):
    ring_refs = (ring_0, ring_1, ring_2, ring_3)
    for j in range(2):
        for y in range(N_Y):
            lanes = slice(y * LANES, (y + 1) * LANES)
            by_slot[j, :N_SLOTS, lanes] = got_own[:, y, j * CAP : (j + 1) * CAP, :].reshape(
                N_SLOTS, LANES
            )
            k = 1 - j
            by_slot[j, N_SLOTS:, lanes] = got_other[:, y, k * CAP : (k + 1) * CAP, :].reshape(
                N_SLOTS, LANES
            )
    d_out_s[:TOK, :] = cot_own[...]
    d_out_s[TOK:, :] = cot_other[...]
    bias_acc[...] = jnp.zeros_like(bias_acc)
    gain_acc[...] = jnp.zeros_like(gain_acc)
    gain = gain_ref[...]
    bias = bias_ref[...]
    chunk = 256
    nt = (((1,), (1,)), ((), ()))
    tn = (((0,), (0,)), ((), ()))
    slot_ids = lax.broadcasted_iota(i32, (chunk, N_SLOTS), 1)

    def one_chunk(i, carry):
        rows = pl.ds(pl.multiple_of(i * chunk, chunk), chunk)
        hit_own = (slot_own[rows, :] == slot_ids).astype(f32).astype(bf16)
        hit_other = (slot_other[rows, :] == slot_ids).astype(f32).astype(bf16)
        j = i // (TOK // chunk)
        emb = jnp.dot(hit_own, by_slot[j, :N_SLOTS, :], preferred_element_type=f32) + jnp.dot(
            hit_other, by_slot[j, N_SLOTS:, :], preferred_element_type=f32
        )
        emb_ref[rows, :] = emb.astype(bf16)
        inv_rms = lax.rsqrt(jnp.mean(emb * emb, axis=-1, keepdims=True) + norm_eps)
        x_hat = emb * inv_rms
        normed = (x_hat * gain).astype(bf16)
        normed_s[rows, :] = normed
        pre = jnp.dot(normed, w_in[...], preferred_element_type=f32) + bias
        square = pre * pre
        tanh_part = jnp.tanh(gelu_coef * (pre + 0.044715 * (square * pre)))
        gate = 0.5 * (1.0 + tanh_part)
        hidden_s[rows, :] = (pre * gate).astype(bf16)
        slope = gate + 0.5 * pre * (1.0 - tanh_part * tanh_part) * (
            gelu_coef + (gelu_coef * 3.0 * 0.044715) * square
        )
        d_act = lax.dot_general(d_out_s[rows, :], w_out[...], nt, preferred_element_type=f32)
        d_pre = d_act * slope
        d_pre_bf = d_pre.astype(bf16)
        d_pre_s[rows, :] = d_pre_bf
        bias_acc[...] += jnp.sum(d_pre.reshape(chunk // 8, 8, HALF), axis=0)
        part = lax.dot_general(d_pre_bf, w_in[...], nt, preferred_element_type=f32)
        part_ref[rows, :] = part
        send_ref[rows, :] = part.astype(bf16)
        gain_acc[...] += jnp.sum((part * x_hat).reshape(chunk // 8, 8, D), axis=0)
        return carry

    lax.fori_loop(0, 2 * TOK // chunk, one_chunk, 0)

    def one_tile(i, carry):
        cols = pl.ds(pl.multiple_of(i * 256, 256), 256)
        gin_s[:, cols] = lax.dot_general(
            normed_s[...], d_pre_s[:, cols], tn, preferred_element_type=f32
        ).astype(bf16)
        return carry

    lax.fori_loop(0, HALF // 256, one_tile, 0)
    g_bias = jnp.sum(bias_acc[...], axis=0, keepdims=True)
    g_gain = jnp.sum(gain_acc[...], axis=0, keepdims=True)
    for r in range(HALF // LANES):
        vec_s[r : r + 1, :] = g_bias[:, r * LANES : (r + 1) * LANES]
    for r in range(D // LANES):
        vec_s[8 + r : 9 + r, :] = g_gain[:, r * LANES : (r + 1) * LANES]
    for shift, ref in enumerate(ring_refs):
        to = lax.rem(place[1] + shift, 4)
        cols = pl.ds(pl.multiple_of(to * 256, 256), 256)
        g_out = lax.dot_general(
            hidden_s[:, cols], d_out_s[...], tn, preferred_element_type=f32
        ).astype(bf16)
        for b in range(4):
            rows = pl.ds(pl.multiple_of(to * 128 + b * 32, 32), 32)
            for y in range(N_Y):
                at = b * N_BLOCK + y * 128
                ref[at : at + 64, :] = g_out[b * 64 : b * 64 + 64, y * LANES : (y + 1) * LANES]
                for p in range(2):
                    lane = (y * 2 + p) * LANES
                    ref[at + 64 + p * 32 : at + 96 + p * 32, :] = gin_s[rows, lane : lane + LANES]
        vec = [vec_s[pl.ds(to * 3 + r, 1), :] for r in range(3)] + [jnp.zeros((13, LANES), f32)]
        ref[4 * N_BLOCK :, :] = jnp.concatenate(vec, axis=0).astype(bf16)


def block(place, slot_own, slot_other, got_own, got_other, cot_own, cot_other, gain, w_in, bias, w_out):
    got = (N_XZ, N_Y, PAIR_CAP, LANES)
    return pl.pallas_call(
        block_kernel,
        grid_spec=pltpu.PrefetchScalarGridSpec(
            num_scalar_prefetch=1,
            grid=(1,),
            in_specs=[
                whole((2 * TOK, 1)),
                whole((2 * TOK, 1)),
                whole(got),
                whole(got),
                whole((TOK, D)),
                whole((TOK, D)),
                whole((1, D)),
                pl.BlockSpec((D, HALF), lambda i, c: (0, c[0])),
                pl.BlockSpec((1, HALF), lambda i, c: (0, c[0])),
                pl.BlockSpec((HALF, D), lambda i, c: (c[0], 0)),
            ],
            out_specs=[
                whole((2 * TOK, D)),
                whole((2 * TOK, D)),
                whole((2 * TOK, D)),
            ]
            + [whole((N_RING, LANES))] * 4,
            scratch_shapes=[
                pltpu.VMEM((2, 2 * N_SLOTS, D), bf16),
                pltpu.VMEM((2 * TOK, D), bf16),
                pltpu.VMEM((2 * TOK, HALF), bf16),
                pltpu.VMEM((2 * TOK, HALF), bf16),
                pltpu.VMEM((8, HALF), f32),
                pltpu.VMEM((8, D), f32),
                pltpu.VMEM((2 * TOK, D), bf16),
                pltpu.VMEM((D, HALF), bf16),
                pltpu.VMEM((16, LANES), f32),
            ],
        ),
        out_shape=[
            jax.ShapeDtypeStruct((2 * TOK, D), bf16),
            jax.ShapeDtypeStruct((2 * TOK, D), f32),
            jax.ShapeDtypeStruct((2 * TOK, D), bf16),
        ]
        + [jax.ShapeDtypeStruct((N_RING, LANES), bf16)] * 4,
        compiler_params=params(48),
        name="block",
    )(place, slot_own, slot_other, got_own, got_other, cot_own, cot_other, gain, w_in, bias, w_out)


def pack_kernel(slot_ref, part_ref, other_ref, emb_ref, gain_ref, cot_own, cot_other, out_ref):
    gain = gain_ref[...]
    slot_ids = lax.broadcasted_iota(i32, (N_SLOTS, TOK), 0)
    for j in range(2):
        rows = slice(j * TOK, (j + 1) * TOK)
        theirs = slice((1 - j) * TOK, (2 - j) * TOK)
        emb = emb_ref[rows, :].astype(f32)
        inv_rms = lax.rsqrt(jnp.mean(emb * emb, axis=-1, keepdims=True) + norm_eps)
        x_hat = emb * inv_rms
        scaled = (part_ref[rows, :] + other_ref[theirs, :].astype(f32)) * gain
        d_out = (cot_own if j == 0 else cot_other)[...].astype(f32)
        d_embed = (
            inv_rms * (scaled - x_hat * jnp.mean(scaled * x_hat, axis=-1, keepdims=True)) + d_out
        ).astype(bf16)
        hit = (slot_ids == slot_ref[j : j + 1, :]).astype(f32).astype(bf16)
        grads = jnp.dot(hit, d_embed, preferred_element_type=f32).astype(bf16)
        for y in range(N_Y):
            out_ref[:, y, j * CAP : (j + 1) * CAP, :] = grads[
                :, y * LANES : (y + 1) * LANES
            ].reshape(N_XZ, CAP, LANES)


def pack(slot_row, part, other, emb, gain, cot_own, cot_other):
    return pl.pallas_call(
        pack_kernel,
        out_shape=jax.ShapeDtypeStruct((N_XZ, N_Y, PAIR_CAP, LANES), bf16),
        compiler_params=params(32),
        cost_estimate=pl.CostEstimate(flops=2 * 10**9, bytes_accessed=10**7, transcendentals=0),
        name="pack",
    )(slot_row, part, other, emb, gain, cot_own, cot_other)


N_ACC = 2


def scatter_kernel(asked, arrived_ref, out_ref, grads, *accs):
    zero = jnp.zeros((512, LANES), f32)

    def clear(i, carry):
        rows = pl.ds(pl.multiple_of(i * 512, 512), 512)
        for acc in (out_ref,) + accs:
            acc[rows, :] = zero
        return carry

    lax.fori_loop(0, ROWS // 512, clear, 0)

    def widen(i, carry):
        rows = pl.ds(pl.multiple_of(i * 512, 512), 512)
        grads[rows, :] = arrived_ref[pl.ds(i * 8, 8)].astype(f32).reshape(512, LANES)
        return carry

    lax.fori_loop(0, N_REQ // 512, widen, 0)
    unroll = 8
    share = N_REQ // N_ACC

    def add(i, carry):
        base = pl.multiple_of(i * unroll, unroll)
        for u in range(unroll):
            for a, acc in enumerate((out_ref,) + accs):
                row = base + (a * share + u)
                at = pl.ds(asked[request_at(base) + (a * share * LANES // PAIR_CAP + u)], 1)
                acc[at, :] = acc[at, :] + grads[pl.ds(row, 1), :]
        return carry

    lax.fori_loop(0, share // unroll, add, 0)

    def merge(i, carry):
        rows = pl.ds(pl.multiple_of(i * 512, 512), 512)
        total = out_ref[rows, :]
        for acc in accs:
            total = total + acc[rows, :]
        out_ref[rows, :] = total
        return carry

    lax.fori_loop(0, ROWS // 512, merge, 0)


def scatter_rows(asked, arrived):
    return pl.pallas_call(
        scatter_kernel,
        grid_spec=pltpu.PrefetchScalarGridSpec(
            num_scalar_prefetch=1,
            grid=(1,),
            in_specs=[whole((N_PEERS, PAIR_CAP, LANES))],
            out_specs=whole((ROWS, LANES)),
            scratch_shapes=[pltpu.VMEM((N_REQ, LANES), f32)]
            + [pltpu.VMEM((ROWS, LANES), f32)] * (N_ACC - 1),
        ),
        out_shape=jax.ShapeDtypeStruct((ROWS, LANES), f32),
        compiler_params=params(28),
        cost_estimate=pl.CostEstimate(flops=10**10, bytes_accessed=10**7, transcendentals=0),
        name="scatter_rows",
    )(asked, arrived)


def ring_add(here, back_1, back_2, back_3, rows):
    first = here[rows, :].astype(f32) + back_2[rows, :].astype(f32)
    return first + (back_1[rows, :].astype(f32) + back_3[rows, :].astype(f32))


def sum_split_kernel(place, here, back_1, back_2, back_3, *outs):
    vec = ring_add(here, back_1, back_2, back_3, slice(4 * N_BLOCK, N_RING)).astype(bf16)
    for shift, out in enumerate(outs):
        to = lax.rem(place[2] + shift, 4)
        for part in range(4):
            step = N_BLOCK // 4
            rows = pl.ds(pl.multiple_of(to * N_BLOCK + part * step, step), step)
            out[part * step : (part + 1) * step, :] = ring_add(
                here, back_1, back_2, back_3, rows
            ).astype(bf16)
        out[N_BLOCK:, :] = vec


def sum_split(place, pieces):
    return pl.pallas_call(
        sum_split_kernel,
        grid_spec=pltpu.PrefetchScalarGridSpec(
            num_scalar_prefetch=1,
            grid=(1,),
            in_specs=[whole((N_RING, LANES))] * 4,
            out_specs=[whole((N_BLOCK + N_VEC, LANES))] * 4,
        ),
        out_shape=[jax.ShapeDtypeStruct((N_BLOCK + N_VEC, LANES), bf16)] * 4,
        compiler_params=params(8),
        name="sum_split",
    )(place, *pieces)


def sum_kernel(here, back_1, back_2, back_3, out):
    n = N_BLOCK + N_VEC
    for at in range(0, n, 88):
        rows = slice(at, min(at + 88, n))
        out[rows, :] = ring_add(here, back_1, back_2, back_3, rows).astype(bf16)


def sum_four(pieces):
    return pl.pallas_call(
        sum_kernel,
        out_shape=jax.ShapeDtypeStruct((N_BLOCK + N_VEC, LANES), bf16),
        compiler_params=params(4),
        name="sum_four",
    )(*pieces)


def join_kernel(here, back_1, back_2, back_3, out):
    for i, ref in enumerate((here, back_1, back_2, back_3)):
        out[i * N_BLOCK : (i + 1) * N_BLOCK, :] = ref[:N_BLOCK, :]
    out[4 * N_BLOCK :, :] = here[N_BLOCK:, :]


def join_four(pieces):
    return pl.pallas_call(
        join_kernel,
        out_shape=jax.ShapeDtypeStruct((N_RING, LANES), bf16),
        compiler_params=params(4),
        name="join_four",
    )(*pieces)


def finish_kernel(scale, place, *refs):
    pieces, (out_ref, in_ref, bias_ref, gain_ref, vec_s) = refs[:8], refs[8:]

    for s in range(8):

        @pl.when(pl.program_id(0) == s)
        def _(ref=pieces[s], s=s):
            a = lax.rem(place[1 if s < 4 else 3] + (4 - s % 4), 4)
            for j in range(4):
                b = lax.rem(place[2 if s < 4 else 4] + (4 - j), 4)
                rows_out = pl.ds(pl.multiple_of(b * 64, 64), 64)
                rows_in = pl.ds(pl.multiple_of(b * 32, 32), 32)
                for y in range(N_Y):
                    at = j * N_BLOCK + y * 128
                    out_ref[rows_out, y * LANES : (y + 1) * LANES] = (
                        ref[at : at + 64, :].astype(f32) * scale
                    )
                    for p in range(2):
                        lane = (y * 2 + p) * LANES
                        in_ref[rows_in, lane : lane + LANES] = (
                            ref[at + 64 + p * 32 : at + 96 + p * 32, :].astype(f32) * scale
                        )
            vec = ref[4 * N_BLOCK :, :].astype(f32) * scale
            for r in range(3):
                vec_s[s // 4, pl.ds(a * 3 + r, 1), :] = vec[r : r + 1, :]

    @pl.when(pl.program_id(0) == 7)
    def _():
        bias_ref[pl.ds(pl.multiple_of(place[0] * 8, 8), 8), :] = vec_s[0, :8, :]
        bias_ref[pl.ds(pl.multiple_of((1 - place[0]) * 8, 8), 8), :] = vec_s[1, :8, :]
        gain_ref[...] = vec_s[0, 8:12, :] + vec_s[1, 8:12, :]


def finish(place, pieces, scale):
    def half_of(s, c):
        return jnp.where(s < 4, c[0], 1 - c[0])

    def row_of(s, c):
        return lax.rem(jnp.where(s < 4, c[1], c[3]) + 8 - s, 4)

    return pl.pallas_call(
        lambda *refs: finish_kernel(scale, *refs),
        grid_spec=pltpu.PrefetchScalarGridSpec(
            num_scalar_prefetch=1,
            grid=(8,),
            in_specs=[whole((N_RING, LANES))] * 8,
            out_specs=[
                pl.BlockSpec((256, D), lambda s, c: (half_of(s, c) * 4 + row_of(s, c), 0)),
                pl.BlockSpec((128, HALF), lambda s, c: (row_of(s, c), half_of(s, c))),
                whole((16, LANES)),
                whole((4, LANES)),
            ],
            scratch_shapes=[pltpu.VMEM((2, 16, LANES), f32)],
        ),
        out_shape=[
            jax.ShapeDtypeStruct((2 * HALF, D), f32),
            jax.ShapeDtypeStruct((D, 2 * HALF), f32),
            jax.ShapeDtypeStruct((16, LANES), f32),
            jax.ShapeDtypeStruct((4, LANES), f32),
        ],
        compiler_params=params(16),
        name="finish",
    )(place, *pieces)


def local(table, item_ids, cotangent, norm_gain, w_in, bias_in, w_out):
    core = lax.axis_index("core").astype(i32)
    x, y, z = (lax.axis_index(name).astype(i32) for name in "xyz")
    is_first = core == 0
    place = jnp.stack(
        [
            core,
            jnp.where(is_first, x, y),
            jnp.where(is_first, y, z),
            jnp.where(is_first, y, x),
            jnp.where(is_first, z, y),
        ]
    )
    own_ids = item_ids.reshape(-1)
    cot_own = cotangent.reshape(TOK, D)
    cot_other = swap(cot_own)
    ids = jnp.stack([own_ids, swap(own_ids)])

    owners = ids // ROWS
    offsets = ids - owners * ROWS
    range_ids = jnp.arange(N_XZ * N_CORE, dtype=i32)
    onehot = (owners[:, :, None] == range_ids).astype(bf16)
    tok_ids = jnp.arange(TOK, dtype=i32)
    lower = (tok_ids[:, None] >= tok_ids[None, :]).astype(bf16)
    running = jnp.einsum("ts,jsr->jtr", lower, onehot, preferred_element_type=f32)
    rank = (jnp.sum(running * onehot.astype(f32), axis=2) - 1.0).astype(i32)
    slot = (owners // 2) * CAP + rank
    is_own = owners % 2 == core
    slot_own = jnp.where(is_own, slot, -1)
    slot_other = jnp.where(is_own, -1, slot)
    slot_ids = jnp.arange(N_SLOTS, dtype=i32)
    wanted = jnp.sum(
        jnp.where(slot_own[:, :, None] == slot_ids, offsets[:, :, None], 0), axis=1
    )
    wanted = jnp.transpose(wanted.reshape(2, N_XZ, CAP), (1, 0, 2))
    wanted = jnp.pad(wanted.reshape(N_XZ, 1, PAIR_CAP), ((0, 0), (0, 0), (0, LANES - PAIR_CAP)))
    requests = jnp.broadcast_to(wanted, (N_XZ, N_Y, LANES)).reshape(N_PEERS, 1, LANES)
    requests, cot_other, slot_own, slot_other = lax.optimization_barrier(
        (requests, cot_other, slot_own, slot_other)
    )
    asked = exchange(requests).reshape(-1)
    fetched = exchange(gather_rows(asked, table)).reshape(N_XZ, N_Y, PAIR_CAP, LANES)
    gain_row = norm_gain.reshape(1, D)
    emb, part, send, *ring = block(
        place,
        slot_own.reshape(2 * TOK, 1),
        slot_other.reshape(2 * TOK, 1),
        fetched,
        swap(fetched),
        cot_own,
        cot_other,
        gain_row,
        w_in,
        bias_in.reshape(1, 2 * HALF),
        w_out,
    )
    other = swap(send)
    split = list(sum_split(place, ring[:1] + [along(0, ring[s], s) for s in (1, 2, 3)]))
    payload = pack(slot_own, part, other, emb, gain_row, cot_own, cot_other)
    arrived = exchange(payload.reshape(N_PEERS, PAIR_CAP, LANES))
    mine = sum_four(split[:1] + [along(1, split[s], s) for s in (1, 2, 3)])
    total = sum_four([mine] + [along(2, mine, s) for s in (1, 2, 3)])
    joined = join_four([total] + [along(1, total, s) for s in (1, 2, 3)])
    pieces = [joined] + [along(0, joined, s) for s in (1, 2, 3)]
    table_grad = scatter_rows(asked, arrived)
    pieces += [swap(p) for p in pieces]
    scale = 1.0 / math.sqrt(TOK * N_PEERS * N_CORE)
    g_out, g_in, g_bias, g_gain = finish(place, pieces, scale)
    return (table_grad, g_in, g_bias.reshape(-1), g_out, g_gain.reshape(-1))


def solution(mesh):
    pairs = Mesh(mesh.devices.reshape(N_X, N_Z, N_CORE, N_Y), EVERY)
    rows = ("x", "z", "core")
    return jax.shard_map(
        local,
        mesh=pairs,
        in_specs=(
            P(rows, "y"),
            P(EVERY, None),
            P(EVERY, None, None),
            P(),
            P(),
            P(),
            P(),
        ),
        out_specs=(P(rows, "y"), P(), P(), P(), P()),
        check_vma=False,
    )
```

```python
import math

import jax
import jax.numpy as jnp
from jax import lax
from jax.experimental import pallas as pl
from jax.experimental.pallas import tpu as pltpu
from jax.sharding import Mesh
from jax.sharding import PartitionSpec as P

norm_eps = 1e-06
gelu_coef = 0.7978845608
bf16 = jnp.bfloat16
f32 = jnp.float32
i32 = jnp.int32

N_X, N_Z, N_CORE, N_Y = 4, 4, 2, 4
N_XZ = N_X * N_Z
PEERS = ("x", "z", "y")
N_PEERS = N_XZ * N_Y
EVERY = ("x", "z", "core", "y")

TOK = 512
D = 512
HALF = 1024
LANES = 128
CAP = 32
PAIR_CAP = 2 * CAP
N_SLOTS = N_XZ * CAP
ROWS = 8192
N_REQ = N_PEERS * PAIR_CAP
N_BLOCK = 512
N_VEC = 16
N_RING = 4 * N_BLOCK + N_VEC


def swap(a):
    return lax.ppermute(a, "core", [(0, 1), (1, 0)])


def exchange(a):
    return lax.all_to_all(a, PEERS, split_axis=0, concat_axis=0, tiled=True)


def device(x, z, core, y):
    return ((x * N_Z + z) * N_CORE + core) * N_Y + y


def rings(of_core):
    found = []
    for core in range(N_CORE):
        for i in range(4):
            for j in range(4):
                at = [{"x": (k, i, j), "y": (i, k, j), "z": (i, j, k)}[of_core[core]] for k in range(4)]
                found.append([device(x, z, core, y) for x, y, z in at])
    return found


RING = (rings("xy"), rings("yz"), rings("zx"))


def along(stage, a, shift):
    pairs = [(ring[i], ring[(i + shift) % 4]) for ring in RING[stage] for i in range(4)]
    return lax.ppermute(a, EVERY, pairs)


def params(mib):
    return pltpu.CompilerParams(vmem_limit_bytes=mib << 20)


def whole(shape, space=pltpu.VMEM):
    return pl.BlockSpec(shape, lambda *_: (0,) * len(shape), memory_space=space)


def request_at(row):
    return lax.shift_left(lax.shift_right_logical(row, 6), 7) + lax.bitwise_and(row, 63)


def gather_kernel(asked, table_ref, out_ref, near, sems, wide, picked):
    step = ROWS // 8
    copies = [
        pltpu.make_async_copy(
            table_ref.at[pl.ds(i * step, step)], near.at[pl.ds(i * step, step)], sems.at[i]
        )
        for i in range(8)
    ]
    for copy in copies:
        copy.start()
    for i, copy in enumerate(copies):
        copy.wait()
        rows = slice(i * step, (i + 1) * step)
        wide[rows, :] = near[rows, :].astype(f32)
    unroll = 16

    def pick(i, carry):
        base = pl.multiple_of(i * unroll, unroll)
        at = request_at(base)
        for u in range(unroll):
            picked[pl.ds(base + u, 1), :] = wide[pl.ds(asked[at + u], 1), :]
        return carry

    lax.fori_loop(0, N_REQ // unroll, pick, 0)

    def narrow(i, carry):
        rows = pl.ds(pl.multiple_of(i * 512, 512), 512)
        out_ref[pl.ds(i * 8, 8)] = picked[rows, :].astype(bf16).reshape(8, PAIR_CAP, LANES)
        return carry

    lax.fori_loop(0, N_REQ // 512, narrow, 0)


def gather_rows(asked, table):
    return pl.pallas_call(
        gather_kernel,
        grid_spec=pltpu.PrefetchScalarGridSpec(
            num_scalar_prefetch=1,
            grid=(1,),
            in_specs=[pl.BlockSpec(memory_space=pltpu.HBM)],
            out_specs=whole((N_PEERS, PAIR_CAP, LANES)),
            scratch_shapes=[
                pltpu.VMEM((ROWS, LANES), bf16),
                pltpu.SemaphoreType.DMA((8,)),
                pltpu.VMEM((ROWS, LANES), f32),
                pltpu.VMEM((N_REQ, LANES), f32),
            ],
        ),
        out_shape=jax.ShapeDtypeStruct((N_PEERS, PAIR_CAP, LANES), bf16),
        compiler_params=params(58),
        name="gather_rows",
    )(asked, table)


def block_kernel(
    place,
    slot_own,
    slot_other,
    got_own,
    got_other,
    cot_own,
    cot_other,
    gain_ref,
    w_in,
    bias_ref,
    w_out,
    emb_ref,
    part_ref,
    send_ref,
    ring_0,
    ring_1,
    ring_2,
    ring_3,
    by_slot,
    normed_s,
    hidden_s,
    d_pre_s,
    bias_acc,
    gain_acc,
    d_out_s,
    gin_s,
    vec_s,
):
    ring_refs = (ring_0, ring_1, ring_2, ring_3)
    for j in range(2):
        for y in range(N_Y):
            lanes = slice(y * LANES, (y + 1) * LANES)
            by_slot[j, :N_SLOTS, lanes] = got_own[:, y, j * CAP : (j + 1) * CAP, :].reshape(
                N_SLOTS, LANES
            )
            k = 1 - j
            by_slot[j, N_SLOTS:, lanes] = got_other[:, y, k * CAP : (k + 1) * CAP, :].reshape(
                N_SLOTS, LANES
            )
    d_out_s[:TOK, :] = cot_own[...]
    d_out_s[TOK:, :] = cot_other[...]
    bias_acc[...] = jnp.zeros_like(bias_acc)
    gain_acc[...] = jnp.zeros_like(gain_acc)
    gain = gain_ref[...]
    bias = bias_ref[...]
    chunk = 256
    nt = (((1,), (1,)), ((), ()))
    tn = (((0,), (0,)), ((), ()))
    slot_ids = lax.broadcasted_iota(i32, (chunk, N_SLOTS), 1)

    def one_chunk(i, carry):
        rows = pl.ds(pl.multiple_of(i * chunk, chunk), chunk)
        hit_own = (slot_own[rows, :] == slot_ids).astype(f32).astype(bf16)
        hit_other = (slot_other[rows, :] == slot_ids).astype(f32).astype(bf16)
        j = i // (TOK // chunk)
        emb = jnp.dot(hit_own, by_slot[j, :N_SLOTS, :], preferred_element_type=f32) + jnp.dot(
            hit_other, by_slot[j, N_SLOTS:, :], preferred_element_type=f32
        )
        emb_ref[rows, :] = emb.astype(bf16)
        inv_rms = lax.rsqrt(jnp.mean(emb * emb, axis=-1, keepdims=True) + norm_eps)
        x_hat = emb * inv_rms
        normed = (x_hat * gain).astype(bf16)
        normed_s[rows, :] = normed
        pre = jnp.dot(normed, w_in[...], preferred_element_type=f32) + bias
        square = pre * pre
        tanh_part = jnp.tanh(gelu_coef * (pre + 0.044715 * (square * pre)))
        gate = 0.5 * (1.0 + tanh_part)
        hidden_s[rows, :] = (pre * gate).astype(bf16)
        slope = gate + 0.5 * pre * (1.0 - tanh_part * tanh_part) * (
            gelu_coef + (gelu_coef * 3.0 * 0.044715) * square
        )
        d_act = lax.dot_general(d_out_s[rows, :], w_out[...], nt, preferred_element_type=f32)
        d_pre = d_act * slope
        d_pre_bf = d_pre.astype(bf16)
        d_pre_s[rows, :] = d_pre_bf
        bias_acc[...] += jnp.sum(d_pre.reshape(chunk // 8, 8, HALF), axis=0)
        part = lax.dot_general(d_pre_bf, w_in[...], nt, preferred_element_type=f32)
        part_ref[rows, :] = part
        send_ref[rows, :] = part.astype(bf16)
        gain_acc[...] += jnp.sum((part * x_hat).reshape(chunk // 8, 8, D), axis=0)
        return carry

    lax.fori_loop(0, 2 * TOK // chunk, one_chunk, 0)

    def one_tile(i, carry):
        cols = pl.ds(pl.multiple_of(i * 256, 256), 256)
        gin_s[:, cols] = lax.dot_general(
            normed_s[...], d_pre_s[:, cols], tn, preferred_element_type=f32
        ).astype(bf16)
        return carry

    lax.fori_loop(0, HALF // 256, one_tile, 0)
    g_bias = jnp.sum(bias_acc[...], axis=0, keepdims=True)
    g_gain = jnp.sum(gain_acc[...], axis=0, keepdims=True)
    for r in range(HALF // LANES):
        vec_s[r : r + 1, :] = g_bias[:, r * LANES : (r + 1) * LANES]
    for r in range(D // LANES):
        vec_s[8 + r : 9 + r, :] = g_gain[:, r * LANES : (r + 1) * LANES]
    for shift, ref in enumerate(ring_refs):
        to = lax.rem(place[1] + shift, 4)
        cols = pl.ds(pl.multiple_of(to * 256, 256), 256)
        g_out = lax.dot_general(
            hidden_s[:, cols], d_out_s[...], tn, preferred_element_type=f32
        ).astype(bf16)
        for b in range(4):
            rows = pl.ds(pl.multiple_of(to * 128 + b * 32, 32), 32)
            for y in range(N_Y):
                at = b * N_BLOCK + y * 128
                ref[at : at + 64, :] = g_out[b * 64 : b * 64 + 64, y * LANES : (y + 1) * LANES]
                for p in range(2):
                    lane = (y * 2 + p) * LANES
                    ref[at + 64 + p * 32 : at + 96 + p * 32, :] = gin_s[rows, lane : lane + LANES]
        vec = [vec_s[pl.ds(to * 3 + r, 1), :] for r in range(3)] + [jnp.zeros((13, LANES), f32)]
        ref[4 * N_BLOCK :, :] = jnp.concatenate(vec, axis=0).astype(bf16)


def block(place, slot_own, slot_other, got_own, got_other, cot_own, cot_other, gain, w_in, bias, w_out):
    got = (N_XZ, N_Y, PAIR_CAP, LANES)
    return pl.pallas_call(
        block_kernel,
        grid_spec=pltpu.PrefetchScalarGridSpec(
            num_scalar_prefetch=1,
            grid=(1,),
            in_specs=[
                whole((2 * TOK, 1)),
                whole((2 * TOK, 1)),
                whole(got),
                whole(got),
                whole((TOK, D)),
                whole((TOK, D)),
                whole((1, D)),
                pl.BlockSpec((D, HALF), lambda i, c: (0, c[0])),
                pl.BlockSpec((1, HALF), lambda i, c: (0, c[0])),
                pl.BlockSpec((HALF, D), lambda i, c: (c[0], 0)),
            ],
            out_specs=[
                whole((2 * TOK, D)),
                whole((2 * TOK, D)),
                whole((2 * TOK, D)),
            ]
            + [whole((N_RING, LANES))] * 4,
            scratch_shapes=[
                pltpu.VMEM((2, 2 * N_SLOTS, D), bf16),
                pltpu.VMEM((2 * TOK, D), bf16),
                pltpu.VMEM((2 * TOK, HALF), bf16),
                pltpu.VMEM((2 * TOK, HALF), bf16),
                pltpu.VMEM((8, HALF), f32),
                pltpu.VMEM((8, D), f32),
                pltpu.VMEM((2 * TOK, D), bf16),
                pltpu.VMEM((D, HALF), bf16),
                pltpu.VMEM((16, LANES), f32),
            ],
        ),
        out_shape=[
            jax.ShapeDtypeStruct((2 * TOK, D), bf16),
            jax.ShapeDtypeStruct((2 * TOK, D), f32),
            jax.ShapeDtypeStruct((2 * TOK, D), bf16),
        ]
        + [jax.ShapeDtypeStruct((N_RING, LANES), bf16)] * 4,
        compiler_params=params(48),
        name="block",
    )(place, slot_own, slot_other, got_own, got_other, cot_own, cot_other, gain, w_in, bias, w_out)


def pack_kernel(slot_ref, part_ref, other_ref, emb_ref, gain_ref, cot_own, cot_other, out_ref):
    gain = gain_ref[...]
    slot_ids = lax.broadcasted_iota(i32, (N_SLOTS, TOK), 0)
    for j in range(2):
        rows = slice(j * TOK, (j + 1) * TOK)
        theirs = slice((1 - j) * TOK, (2 - j) * TOK)
        emb = emb_ref[rows, :].astype(f32)
        inv_rms = lax.rsqrt(jnp.mean(emb * emb, axis=-1, keepdims=True) + norm_eps)
        x_hat = emb * inv_rms
        scaled = (part_ref[rows, :] + other_ref[theirs, :].astype(f32)) * gain
        d_out = (cot_own if j == 0 else cot_other)[...].astype(f32)
        d_embed = (
            inv_rms * (scaled - x_hat * jnp.mean(scaled * x_hat, axis=-1, keepdims=True)) + d_out
        ).astype(bf16)
        hit = (slot_ids == slot_ref[j : j + 1, :]).astype(f32).astype(bf16)
        grads = jnp.dot(hit, d_embed, preferred_element_type=f32).astype(bf16)
        for y in range(N_Y):
            out_ref[:, y, j * CAP : (j + 1) * CAP, :] = grads[
                :, y * LANES : (y + 1) * LANES
            ].reshape(N_XZ, CAP, LANES)


def pack(slot_row, part, other, emb, gain, cot_own, cot_other):
    return pl.pallas_call(
        pack_kernel,
        out_shape=jax.ShapeDtypeStruct((N_XZ, N_Y, PAIR_CAP, LANES), bf16),
        compiler_params=params(32),
        cost_estimate=pl.CostEstimate(flops=2 * 10**9, bytes_accessed=10**7, transcendentals=0),
        name="pack",
    )(slot_row, part, other, emb, gain, cot_own, cot_other)


N_ACC = 2


def scatter_kernel(asked, arrived_ref, out_ref, grads, *accs):
    zero = jnp.zeros((512, LANES), f32)

    def clear(i, carry):
        rows = pl.ds(pl.multiple_of(i * 512, 512), 512)
        for acc in (out_ref,) + accs:
            acc[rows, :] = zero
        return carry

    lax.fori_loop(0, ROWS // 512, clear, 0)

    def widen(i, carry):
        rows = pl.ds(pl.multiple_of(i * 512, 512), 512)
        grads[rows, :] = arrived_ref[pl.ds(i * 8, 8)].astype(f32).reshape(512, LANES)
        return carry

    lax.fori_loop(0, N_REQ // 512, widen, 0)
    unroll = 8
    share = N_REQ // N_ACC

    def add(i, carry):
        base = pl.multiple_of(i * unroll, unroll)
        for u in range(unroll):
            for a, acc in enumerate((out_ref,) + accs):
                row = base + (a * share + u)
                at = pl.ds(asked[request_at(base) + (a * share * LANES // PAIR_CAP + u)], 1)
                acc[at, :] = acc[at, :] + grads[pl.ds(row, 1), :]
        return carry

    lax.fori_loop(0, share // unroll, add, 0)

    def merge(i, carry):
        rows = pl.ds(pl.multiple_of(i * 512, 512), 512)
        total = out_ref[rows, :]
        for acc in accs:
            total = total + acc[rows, :]
        out_ref[rows, :] = total
        return carry

    lax.fori_loop(0, ROWS // 512, merge, 0)


def scatter_rows(asked, arrived):
    return pl.pallas_call(
        scatter_kernel,
        grid_spec=pltpu.PrefetchScalarGridSpec(
            num_scalar_prefetch=1,
            grid=(1,),
            in_specs=[whole((N_PEERS, PAIR_CAP, LANES))],
            out_specs=whole((ROWS, LANES)),
            scratch_shapes=[pltpu.VMEM((N_REQ, LANES), f32)]
            + [pltpu.VMEM((ROWS, LANES), f32)] * (N_ACC - 1),
        ),
        out_shape=jax.ShapeDtypeStruct((ROWS, LANES), f32),
        compiler_params=params(28),
        cost_estimate=pl.CostEstimate(flops=10**10, bytes_accessed=10**7, transcendentals=0),
        name="scatter_rows",
    )(asked, arrived)


def ring_add(here, back_1, back_2, back_3, rows):
    first = here[rows, :].astype(f32) + back_2[rows, :].astype(f32)
    return first + (back_1[rows, :].astype(f32) + back_3[rows, :].astype(f32))


def sum_split_kernel(place, here, back_1, back_2, back_3, *outs):
    vec = ring_add(here, back_1, back_2, back_3, slice(4 * N_BLOCK, N_RING)).astype(bf16)
    for shift, out in enumerate(outs):
        to = lax.rem(place[2] + shift, 4)
        for part in range(4):
            step = N_BLOCK // 4
            rows = pl.ds(pl.multiple_of(to * N_BLOCK + part * step, step), step)
            out[part * step : (part + 1) * step, :] = ring_add(
                here, back_1, back_2, back_3, rows
            ).astype(bf16)
        out[N_BLOCK:, :] = vec


def sum_split(place, pieces):
    return pl.pallas_call(
        sum_split_kernel,
        grid_spec=pltpu.PrefetchScalarGridSpec(
            num_scalar_prefetch=1,
            grid=(1,),
            in_specs=[whole((N_RING, LANES))] * 4,
            out_specs=[whole((N_BLOCK + N_VEC, LANES))] * 4,
        ),
        out_shape=[jax.ShapeDtypeStruct((N_BLOCK + N_VEC, LANES), bf16)] * 4,
        compiler_params=params(8),
        name="sum_split",
    )(place, *pieces)


def sum_kernel(here, back_1, back_2, back_3, out):
    n = N_BLOCK + N_VEC
    for at in range(0, n, 88):
        rows = slice(at, min(at + 88, n))
        out[rows, :] = ring_add(here, back_1, back_2, back_3, rows).astype(bf16)


def sum_four(pieces):
    return pl.pallas_call(
        sum_kernel,
        out_shape=jax.ShapeDtypeStruct((N_BLOCK + N_VEC, LANES), bf16),
        compiler_params=params(4),
        name="sum_four",
    )(*pieces)


def join_kernel(here, back_1, back_2, back_3, out):
    for i, ref in enumerate((here, back_1, back_2, back_3)):
        out[i * N_BLOCK : (i + 1) * N_BLOCK, :] = ref[:N_BLOCK, :]
    out[4 * N_BLOCK :, :] = here[N_BLOCK:, :]


def join_four(pieces):
    return pl.pallas_call(
        join_kernel,
        out_shape=jax.ShapeDtypeStruct((N_RING, LANES), bf16),
        compiler_params=params(4),
        name="join_four",
    )(*pieces)


def finish_kernel(scale, place, *refs):
    pieces, (out_ref, in_ref, bias_ref, gain_ref, vec_s) = refs[:8], refs[8:]

    for s in range(8):

        @pl.when(pl.program_id(0) == s)
        def _(ref=pieces[s], s=s):
            a = lax.rem(place[1 if s < 4 else 3] + (4 - s % 4), 4)
            for j in range(4):
                b = lax.rem(place[2 if s < 4 else 4] + (4 - j), 4)
                rows_out = pl.ds(pl.multiple_of(b * 64, 64), 64)
                rows_in = pl.ds(pl.multiple_of(b * 32, 32), 32)
                for y in range(N_Y):
                    at = j * N_BLOCK + y * 128
                    out_ref[rows_out, y * LANES : (y + 1) * LANES] = (
                        ref[at : at + 64, :].astype(f32) * scale
                    )
                    for p in range(2):
                        lane = (y * 2 + p) * LANES
                        in_ref[rows_in, lane : lane + LANES] = (
                            ref[at + 64 + p * 32 : at + 96 + p * 32, :].astype(f32) * scale
                        )
            vec = ref[4 * N_BLOCK :, :].astype(f32) * scale
            for r in range(3):
                vec_s[s // 4, pl.ds(a * 3 + r, 1), :] = vec[r : r + 1, :]

    @pl.when(pl.program_id(0) == 7)
    def _():
        bias_ref[pl.ds(pl.multiple_of(place[0] * 8, 8), 8), :] = vec_s[0, :8, :]
        bias_ref[pl.ds(pl.multiple_of((1 - place[0]) * 8, 8), 8), :] = vec_s[1, :8, :]
        gain_ref[...] = vec_s[0, 8:12, :] + vec_s[1, 8:12, :]


def finish(place, pieces, scale):
    def half_of(s, c):
        return jnp.where(s < 4, c[0], 1 - c[0])

    def row_of(s, c):
        return lax.rem(jnp.where(s < 4, c[1], c[3]) + 8 - s, 4)

    return pl.pallas_call(
        lambda *refs: finish_kernel(scale, *refs),
        grid_spec=pltpu.PrefetchScalarGridSpec(
            num_scalar_prefetch=1,
            grid=(8,),
            in_specs=[whole((N_RING, LANES))] * 8,
            out_specs=[
                pl.BlockSpec((256, D), lambda s, c: (half_of(s, c) * 4 + row_of(s, c), 0)),
                pl.BlockSpec((128, HALF), lambda s, c: (row_of(s, c), half_of(s, c))),
                whole((16, LANES)),
                whole((4, LANES)),
            ],
            scratch_shapes=[pltpu.VMEM((2, 16, LANES), f32)],
        ),
        out_shape=[
            jax.ShapeDtypeStruct((2 * HALF, D), f32),
            jax.ShapeDtypeStruct((D, 2 * HALF), f32),
            jax.ShapeDtypeStruct((16, LANES), f32),
            jax.ShapeDtypeStruct((4, LANES), f32),
        ],
        compiler_params=params(16),
        name="finish",
    )(place, *pieces)


def local(table, item_ids, cotangent, norm_gain, w_in, bias_in, w_out):
    core = lax.axis_index("core").astype(i32)
    x, y, z = (lax.axis_index(name).astype(i32) for name in "xyz")
    is_first = core == 0
    place = jnp.stack(
        [
            core,
            jnp.where(is_first, x, y),
            jnp.where(is_first, y, z),
            jnp.where(is_first, y, x),
            jnp.where(is_first, z, y),
        ]
    )
    own_ids = item_ids.reshape(-1)
    cot_own = cotangent.reshape(TOK, D)
    cot_other = swap(cot_own)
    ids = jnp.stack([own_ids, swap(own_ids)])

    owners = ids // ROWS
    offsets = ids - owners * ROWS
    range_ids = jnp.arange(N_XZ * N_CORE, dtype=i32)
    onehot = (owners[:, :, None] == range_ids).astype(bf16)
    tok_ids = jnp.arange(TOK, dtype=i32)
    lower = (tok_ids[:, None] >= tok_ids[None, :]).astype(bf16)
    running = jnp.einsum("ts,jsr->jtr", lower, onehot, preferred_element_type=f32)
    rank = (jnp.sum(running * onehot.astype(f32), axis=2) - 1.0).astype(i32)
    slot = (owners // 2) * CAP + rank
    is_own = owners % 2 == core
    slot_own = jnp.where(is_own, slot, -1)
    slot_other = jnp.where(is_own, -1, slot)
    slot_ids = jnp.arange(N_SLOTS, dtype=i32)
    wanted = jnp.sum(
        jnp.where(slot_own[:, :, None] == slot_ids, offsets[:, :, None], 0), axis=1
    )
    wanted = jnp.transpose(wanted.reshape(2, N_XZ, CAP), (1, 0, 2))
    wanted = jnp.pad(wanted.reshape(N_XZ, 1, PAIR_CAP), ((0, 0), (0, 0), (0, LANES - PAIR_CAP)))
    requests = jnp.broadcast_to(wanted, (N_XZ, N_Y, LANES)).reshape(N_PEERS, 1, LANES)
    requests, cot_other, slot_own, slot_other = lax.optimization_barrier(
        (requests, cot_other, slot_own, slot_other)
    )
    asked = exchange(requests).reshape(-1)
    fetched = exchange(gather_rows(asked, table)).reshape(N_XZ, N_Y, PAIR_CAP, LANES)
    gain_row = norm_gain.reshape(1, D)
    emb, part, send, *ring = block(
        place,
        slot_own.reshape(2 * TOK, 1),
        slot_other.reshape(2 * TOK, 1),
        fetched,
        swap(fetched),
        cot_own,
        cot_other,
        gain_row,
        w_in,
        bias_in.reshape(1, 2 * HALF),
        w_out,
    )
    other = swap(send)
    ring_got = [along(0, ring[s], s) for s in (1, 2, 3)]
    payload = pack(slot_own, part, other, emb, gain_row, cot_own, cot_other)
    place_late, payload, *ring_got = lax.optimization_barrier((place, payload, *ring_got))
    split = list(sum_split(place_late, ring[:1] + ring_got))
    arrived = exchange(payload.reshape(N_PEERS, PAIR_CAP, LANES))
    mine = sum_four(split[:1] + [along(1, split[s], s) for s in (1, 2, 3)])
    total = sum_four([mine] + [along(2, mine, s) for s in (1, 2, 3)])
    joined = join_four([total] + [along(1, total, s) for s in (1, 2, 3)])
    pieces = [joined] + [along(0, joined, s) for s in (1, 2, 3)]
    table_grad = scatter_rows(asked, arrived)
    *late, table_grad = lax.optimization_barrier((*pieces, table_grad))
    pieces += [swap(p) for p in late]
    scale = 1.0 / math.sqrt(TOK * N_PEERS * N_CORE)
    g_out, g_in, g_bias, g_gain = finish(place, pieces, scale)
    return (table_grad, g_in, g_bias.reshape(-1), g_out, g_gain.reshape(-1))


def solution(mesh):
    pairs = Mesh(mesh.devices.reshape(N_X, N_Z, N_CORE, N_Y), EVERY)
    rows = ("x", "z", "core")
    return jax.shard_map(
        local,
        mesh=pairs,
        in_specs=(
            P(rows, "y"),
            P(EVERY, None),
            P(EVERY, None, None),
            P(),
            P(),
            P(),
            P(),
        ),
        out_specs=(P(rows, "y"), P(), P(), P(), P()),
        check_vma=False,
    )
```

```python
import math

import jax
import jax.numpy as jnp
from jax import lax
from jax.experimental import pallas as pl
from jax.experimental.pallas import tpu as pltpu
from jax.sharding import Mesh
from jax.sharding import PartitionSpec as P

norm_eps = 1e-06
gelu_coef = 0.7978845608
bf16 = jnp.bfloat16
f32 = jnp.float32
i32 = jnp.int32

N_X, N_Z, N_CORE, N_Y = 4, 4, 2, 4
N_XZ = N_X * N_Z
PEERS = ("x", "z", "y")
N_PEERS = N_XZ * N_Y
EVERY = ("x", "z", "core", "y")

TOK = 512
D = 512
HALF = 1024
LANES = 128
CAP = 32
PAIR_CAP = 2 * CAP
N_SLOTS = N_XZ * CAP
ROWS = 8192
N_REQ = N_PEERS * PAIR_CAP
N_BLOCK = 512
N_VEC = 16
N_RING = 4 * N_BLOCK + N_VEC


def swap(a):
    return lax.ppermute(a, "core", [(0, 1), (1, 0)])


def exchange(a):
    return lax.all_to_all(a, PEERS, split_axis=0, concat_axis=0, tiled=True)


def device(x, z, core, y):
    return ((x * N_Z + z) * N_CORE + core) * N_Y + y


def rings(of_core):
    found = []
    for core in range(N_CORE):
        for i in range(4):
            for j in range(4):
                at = [{"x": (k, i, j), "y": (i, k, j), "z": (i, j, k)}[of_core[core]] for k in range(4)]
                found.append([device(x, z, core, y) for x, y, z in at])
    return found


RING = (rings("xy"), rings("yz"), rings("zx"))


def along(stage, a, shift):
    pairs = [(ring[i], ring[(i + shift) % 4]) for ring in RING[stage] for i in range(4)]
    return lax.ppermute(a, EVERY, pairs)


def params(mib):
    return pltpu.CompilerParams(vmem_limit_bytes=mib << 20)


def whole(shape, space=pltpu.VMEM):
    return pl.BlockSpec(shape, lambda *_: (0,) * len(shape), memory_space=space)


def request_at(row):
    return lax.shift_left(lax.shift_right_logical(row, 6), 7) + lax.bitwise_and(row, 63)


def gather_kernel(asked, table_ref, out_ref, near, sems, wide, picked):
    step = ROWS // 8
    copies = [
        pltpu.make_async_copy(
            table_ref.at[pl.ds(i * step, step)], near.at[pl.ds(i * step, step)], sems.at[i]
        )
        for i in range(8)
    ]
    for copy in copies:
        copy.start()
    for i, copy in enumerate(copies):
        copy.wait()
        rows = slice(i * step, (i + 1) * step)
        wide[rows, :] = near[rows, :].astype(f32)
    unroll = 16

    def pick(i, carry):
        base = pl.multiple_of(i * unroll, unroll)
        at = request_at(base)
        for u in range(unroll):
            picked[pl.ds(base + u, 1), :] = wide[pl.ds(asked[at + u], 1), :]
        return carry

    lax.fori_loop(0, N_REQ // unroll, pick, 0)

    def narrow(i, carry):
        rows = pl.ds(pl.multiple_of(i * 512, 512), 512)
        out_ref[pl.ds(i * 8, 8)] = picked[rows, :].astype(bf16).reshape(8, PAIR_CAP, LANES)
        return carry

    lax.fori_loop(0, N_REQ // 512, narrow, 0)


def gather_rows(asked, table):
    return pl.pallas_call(
        gather_kernel,
        grid_spec=pltpu.PrefetchScalarGridSpec(
            num_scalar_prefetch=1,
            grid=(1,),
            in_specs=[pl.BlockSpec(memory_space=pltpu.HBM)],
            out_specs=whole((N_PEERS, PAIR_CAP, LANES)),
            scratch_shapes=[
                pltpu.VMEM((ROWS, LANES), bf16),
                pltpu.SemaphoreType.DMA((8,)),
                pltpu.VMEM((ROWS, LANES), f32),
                pltpu.VMEM((N_REQ, LANES), f32),
            ],
        ),
        out_shape=jax.ShapeDtypeStruct((N_PEERS, PAIR_CAP, LANES), bf16),
        compiler_params=params(58),
        name="gather_rows",
    )(asked, table)


def block_kernel(
    place,
    slot_own,
    slot_other,
    got_own,
    got_other,
    cot_own,
    cot_other,
    gain_ref,
    w_in,
    bias_ref,
    w_out,
    emb_ref,
    part_ref,
    send_ref,
    ring_0,
    ring_1,
    ring_2,
    ring_3,
    by_slot,
    normed_s,
    hidden_s,
    d_pre_s,
    bias_acc,
    gain_acc,
    d_out_s,
    gin_s,
    vec_s,
):
    ring_refs = (ring_0, ring_1, ring_2, ring_3)
    for j in range(2):
        for y in range(N_Y):
            lanes = slice(y * LANES, (y + 1) * LANES)
            by_slot[j, :N_SLOTS, lanes] = got_own[:, y, j * CAP : (j + 1) * CAP, :].reshape(
                N_SLOTS, LANES
            )
            k = 1 - j
            by_slot[j, N_SLOTS:, lanes] = got_other[:, y, k * CAP : (k + 1) * CAP, :].reshape(
                N_SLOTS, LANES
            )
    d_out_s[:TOK, :] = cot_own[...]
    d_out_s[TOK:, :] = cot_other[...]
    bias_acc[...] = jnp.zeros_like(bias_acc)
    gain_acc[...] = jnp.zeros_like(gain_acc)
    gain = gain_ref[...]
    bias = bias_ref[...]
    chunk = 256
    nt = (((1,), (1,)), ((), ()))
    tn = (((0,), (0,)), ((), ()))
    slot_ids = lax.broadcasted_iota(i32, (chunk, N_SLOTS), 1)

    def one_chunk(i, carry):
        rows = pl.ds(pl.multiple_of(i * chunk, chunk), chunk)
        hit_own = (slot_own[rows, :] == slot_ids).astype(f32).astype(bf16)
        hit_other = (slot_other[rows, :] == slot_ids).astype(f32).astype(bf16)
        j = i // (TOK // chunk)
        emb = jnp.dot(hit_own, by_slot[j, :N_SLOTS, :], preferred_element_type=f32) + jnp.dot(
            hit_other, by_slot[j, N_SLOTS:, :], preferred_element_type=f32
        )
        emb_ref[rows, :] = emb.astype(bf16)
        inv_rms = lax.rsqrt(jnp.mean(emb * emb, axis=-1, keepdims=True) + norm_eps)
        x_hat = emb * inv_rms
        normed = (x_hat * gain).astype(bf16)
        normed_s[rows, :] = normed
        pre = jnp.dot(normed, w_in[...], preferred_element_type=f32) + bias
        square = pre * pre
        tanh_part = jnp.tanh(gelu_coef * (pre + 0.044715 * (square * pre)))
        gate = 0.5 * (1.0 + tanh_part)
        hidden_s[rows, :] = (pre * gate).astype(bf16)
        slope = gate + 0.5 * pre * (1.0 - tanh_part * tanh_part) * (
            gelu_coef + (gelu_coef * 3.0 * 0.044715) * square
        )
        d_act = lax.dot_general(d_out_s[rows, :], w_out[...], nt, preferred_element_type=f32)
        d_pre = d_act * slope
        d_pre_bf = d_pre.astype(bf16)
        d_pre_s[rows, :] = d_pre_bf
        bias_acc[...] += jnp.sum(d_pre.reshape(chunk // 8, 8, HALF), axis=0)
        part = lax.dot_general(d_pre_bf, w_in[...], nt, preferred_element_type=f32)
        part_ref[rows, :] = part
        send_ref[rows, :] = part.astype(bf16)
        gain_acc[...] += jnp.sum((part * x_hat).reshape(chunk // 8, 8, D), axis=0)
        return carry

    lax.fori_loop(0, 2 * TOK // chunk, one_chunk, 0)

    def one_tile(i, carry):
        cols = pl.ds(pl.multiple_of(i * 256, 256), 256)
        gin_s[:, cols] = lax.dot_general(
            normed_s[...], d_pre_s[:, cols], tn, preferred_element_type=f32
        ).astype(bf16)
        return carry

    lax.fori_loop(0, HALF // 256, one_tile, 0)
    g_bias = jnp.sum(bias_acc[...], axis=0, keepdims=True)
    g_gain = jnp.sum(gain_acc[...], axis=0, keepdims=True)
    for r in range(HALF // LANES):
        vec_s[r : r + 1, :] = g_bias[:, r * LANES : (r + 1) * LANES]
    for r in range(D // LANES):
        vec_s[8 + r : 9 + r, :] = g_gain[:, r * LANES : (r + 1) * LANES]
    for shift, ref in enumerate(ring_refs):
        to = lax.rem(place[1] + shift, 4)
        cols = pl.ds(pl.multiple_of(to * 256, 256), 256)
        g_out = lax.dot_general(
            hidden_s[:, cols], d_out_s[...], tn, preferred_element_type=f32
        ).astype(bf16)
        for b in range(4):
            rows = pl.ds(pl.multiple_of(to * 128 + b * 32, 32), 32)
            for y in range(N_Y):
                at = b * N_BLOCK + y * 128
                ref[at : at + 64, :] = g_out[b * 64 : b * 64 + 64, y * LANES : (y + 1) * LANES]
                for p in range(2):
                    lane = (y * 2 + p) * LANES
                    ref[at + 64 + p * 32 : at + 96 + p * 32, :] = gin_s[rows, lane : lane + LANES]
        vec = [vec_s[pl.ds(to * 3 + r, 1), :] for r in range(3)] + [jnp.zeros((13, LANES), f32)]
        ref[4 * N_BLOCK :, :] = jnp.concatenate(vec, axis=0).astype(bf16)


def block(place, slot_own, slot_other, got_own, got_other, cot_own, cot_other, gain, w_in, bias, w_out):
    got = (N_XZ, N_Y, PAIR_CAP, LANES)
    return pl.pallas_call(
        block_kernel,
        grid_spec=pltpu.PrefetchScalarGridSpec(
            num_scalar_prefetch=1,
            grid=(1,),
            in_specs=[
                whole((2 * TOK, 1)),
                whole((2 * TOK, 1)),
                whole(got),
                whole(got),
                whole((TOK, D)),
                whole((TOK, D)),
                whole((1, D)),
                pl.BlockSpec((D, HALF), lambda i, c: (0, c[0])),
                pl.BlockSpec((1, HALF), lambda i, c: (0, c[0])),
                pl.BlockSpec((HALF, D), lambda i, c: (c[0], 0)),
            ],
            out_specs=[
                whole((2 * TOK, D)),
                whole((2 * TOK, D)),
                whole((2 * TOK, D)),
            ]
            + [whole((N_RING, LANES))] * 4,
            scratch_shapes=[
                pltpu.VMEM((2, 2 * N_SLOTS, D), bf16),
                pltpu.VMEM((2 * TOK, D), bf16),
                pltpu.VMEM((2 * TOK, HALF), bf16),
                pltpu.VMEM((2 * TOK, HALF), bf16),
                pltpu.VMEM((8, HALF), f32),
                pltpu.VMEM((8, D), f32),
                pltpu.VMEM((2 * TOK, D), bf16),
                pltpu.VMEM((D, HALF), bf16),
                pltpu.VMEM((16, LANES), f32),
            ],
        ),
        out_shape=[
            jax.ShapeDtypeStruct((2 * TOK, D), bf16),
            jax.ShapeDtypeStruct((2 * TOK, D), f32),
            jax.ShapeDtypeStruct((2 * TOK, D), bf16),
        ]
        + [jax.ShapeDtypeStruct((N_RING, LANES), bf16)] * 4,
        compiler_params=params(48),
        name="block",
    )(place, slot_own, slot_other, got_own, got_other, cot_own, cot_other, gain, w_in, bias, w_out)


def pack_kernel(slot_ref, part_ref, other_ref, emb_ref, gain_ref, cot_own, cot_other, out_ref):
    gain = gain_ref[...]
    slot_ids = lax.broadcasted_iota(i32, (N_SLOTS, TOK), 0)
    for j in range(2):
        rows = slice(j * TOK, (j + 1) * TOK)
        theirs = slice((1 - j) * TOK, (2 - j) * TOK)
        emb = emb_ref[rows, :].astype(f32)
        inv_rms = lax.rsqrt(jnp.mean(emb * emb, axis=-1, keepdims=True) + norm_eps)
        x_hat = emb * inv_rms
        scaled = (part_ref[rows, :] + other_ref[theirs, :].astype(f32)) * gain
        d_out = (cot_own if j == 0 else cot_other)[...].astype(f32)
        d_embed = (
            inv_rms * (scaled - x_hat * jnp.mean(scaled * x_hat, axis=-1, keepdims=True)) + d_out
        ).astype(bf16)
        hit = (slot_ids == slot_ref[j : j + 1, :]).astype(f32).astype(bf16)
        grads = jnp.dot(hit, d_embed, preferred_element_type=f32).astype(bf16)
        for y in range(N_Y):
            out_ref[:, y, j * CAP : (j + 1) * CAP, :] = grads[
                :, y * LANES : (y + 1) * LANES
            ].reshape(N_XZ, CAP, LANES)


def pack(slot_row, part, other, emb, gain, cot_own, cot_other):
    return pl.pallas_call(
        pack_kernel,
        out_shape=jax.ShapeDtypeStruct((N_XZ, N_Y, PAIR_CAP, LANES), bf16),
        compiler_params=params(32),
        cost_estimate=pl.CostEstimate(flops=2 * 10**9, bytes_accessed=10**7, transcendentals=0),
        name="pack",
    )(slot_row, part, other, emb, gain, cot_own, cot_other)


N_ACC = 2


def scatter_kernel(asked, arrived_ref, out_ref, grads, *accs):
    zero = jnp.zeros((512, LANES), f32)

    def clear(i, carry):
        rows = pl.ds(pl.multiple_of(i * 512, 512), 512)
        for acc in (out_ref,) + accs:
            acc[rows, :] = zero
        return carry

    lax.fori_loop(0, ROWS // 512, clear, 0)

    def widen(i, carry):
        rows = pl.ds(pl.multiple_of(i * 512, 512), 512)
        grads[rows, :] = arrived_ref[pl.ds(i * 8, 8)].astype(f32).reshape(512, LANES)
        return carry

    lax.fori_loop(0, N_REQ // 512, widen, 0)
    unroll = 8
    share = N_REQ // N_ACC

    def add(i, carry):
        base = pl.multiple_of(i * unroll, unroll)
        for u in range(unroll):
            for a, acc in enumerate((out_ref,) + accs):
                row = base + (a * share + u)
                at = pl.ds(asked[request_at(base) + (a * share * LANES // PAIR_CAP + u)], 1)
                acc[at, :] = acc[at, :] + grads[pl.ds(row, 1), :]
        return carry

    lax.fori_loop(0, share // unroll, add, 0)

    def merge(i, carry):
        rows = pl.ds(pl.multiple_of(i * 512, 512), 512)
        total = out_ref[rows, :]
        for acc in accs:
            total = total + acc[rows, :]
        out_ref[rows, :] = total
        return carry

    lax.fori_loop(0, ROWS // 512, merge, 0)


def scatter_rows(asked, arrived):
    return pl.pallas_call(
        scatter_kernel,
        grid_spec=pltpu.PrefetchScalarGridSpec(
            num_scalar_prefetch=1,
            grid=(1,),
            in_specs=[whole((N_PEERS, PAIR_CAP, LANES))],
            out_specs=whole((ROWS, LANES)),
            scratch_shapes=[pltpu.VMEM((N_REQ, LANES), f32)]
            + [pltpu.VMEM((ROWS, LANES), f32)] * (N_ACC - 1),
        ),
        out_shape=jax.ShapeDtypeStruct((ROWS, LANES), f32),
        compiler_params=params(28),
        cost_estimate=pl.CostEstimate(flops=10**10, bytes_accessed=10**7, transcendentals=0),
        name="scatter_rows",
    )(asked, arrived)


def ring_add(here, back_1, back_2, back_3, rows):
    first = here[rows, :].astype(f32) + back_2[rows, :].astype(f32)
    return first + (back_1[rows, :].astype(f32) + back_3[rows, :].astype(f32))


def sum_split_kernel(place, here, back_1, back_2, back_3, *outs):
    vec = ring_add(here, back_1, back_2, back_3, slice(4 * N_BLOCK, N_RING)).astype(bf16)
    for shift, out in enumerate(outs):
        to = lax.rem(place[2] + shift, 4)
        for part in range(4):
            step = N_BLOCK // 4
            rows = pl.ds(pl.multiple_of(to * N_BLOCK + part * step, step), step)
            out[part * step : (part + 1) * step, :] = ring_add(
                here, back_1, back_2, back_3, rows
            ).astype(bf16)
        out[N_BLOCK:, :] = vec


def sum_split(place, pieces):
    return pl.pallas_call(
        sum_split_kernel,
        grid_spec=pltpu.PrefetchScalarGridSpec(
            num_scalar_prefetch=1,
            grid=(1,),
            in_specs=[whole((N_RING, LANES))] * 4,
            out_specs=[whole((N_BLOCK + N_VEC, LANES))] * 4,
        ),
        out_shape=[jax.ShapeDtypeStruct((N_BLOCK + N_VEC, LANES), bf16)] * 4,
        compiler_params=params(8),
        cost_estimate=pl.CostEstimate(flops=2*10**9, bytes_accessed=10**6, transcendentals=0),
        name="sum_split",
    )(place, *pieces)


def sum_kernel(here, back_1, back_2, back_3, out):
    n = N_BLOCK + N_VEC
    for at in range(0, n, 88):
        rows = slice(at, min(at + 88, n))
        out[rows, :] = ring_add(here, back_1, back_2, back_3, rows).astype(bf16)


def sum_four(pieces):
    return pl.pallas_call(
        sum_kernel,
        out_shape=jax.ShapeDtypeStruct((N_BLOCK + N_VEC, LANES), bf16),
        compiler_params=params(4),
        cost_estimate=pl.CostEstimate(flops=2*10**9, bytes_accessed=10**6, transcendentals=0),
        name="sum_four",
    )(*pieces)


def join_kernel(here, back_1, back_2, back_3, out):
    for i, ref in enumerate((here, back_1, back_2, back_3)):
        out[i * N_BLOCK : (i + 1) * N_BLOCK, :] = ref[:N_BLOCK, :]
    out[4 * N_BLOCK :, :] = here[N_BLOCK:, :]


def join_four(pieces):
    return pl.pallas_call(
        join_kernel,
        out_shape=jax.ShapeDtypeStruct((N_RING, LANES), bf16),
        compiler_params=params(4),
        cost_estimate=pl.CostEstimate(flops=2*10**9, bytes_accessed=10**6, transcendentals=0),
        name="join_four",
    )(*pieces)


def finish_kernel(scale, place, *refs):
    pieces, (out_ref, in_ref, bias_ref, gain_ref, vec_s) = refs[:8], refs[8:]

    for s in range(8):

        @pl.when(pl.program_id(0) == s)
        def _(ref=pieces[s], s=s):
            a = lax.rem(place[1 if s < 4 else 3] + (4 - s % 4), 4)
            for j in range(4):
                b = lax.rem(place[2 if s < 4 else 4] + (4 - j), 4)
                rows_out = pl.ds(pl.multiple_of(b * 64, 64), 64)
                rows_in = pl.ds(pl.multiple_of(b * 32, 32), 32)
                for y in range(N_Y):
                    at = j * N_BLOCK + y * 128
                    out_ref[rows_out, y * LANES : (y + 1) * LANES] = (
                        ref[at : at + 64, :].astype(f32) * scale
                    )
                    for p in range(2):
                        lane = (y * 2 + p) * LANES
                        in_ref[rows_in, lane : lane + LANES] = (
                            ref[at + 64 + p * 32 : at + 96 + p * 32, :].astype(f32) * scale
                        )
            vec = ref[4 * N_BLOCK :, :].astype(f32) * scale
            for r in range(3):
                vec_s[s // 4, pl.ds(a * 3 + r, 1), :] = vec[r : r + 1, :]

    @pl.when(pl.program_id(0) == 7)
    def _():
        bias_ref[pl.ds(pl.multiple_of(place[0] * 8, 8), 8), :] = vec_s[0, :8, :]
        bias_ref[pl.ds(pl.multiple_of((1 - place[0]) * 8, 8), 8), :] = vec_s[1, :8, :]
        gain_ref[...] = vec_s[0, 8:12, :] + vec_s[1, 8:12, :]


def finish(place, pieces, scale):
    def half_of(s, c):
        return jnp.where(s < 4, c[0], 1 - c[0])

    def row_of(s, c):
        return lax.rem(jnp.where(s < 4, c[1], c[3]) + 8 - s, 4)

    return pl.pallas_call(
        lambda *refs: finish_kernel(scale, *refs),
        grid_spec=pltpu.PrefetchScalarGridSpec(
            num_scalar_prefetch=1,
            grid=(8,),
            in_specs=[whole((N_RING, LANES))] * 8,
            out_specs=[
                pl.BlockSpec((256, D), lambda s, c: (half_of(s, c) * 4 + row_of(s, c), 0)),
                pl.BlockSpec((128, HALF), lambda s, c: (row_of(s, c), half_of(s, c))),
                whole((16, LANES)),
                whole((4, LANES)),
            ],
            scratch_shapes=[pltpu.VMEM((2, 16, LANES), f32)],
        ),
        out_shape=[
            jax.ShapeDtypeStruct((2 * HALF, D), f32),
            jax.ShapeDtypeStruct((D, 2 * HALF), f32),
            jax.ShapeDtypeStruct((16, LANES), f32),
            jax.ShapeDtypeStruct((4, LANES), f32),
        ],
        compiler_params=params(16),
        name="finish",
    )(place, *pieces)


def local(table, item_ids, cotangent, norm_gain, w_in, bias_in, w_out):
    core = lax.axis_index("core").astype(i32)
    x, y, z = (lax.axis_index(name).astype(i32) for name in "xyz")
    is_first = core == 0
    place = jnp.stack(
        [
            core,
            jnp.where(is_first, x, y),
            jnp.where(is_first, y, z),
            jnp.where(is_first, y, x),
            jnp.where(is_first, z, y),
        ]
    )
    own_ids = item_ids.reshape(-1)
    cot_own = cotangent.reshape(TOK, D)
    cot_other = swap(cot_own)
    ids = jnp.stack([own_ids, swap(own_ids)])

    owners = ids // ROWS
    offsets = ids - owners * ROWS
    range_ids = jnp.arange(N_XZ * N_CORE, dtype=i32)
    onehot = (owners[:, :, None] == range_ids).astype(bf16)
    tok_ids = jnp.arange(TOK, dtype=i32)
    lower = (tok_ids[:, None] >= tok_ids[None, :]).astype(bf16)
    running = jnp.einsum("ts,jsr->jtr", lower, onehot, preferred_element_type=f32)
    rank = (jnp.sum(running * onehot.astype(f32), axis=2) - 1.0).astype(i32)
    slot = (owners // 2) * CAP + rank
    is_own = owners % 2 == core
    slot_own = jnp.where(is_own, slot, -1)
    slot_other = jnp.where(is_own, -1, slot)
    slot_ids = jnp.arange(N_SLOTS, dtype=i32)
    wanted = jnp.sum(
        jnp.where(slot_own[:, :, None] == slot_ids, offsets[:, :, None], 0), axis=1
    )
    wanted = jnp.transpose(wanted.reshape(2, N_XZ, CAP), (1, 0, 2))
    wanted = jnp.pad(wanted.reshape(N_XZ, 1, PAIR_CAP), ((0, 0), (0, 0), (0, LANES - PAIR_CAP)))
    requests = jnp.broadcast_to(wanted, (N_XZ, N_Y, LANES)).reshape(N_PEERS, 1, LANES)
    requests, cot_other, slot_own, slot_other = lax.optimization_barrier(
        (requests, cot_other, slot_own, slot_other)
    )
    asked = exchange(requests).reshape(-1)
    fetched = exchange(gather_rows(asked, table)).reshape(N_XZ, N_Y, PAIR_CAP, LANES)
    gain_row = norm_gain.reshape(1, D)
    emb, part, send, *ring = block(
        place,
        slot_own.reshape(2 * TOK, 1),
        slot_other.reshape(2 * TOK, 1),
        fetched,
        swap(fetched),
        cot_own,
        cot_other,
        gain_row,
        w_in,
        bias_in.reshape(1, 2 * HALF),
        w_out,
    )
    other = swap(send)
    ring_got = [along(0, ring[s], s) for s in (1, 2, 3)]
    payload = pack(slot_own, part, other, emb, gain_row, cot_own, cot_other)
    place_late, payload = lax.optimization_barrier((place, payload))
    split = list(sum_split(place_late, ring[:1] + ring_got))
    arrived = exchange(payload.reshape(N_PEERS, PAIR_CAP, LANES))
    mine = sum_four(split[:1] + [along(1, split[s], s) for s in (1, 2, 3)])
    total = sum_four([mine] + [along(2, mine, s) for s in (1, 2, 3)])
    joined = join_four([total] + [along(1, total, s) for s in (1, 2, 3)])
    pieces = [joined] + [along(0, joined, s) for s in (1, 2, 3)]
    table_grad = scatter_rows(asked, arrived)
    *late, table_grad = lax.optimization_barrier((*pieces, table_grad))
    pieces += [swap(p) for p in late]
    scale = 1.0 / math.sqrt(TOK * N_PEERS * N_CORE)
    g_out, g_in, g_bias, g_gain = finish(place, pieces, scale)
    return (table_grad, g_in, g_bias.reshape(-1), g_out, g_gain.reshape(-1))


def solution(mesh):
    pairs = Mesh(mesh.devices.reshape(N_X, N_Z, N_CORE, N_Y), EVERY)
    rows = ("x", "z", "core")
    return jax.shard_map(
        local,
        mesh=pairs,
        in_specs=(
            P(rows, "y"),
            P(EVERY, None),
            P(EVERY, None, None),
            P(),
            P(),
            P(),
            P(),
        ),
        out_specs=(P(rows, "y"), P(), P(), P(), P()),
        check_vma=False,
    )
```

```python
import math

import jax
import jax.numpy as jnp
from jax import lax
from jax.experimental import pallas as pl
from jax.experimental.pallas import tpu as pltpu
from jax.sharding import Mesh
from jax.sharding import PartitionSpec as P

norm_eps = 1e-06
gelu_coef = 0.7978845608
bf16 = jnp.bfloat16
f32 = jnp.float32
i32 = jnp.int32

N_X, N_Z, N_CORE, N_Y = 4, 4, 2, 4
N_XZ = N_X * N_Z
PEERS = ("x", "z", "y")
N_PEERS = N_XZ * N_Y
EVERY = ("x", "z", "core", "y")

TOK = 512
D = 512
HALF = 1024
LANES = 128
CAP = 32
PAIR_CAP = 2 * CAP
N_SLOTS = N_XZ * CAP
ROWS = 8192
N_REQ = N_PEERS * PAIR_CAP
N_BLOCK = 512
N_VEC = 16
N_RING = 4 * N_BLOCK + N_VEC


def swap(a):
    return lax.ppermute(a, "core", [(0, 1), (1, 0)])


def exchange(a):
    return lax.all_to_all(a, PEERS, split_axis=0, concat_axis=0, tiled=True)


def device(x, z, core, y):
    return ((x * N_Z + z) * N_CORE + core) * N_Y + y


def rings(of_core):
    found = []
    for core in range(N_CORE):
        for i in range(4):
            for j in range(4):
                at = [{"x": (k, i, j), "y": (i, k, j), "z": (i, j, k)}[of_core[core]] for k in range(4)]
                found.append([device(x, z, core, y) for x, y, z in at])
    return found


RING = (rings("xy"), rings("yz"), rings("zx"))


def along(stage, a, shift):
    pairs = [(ring[i], ring[(i + shift) % 4]) for ring in RING[stage] for i in range(4)]
    return lax.ppermute(a, EVERY, pairs)


def params(mib):
    return pltpu.CompilerParams(vmem_limit_bytes=mib << 20)


def whole(shape, space=pltpu.VMEM):
    return pl.BlockSpec(shape, lambda *_: (0,) * len(shape), memory_space=space)


SCALARS = pl.BlockSpec(memory_space=pltpu.SMEM)
NEAR = pl.BlockSpec(memory_space=pltpu.VMEM)


GATHER_MIB = 50


def request_at(row):
    return lax.shift_left(lax.shift_right_logical(row, 6), 7) + lax.bitwise_and(row, 63)


def gather_kernel(
    asked, core, table_ref, w_in_ref, w_out_ref, out_ref, w_in_near, w_out_near, near, sems, wide, picked,
):
    step = ROWS // 8
    half = pl.ds(pl.multiple_of(core[0] * HALF, HALF), HALF)
    staged = [
        pltpu.make_async_copy(w_in_ref.at[:, half], w_in_near, sems.at[8]),
        pltpu.make_async_copy(w_out_ref.at[half, :], w_out_near, sems.at[9]),
    ]
    copies = [
        pltpu.make_async_copy(
            table_ref.at[pl.ds(i * step, step)], near.at[pl.ds(i * step, step)], sems.at[i]
        )
        for i in range(8)
    ]
    for copy in copies:
        copy.start()
    for copy in staged:
        copy.start()
    for i, copy in enumerate(copies):
        copy.wait()
        rows = slice(i * step, (i + 1) * step)
        wide[rows, :] = near[rows, :].astype(f32)

    def pick(i, carry):
        for u in range(PAIR_CAP):
            picked[pl.ds(i * PAIR_CAP + u, 1), :] = wide[pl.ds(asked[i * LANES + u], 1), :]
        rows = pl.ds(pl.multiple_of(i * PAIR_CAP, PAIR_CAP), PAIR_CAP)
        out_ref[i] = picked[rows, :].astype(bf16)
        return carry

    lax.fori_loop(0, N_PEERS, pick, 0)
    for copy in staged:
        copy.wait()


def gather_rows(asked, core, table, w_in, w_out):
    return pl.pallas_call(
        gather_kernel,
        in_specs=[SCALARS] * 2 + [pl.BlockSpec(memory_space=pltpu.HBM)] * 3,
        out_specs=[NEAR] * 3,
        scratch_shapes=[
            pltpu.VMEM((ROWS, LANES), bf16),
            pltpu.SemaphoreType.DMA((10,)),
            pltpu.VMEM((ROWS, LANES), f32),
            pltpu.VMEM((N_REQ, LANES), f32),
        ],
        out_shape=[
            jax.ShapeDtypeStruct((N_PEERS, PAIR_CAP, LANES), bf16),
            jax.ShapeDtypeStruct((D, HALF), bf16),
            jax.ShapeDtypeStruct((HALF, D), bf16),
        ],
        compiler_params=params(GATHER_MIB),
        name="gather_rows",
    )(asked, core, table, w_in, w_out)


CHUNK = 512
UNROLL = 1
GIN = 1024
BLOCK_MIB = 40


def block_kernel(
    place,
    slot_own,
    slot_other,
    got_own,
    got_other,
    cot_own,
    cot_other,
    gain_ref,
    w_in,
    bias_ref,
    w_out,
    emb_ref,
    send_ref,
    ring_0,
    ring_1,
    ring_2,
    ring_3,
    by_slot,
    normed_s,
    hidden_s,
    d_pre_s,
    bias_acc,
    gain_acc,
    d_out_s,
    gin_s,
    vec_s,
):
    ring_refs = (ring_0, ring_1, ring_2, ring_3)
    own_half = pl.ds(pl.multiple_of(place[0] * HALF, HALF), HALF)
    for j in range(2):
        for y in range(N_Y):
            lanes = slice(y * LANES, (y + 1) * LANES)
            by_slot[j, :N_SLOTS, lanes] = got_own[:, y, j * CAP : (j + 1) * CAP, :].reshape(
                N_SLOTS, LANES
            )
            k = 1 - j
            by_slot[j, N_SLOTS:, lanes] = got_other[:, y, k * CAP : (k + 1) * CAP, :].reshape(
                N_SLOTS, LANES
            )
    d_out_s[:TOK, :] = cot_own[...]
    d_out_s[TOK:, :] = cot_other[...]
    bias_acc[...] = jnp.zeros_like(bias_acc)
    gain_acc[...] = jnp.zeros_like(gain_acc)
    gain = gain_ref[...]
    bias = bias_ref[:, own_half]
    chunk = CHUNK
    nt = (((1,), (1,)), ((), ()))
    tn = (((0,), (0,)), ((), ()))
    slot_ids = lax.broadcasted_iota(i32, (chunk, N_SLOTS), 1)

    def one_chunk(i, carry):
        rows = pl.ds(pl.multiple_of(i * chunk, chunk), chunk)
        hit_own = (slot_own[rows, :] == slot_ids).astype(f32).astype(bf16)
        hit_other = (slot_other[rows, :] == slot_ids).astype(f32).astype(bf16)
        j = i // (TOK // chunk)
        emb = jnp.dot(hit_own, by_slot[j, :N_SLOTS, :], preferred_element_type=f32) + jnp.dot(
            hit_other, by_slot[j, N_SLOTS:, :], preferred_element_type=f32
        )
        emb_ref[rows, :] = emb.astype(bf16)
        inv_rms = lax.rsqrt(jnp.mean(emb * emb, axis=-1, keepdims=True) + norm_eps)
        x_hat = emb * inv_rms
        normed = (x_hat * gain).astype(bf16)
        normed_s[rows, :] = normed
        pre = jnp.dot(normed, w_in[...], preferred_element_type=f32) + bias
        square = pre * pre
        tanh_part = jnp.tanh(gelu_coef * (pre + 0.044715 * (square * pre)))
        gate = 0.5 * (1.0 + tanh_part)
        hidden_s[rows, :] = (pre * gate).astype(bf16)
        slope = gate + 0.5 * pre * (1.0 - tanh_part * tanh_part) * (
            gelu_coef + (gelu_coef * 3.0 * 0.044715) * square
        )
        d_act = lax.dot_general(d_out_s[rows, :], w_out[...], nt, preferred_element_type=f32)
        d_pre = d_act * slope
        d_pre_bf = d_pre.astype(bf16)
        d_pre_s[rows, :] = d_pre_bf
        bias_acc[...] += jnp.sum(d_pre.reshape(chunk // 8, 8, HALF), axis=0)
        part = lax.dot_general(d_pre_bf, w_in[...], nt, preferred_element_type=f32)
        send_ref[rows, :] = part.astype(bf16)
        gain_acc[...] += jnp.sum((part * x_hat).reshape(chunk // 8, 8, D), axis=0)
        return carry

    lax.fori_loop(0, 2 * TOK // chunk, one_chunk, 0, unroll=UNROLL)

    def one_tile(i, carry):
        cols = pl.ds(pl.multiple_of(i * GIN, GIN), GIN)
        gin_s[:, cols] = lax.dot_general(
            normed_s[...], d_pre_s[:, cols], tn, preferred_element_type=f32
        ).astype(bf16)
        return carry

    lax.fori_loop(0, HALF // GIN, one_tile, 0)
    g_bias = jnp.sum(bias_acc[...], axis=0, keepdims=True)
    g_gain = jnp.sum(gain_acc[...], axis=0, keepdims=True)
    for r in range(HALF // LANES):
        vec_s[r : r + 1, :] = g_bias[:, r * LANES : (r + 1) * LANES]
    for r in range(D // LANES):
        vec_s[8 + r : 9 + r, :] = g_gain[:, r * LANES : (r + 1) * LANES]
    for shift, ref in enumerate(ring_refs):
        to = lax.rem(place[1] + shift, 4)
        cols = pl.ds(pl.multiple_of(to * 256, 256), 256)
        g_out = lax.dot_general(
            hidden_s[:, cols], d_out_s[...], tn, preferred_element_type=f32
        ).astype(bf16)
        for b in range(4):
            rows = pl.ds(pl.multiple_of(to * 128 + b * 32, 32), 32)
            for y in range(N_Y):
                at = b * N_BLOCK + y * 128
                ref[at : at + 64, :] = g_out[b * 64 : b * 64 + 64, y * LANES : (y + 1) * LANES]
                for p in range(2):
                    lane = (y * 2 + p) * LANES
                    ref[at + 64 + p * 32 : at + 96 + p * 32, :] = gin_s[rows, lane : lane + LANES]
        vec = [vec_s[pl.ds(to * 3 + r, 1), :] for r in range(3)] + [jnp.zeros((13, LANES), f32)]
        ref[4 * N_BLOCK :, :] = jnp.concatenate(vec, axis=0).astype(bf16)


def block(place, slot_own, slot_other, got_own, got_other, cot_own, cot_other, gain, w_in, bias, w_out):
    return pl.pallas_call(
        block_kernel,
        in_specs=[SCALARS] + [NEAR] * 10,
        out_specs=[NEAR] * 6,
        scratch_shapes=[
            pltpu.VMEM((2, 2 * N_SLOTS, D), bf16),
            pltpu.VMEM((2 * TOK, D), bf16),
            pltpu.VMEM((2 * TOK, HALF), bf16),
            pltpu.VMEM((2 * TOK, HALF), bf16),
            pltpu.VMEM((8, HALF), f32),
            pltpu.VMEM((8, D), f32),
            pltpu.VMEM((2 * TOK, D), bf16),
            pltpu.VMEM((D, HALF), bf16),
            pltpu.VMEM((16, LANES), f32),
        ],
        out_shape=[jax.ShapeDtypeStruct((2 * TOK, D), bf16)] * 2
        + [jax.ShapeDtypeStruct((N_RING, LANES), bf16)] * 4,
        compiler_params=params(BLOCK_MIB),
        name="block",
    )(place, slot_own, slot_other, got_own, got_other, cot_own, cot_other, gain, w_in, bias, w_out)


def pack_kernel(slot_ref, part_ref, other_ref, emb_ref, gain_ref, cot_own, cot_other, out_ref):
    gain = gain_ref[...]
    slot_ids = lax.broadcasted_iota(i32, (N_SLOTS, TOK), 0)
    for j in range(2):
        rows = slice(j * TOK, (j + 1) * TOK)
        theirs = slice((1 - j) * TOK, (2 - j) * TOK)
        emb = emb_ref[rows, :].astype(f32)
        inv_rms = lax.rsqrt(jnp.mean(emb * emb, axis=-1, keepdims=True) + norm_eps)
        x_hat = emb * inv_rms
        scaled = (part_ref[rows, :].astype(f32) + other_ref[theirs, :].astype(f32)) * gain
        d_out = (cot_own if j == 0 else cot_other)[...].astype(f32)
        d_embed = (
            inv_rms * (scaled - x_hat * jnp.mean(scaled * x_hat, axis=-1, keepdims=True)) + d_out
        ).astype(bf16)
        hit = (slot_ids == slot_ref[j : j + 1, :]).astype(f32).astype(bf16)
        grads = jnp.dot(hit, d_embed, preferred_element_type=f32).astype(bf16)
        for y in range(N_Y):
            out_ref[:, y, j * CAP : (j + 1) * CAP, :] = grads[
                :, y * LANES : (y + 1) * LANES
            ].reshape(N_XZ, CAP, LANES)


def pack(slot_row, part, other, emb, gain, cot_own, cot_other):
    return pl.pallas_call(
        pack_kernel,
        out_shape=jax.ShapeDtypeStruct((N_XZ, N_Y, PAIR_CAP, LANES), bf16),
        compiler_params=params(32),
        cost_estimate=pl.CostEstimate(flops=2 * 10**9, bytes_accessed=10**7, transcendentals=0),
        name="pack",
    )(slot_row, part, other, emb, gain, cot_own, cot_other)


N_ACC = 8
SCATTER_MIB = 48


def scatter_kernel(asked, arrived_ref, out_ref, grads, *accs):
    zero = jnp.zeros((512, LANES), f32)

    def clear(i, carry):
        rows = pl.ds(pl.multiple_of(i * 512, 512), 512)
        for acc in (out_ref,) + accs:
            acc[rows, :] = zero
        return carry

    lax.fori_loop(0, ROWS // 512, clear, 0)

    def widen(i, carry):
        rows = pl.ds(pl.multiple_of(i * 512, 512), 512)
        grads[rows, :] = arrived_ref[pl.ds(i * 8, 8)].astype(f32).reshape(512, LANES)
        return carry

    lax.fori_loop(0, N_REQ // 512, widen, 0)
    unroll = 8
    share = N_REQ // N_ACC

    def add(i, carry):
        base = pl.multiple_of(i * unroll, unroll)
        for u in range(unroll):
            for a, acc in enumerate((out_ref,) + accs):
                row = base + (a * share + u)
                at = pl.ds(asked[request_at(base) + (a * share * LANES // PAIR_CAP + u)], 1)
                acc[at, :] = acc[at, :] + grads[pl.ds(row, 1), :]
        return carry

    lax.fori_loop(0, share // unroll, add, 0)

    def merge(i, carry):
        rows = pl.ds(pl.multiple_of(i * 512, 512), 512)
        total = out_ref[rows, :]
        for acc in accs:
            total = total + acc[rows, :]
        out_ref[rows, :] = total
        return carry

    lax.fori_loop(0, ROWS // 512, merge, 0)


def scatter_rows(asked, arrived):
    return pl.pallas_call(
        scatter_kernel,
        in_specs=[SCALARS, NEAR],
        out_specs=NEAR,
        scratch_shapes=[pltpu.VMEM((N_REQ, LANES), f32)]
        + [pltpu.VMEM((ROWS, LANES), f32)] * (N_ACC - 1),
        out_shape=jax.ShapeDtypeStruct((ROWS, LANES), f32),
        compiler_params=params(SCATTER_MIB),
        cost_estimate=pl.CostEstimate(flops=10**10, bytes_accessed=10**7, transcendentals=0),
        name="scatter_rows",
    )(asked, arrived)


def ring_add(here, back_1, back_2, back_3, rows):
    first = here[rows, :].astype(f32) + back_2[rows, :].astype(f32)
    return first + (back_1[rows, :].astype(f32) + back_3[rows, :].astype(f32))


def sum_split_kernel(place, here, back_1, back_2, back_3, *outs):
    vec = ring_add(here, back_1, back_2, back_3, slice(4 * N_BLOCK, N_RING)).astype(bf16)
    for shift, out in enumerate(outs):
        to = lax.rem(place[2] + shift, 4)
        for part in range(4):
            step = N_BLOCK // 4
            rows = pl.ds(pl.multiple_of(to * N_BLOCK + part * step, step), step)
            out[part * step : (part + 1) * step, :] = ring_add(
                here, back_1, back_2, back_3, rows
            ).astype(bf16)
        out[N_BLOCK:, :] = vec


def sum_split(place, pieces):
    return pl.pallas_call(
        sum_split_kernel,
        in_specs=[SCALARS] + [NEAR] * 4,
        out_specs=[NEAR] * 4,
        out_shape=[jax.ShapeDtypeStruct((N_BLOCK + N_VEC, LANES), bf16)] * 4,
        compiler_params=params(8),
        cost_estimate=pl.CostEstimate(flops=2*10**9, bytes_accessed=10**6, transcendentals=0),
        name="sum_split",
    )(place, *pieces)


def sum_kernel(here, back_1, back_2, back_3, out):
    n = N_BLOCK + N_VEC
    for at in range(0, n, 88):
        rows = slice(at, min(at + 88, n))
        out[rows, :] = ring_add(here, back_1, back_2, back_3, rows).astype(bf16)


def sum_four(pieces):
    return pl.pallas_call(
        sum_kernel,
        out_shape=jax.ShapeDtypeStruct((N_BLOCK + N_VEC, LANES), bf16),
        compiler_params=params(4),
        cost_estimate=pl.CostEstimate(flops=2*10**9, bytes_accessed=10**6, transcendentals=0),
        name="sum_four",
    )(*pieces)


def join_kernel(here, back_1, back_2, back_3, out):
    for i, ref in enumerate((here, back_1, back_2, back_3)):
        out[i * N_BLOCK : (i + 1) * N_BLOCK, :] = ref[:N_BLOCK, :]
    out[4 * N_BLOCK :, :] = here[N_BLOCK:, :]


def join_four(pieces):
    return pl.pallas_call(
        join_kernel,
        out_shape=jax.ShapeDtypeStruct((N_RING, LANES), bf16),
        compiler_params=params(4),
        cost_estimate=pl.CostEstimate(flops=2*10**9, bytes_accessed=10**6, transcendentals=0),
        name="join_four",
    )(*pieces)


def finish_kernel(scale, place, *refs):
    pieces, (out_ref, in_ref, bias_ref, gain_ref, vec_s) = refs[:8], refs[8:]

    for s in range(8):

        @pl.when(pl.program_id(0) == s)
        def _(ref=pieces[s], s=s):
            a = lax.rem(place[1 if s < 4 else 3] + (4 - s % 4), 4)
            for j in range(4):
                b = lax.rem(place[2 if s < 4 else 4] + (4 - j), 4)
                rows_out = pl.ds(pl.multiple_of(b * 64, 64), 64)
                rows_in = pl.ds(pl.multiple_of(b * 32, 32), 32)
                for y in range(N_Y):
                    at = j * N_BLOCK + y * 128
                    out_ref[rows_out, y * LANES : (y + 1) * LANES] = (
                        ref[at : at + 64, :].astype(f32) * scale
                    )
                    for p in range(2):
                        lane = (y * 2 + p) * LANES
                        in_ref[rows_in, lane : lane + LANES] = (
                            ref[at + 64 + p * 32 : at + 96 + p * 32, :].astype(f32) * scale
                        )
            vec = ref[4 * N_BLOCK :, :].astype(f32) * scale
            for r in range(3):
                vec_s[s // 4, pl.ds(a * 3 + r, 1), :] = vec[r : r + 1, :]

    @pl.when(pl.program_id(0) == 7)
    def _():
        bias_ref[pl.ds(pl.multiple_of(place[0] * 8, 8), 8), :] = vec_s[0, :8, :]
        bias_ref[pl.ds(pl.multiple_of((1 - place[0]) * 8, 8), 8), :] = vec_s[1, :8, :]
        gain_ref[...] = vec_s[0, 8:12, :] + vec_s[1, 8:12, :]


def finish(place, pieces, scale):
    def half_of(s, c):
        return jnp.where(s < 4, c[0], 1 - c[0])

    def row_of(s, c):
        return lax.rem(jnp.where(s < 4, c[1], c[3]) + 8 - s, 4)

    return pl.pallas_call(
        lambda *refs: finish_kernel(scale, *refs),
        grid_spec=pltpu.PrefetchScalarGridSpec(
            num_scalar_prefetch=1,
            grid=(8,),
            in_specs=[whole((N_RING, LANES))] * 8,
            out_specs=[
                pl.BlockSpec((256, D), lambda s, c: (half_of(s, c) * 4 + row_of(s, c), 0)),
                pl.BlockSpec((128, HALF), lambda s, c: (row_of(s, c), half_of(s, c))),
                whole((16, LANES)),
                whole((4, LANES)),
            ],
            scratch_shapes=[pltpu.VMEM((2, 16, LANES), f32)],
        ),
        out_shape=[
            jax.ShapeDtypeStruct((2 * HALF, D), f32),
            jax.ShapeDtypeStruct((D, 2 * HALF), f32),
            jax.ShapeDtypeStruct((16, LANES), f32),
            jax.ShapeDtypeStruct((4, LANES), f32),
        ],
        compiler_params=params(16),
        name="finish",
    )(place, *pieces)


def local(table, item_ids, cotangent, norm_gain, w_in, bias_in, w_out):
    core = lax.axis_index("core").astype(i32)
    x, y, z = (lax.axis_index(name).astype(i32) for name in "xyz")
    is_first = core == 0
    place = jnp.stack(
        [
            core,
            jnp.where(is_first, x, y),
            jnp.where(is_first, y, z),
            jnp.where(is_first, y, x),
            jnp.where(is_first, z, y),
        ]
    )
    own_ids = item_ids.reshape(-1)
    cot_own = cotangent.reshape(TOK, D)
    cot_other = swap(cot_own)
    ids = jnp.stack([own_ids, swap(own_ids)])

    owners = ids // ROWS
    offsets = ids - owners * ROWS
    range_ids = jnp.arange(N_XZ * N_CORE, dtype=i32)
    onehot = (owners[:, :, None] == range_ids).astype(bf16)
    tok_ids = jnp.arange(TOK, dtype=i32)
    lower = (tok_ids[:, None] >= tok_ids[None, :]).astype(bf16)
    running = jnp.einsum("ts,jsr->jtr", lower, onehot, preferred_element_type=f32)
    rank = (jnp.sum(running * onehot.astype(f32), axis=2) - 1.0).astype(i32)
    slot = (owners // 2) * CAP + rank
    is_own = owners % 2 == core
    slot_own = jnp.where(is_own, slot, -1)
    slot_other = jnp.where(is_own, -1, slot)
    slot_ids = jnp.arange(N_SLOTS, dtype=i32)
    wanted = jnp.sum(
        jnp.where(slot_own[:, :, None] == slot_ids, offsets[:, :, None], 0), axis=1
    )
    wanted = jnp.transpose(wanted.reshape(2, N_XZ, CAP), (1, 0, 2))
    wanted = jnp.pad(wanted.reshape(N_XZ, 1, PAIR_CAP), ((0, 0), (0, 0), (0, LANES - PAIR_CAP)))
    requests = jnp.broadcast_to(wanted, (N_XZ, N_Y, LANES)).reshape(N_PEERS, 1, LANES)
    requests, cot_other, slot_own, slot_other = lax.optimization_barrier(
        (requests, cot_other, slot_own, slot_other)
    )
    asked = exchange(requests).reshape(-1)
    looked, w_in_half, w_out_half = gather_rows(asked, place, table, w_in, w_out)
    fetched = exchange(looked).reshape(N_XZ, N_Y, PAIR_CAP, LANES)
    gain_row = norm_gain.reshape(1, D)
    emb, send, *ring = block(
        place,
        slot_own.reshape(2 * TOK, 1),
        slot_other.reshape(2 * TOK, 1),
        fetched,
        swap(fetched),
        cot_own,
        cot_other,
        gain_row,
        w_in_half,
        bias_in.reshape(1, 2 * HALF),
        w_out_half,
    )
    other = swap(send)
    ring_got = [along(0, ring[s], s) for s in (1, 2, 3)]
    payload = pack(slot_own, send, other, emb, gain_row, cot_own, cot_other)
    place_late, payload = lax.optimization_barrier((place, payload))
    split = list(sum_split(place_late, ring[:1] + ring_got))
    arrived = exchange(payload.reshape(N_PEERS, PAIR_CAP, LANES))
    mine = sum_four(split[:1] + [along(1, split[s], s) for s in (1, 2, 3)])
    total = sum_four([mine] + [along(2, mine, s) for s in (1, 2, 3)])
    joined = join_four([total] + [along(1, total, s) for s in (1, 2, 3)])
    pieces = [joined] + [along(0, joined, s) for s in (1, 2, 3)]
    table_grad = scatter_rows(asked, arrived)
    *late, table_grad = lax.optimization_barrier((*pieces, table_grad))
    pieces += [swap(p) for p in late]
    scale = 1.0 / math.sqrt(TOK * N_PEERS * N_CORE)
    g_out, g_in, g_bias, g_gain = finish(place, pieces, scale)
    return (table_grad, g_in, g_bias.reshape(-1), g_out, g_gain.reshape(-1))


def solution(mesh):
    pairs = Mesh(mesh.devices.reshape(N_X, N_Z, N_CORE, N_Y), EVERY)
    rows = ("x", "z", "core")
    return jax.shard_map(
        local,
        mesh=pairs,
        in_specs=(
            P(rows, "y"),
            P(EVERY, None),
            P(EVERY, None, None),
            P(),
            P(),
            P(),
            P(),
        ),
        out_specs=(P(rows, "y"), P(), P(), P(), P()),
        check_vma=False,
    )
```

```python
import math

import jax
import jax.numpy as jnp
from jax import lax
from jax.experimental import pallas as pl
from jax.experimental.pallas import tpu as pltpu
from jax.sharding import Mesh
from jax.sharding import PartitionSpec as P

norm_eps = 1e-06
gelu_coef = 0.7978845608
bf16 = jnp.bfloat16
f32 = jnp.float32
i32 = jnp.int32

N_X, N_Z, N_CORE, N_Y = 4, 4, 2, 4
N_XZ = N_X * N_Z
PEERS = ("x", "z", "y")
N_PEERS = N_XZ * N_Y
EVERY = ("x", "z", "core", "y")

TOK = 512
D = 512
HALF = 1024
LANES = 128
CAP = 32
PAIR_CAP = 2 * CAP
N_SLOTS = N_XZ * CAP
ROWS = 8192
N_REQ = N_PEERS * PAIR_CAP
N_BLOCK = 512
N_VEC = 16
N_RING = 4 * N_BLOCK + N_VEC


def swap(a):
    return lax.ppermute(a, "core", [(0, 1), (1, 0)])


def exchange(a):
    return lax.all_to_all(a, PEERS, split_axis=0, concat_axis=0, tiled=True)


def device(x, z, core, y):
    return ((x * N_Z + z) * N_CORE + core) * N_Y + y


def rings(of_core):
    found = []
    for core in range(N_CORE):
        for i in range(4):
            for j in range(4):
                at = [{"x": (k, i, j), "y": (i, k, j), "z": (i, j, k)}[of_core[core]] for k in range(4)]
                found.append([device(x, z, core, y) for x, y, z in at])
    return found


RING = (rings("xy"), rings("yz"), rings("zx"))


def along(stage, a, shift):
    pairs = [(ring[i], ring[(i + shift) % 4]) for ring in RING[stage] for i in range(4)]
    return lax.ppermute(a, EVERY, pairs)


def params(mib):
    return pltpu.CompilerParams(vmem_limit_bytes=mib << 20)


def whole(shape, space=pltpu.VMEM):
    return pl.BlockSpec(shape, lambda *_: (0,) * len(shape), memory_space=space)


SCALARS = pl.BlockSpec(memory_space=pltpu.SMEM)
NEAR = pl.BlockSpec(memory_space=pltpu.VMEM)
FAR = pl.BlockSpec(memory_space=pltpu.HBM)


GATHER_MIB = 54


def request_at(row):
    return lax.shift_left(lax.shift_right_logical(row, 6), 7) + lax.bitwise_and(row, 63)


def gather_kernel(asked, table_ref, out_ref, near, sems, wide, picked):
    step = ROWS // 8
    copies = [
        pltpu.make_async_copy(
            table_ref.at[pl.ds(i * step, step)], near.at[pl.ds(i * step, step)], sems.at[i]
        )
        for i in range(8)
    ]
    for copy in copies:
        copy.start()
    for i, copy in enumerate(copies):
        copy.wait()
        rows = slice(i * step, (i + 1) * step)
        wide[rows, :] = near[rows, :].astype(f32)

    def pick(i, carry):
        for u in range(PAIR_CAP):
            picked[pl.ds(i * PAIR_CAP + u, 1), :] = wide[pl.ds(asked[i * LANES + u], 1), :]
        rows = pl.ds(pl.multiple_of(i * PAIR_CAP, PAIR_CAP), PAIR_CAP)
        out_ref[i] = picked[rows, :].astype(bf16)
        return carry

    lax.fori_loop(0, N_PEERS, pick, 0)


def gather_rows(asked, table):
    return pl.pallas_call(
        gather_kernel,
        in_specs=[SCALARS, FAR],
        out_specs=NEAR,
        scratch_shapes=[
            pltpu.VMEM((ROWS, LANES), bf16),
            pltpu.SemaphoreType.DMA((8,)),
            pltpu.VMEM((ROWS, LANES), f32),
            pltpu.VMEM((N_REQ, LANES), f32),
        ],
        out_shape=jax.ShapeDtypeStruct((N_PEERS, PAIR_CAP, LANES), bf16),
        compiler_params=params(GATHER_MIB),
        name="gather_rows",
    )(asked, table)


CHUNK = 512
GIN = 1024
BLOCK_MIB = 46


def block_kernel(
    place,
    slot_own,
    slot_other,
    got_own,
    got_other,
    cot_own,
    cot_other,
    gain_ref,
    w_in_far,
    bias_ref,
    w_out_far,
    emb_ref,
    send_ref,
    ring_0,
    ring_1,
    ring_2,
    ring_3,
    by_slot,
    normed_s,
    hidden_s,
    d_pre_s,
    bias_acc,
    gain_acc,
    d_out_s,
    gin_s,
    vec_s,
    w_in,
    w_out,
    sems,
):
    ring_refs = (ring_0, ring_1, ring_2, ring_3)
    own_half = pl.ds(pl.multiple_of(place[0] * HALF, HALF), HALF)
    w_in_copy = pltpu.make_async_copy(w_in_far.at[:, own_half], w_in, sems.at[0])
    late_copies = [
        pltpu.make_async_copy(w_out_far.at[own_half, :], w_out, sems.at[1]),
        pltpu.make_async_copy(cot_own, d_out_s.at[pl.ds(0, TOK)], sems.at[2]),
        pltpu.make_async_copy(cot_other, d_out_s.at[pl.ds(TOK, TOK)], sems.at[3]),
    ]
    w_in_copy.start()
    for copy in late_copies:
        copy.start()
    for j in range(2):
        for y in range(N_Y):
            lanes = slice(y * LANES, (y + 1) * LANES)
            by_slot[j, :N_SLOTS, lanes] = got_own[:, y, j * CAP : (j + 1) * CAP, :].reshape(
                N_SLOTS, LANES
            )
            k = 1 - j
            by_slot[j, N_SLOTS:, lanes] = got_other[:, y, k * CAP : (k + 1) * CAP, :].reshape(
                N_SLOTS, LANES
            )
    bias_acc[...] = jnp.zeros_like(bias_acc)
    gain_acc[...] = jnp.zeros_like(gain_acc)
    gain = gain_ref[...]
    bias = bias_ref[:, own_half]
    chunk = CHUNK
    nt = (((1,), (1,)), ((), ()))
    tn = (((0,), (0,)), ((), ()))
    slot_ids = lax.broadcasted_iota(i32, (chunk, N_SLOTS), 1)

    for i in range(2 * TOK // chunk):
        rows = slice(i * chunk, (i + 1) * chunk)
        hit_own = (slot_own[rows, :] == slot_ids).astype(f32).astype(bf16)
        hit_other = (slot_other[rows, :] == slot_ids).astype(f32).astype(bf16)
        j = i // (TOK // chunk)
        emb = jnp.dot(hit_own, by_slot[j, :N_SLOTS, :], preferred_element_type=f32) + jnp.dot(
            hit_other, by_slot[j, N_SLOTS:, :], preferred_element_type=f32
        )
        emb_ref[rows, :] = emb.astype(bf16)
        inv_rms = lax.rsqrt(jnp.mean(emb * emb, axis=-1, keepdims=True) + norm_eps)
        x_hat = emb * inv_rms
        normed = (x_hat * gain).astype(bf16)
        normed_s[rows, :] = normed
        if i == 0:
            w_in_copy.wait()
        pre = jnp.dot(normed, w_in[...], preferred_element_type=f32) + bias
        square = pre * pre
        tanh_part = jnp.tanh(gelu_coef * (pre + 0.044715 * (square * pre)))
        gate = 0.5 * (1.0 + tanh_part)
        hidden_s[rows, :] = (pre * gate).astype(bf16)
        slope = gate + 0.5 * pre * (1.0 - tanh_part * tanh_part) * (
            gelu_coef + (gelu_coef * 3.0 * 0.044715) * square
        )
        if i == 0:
            for copy in late_copies:
                copy.wait()
        d_act = lax.dot_general(d_out_s[rows, :], w_out[...], nt, preferred_element_type=f32)
        d_pre = d_act * slope
        d_pre_bf = d_pre.astype(bf16)
        d_pre_s[rows, :] = d_pre_bf
        bias_acc[...] += jnp.sum(d_pre.reshape(chunk // 8, 8, HALF), axis=0)
        part = lax.dot_general(d_pre_bf, w_in[...], nt, preferred_element_type=f32)
        send_ref[rows, :] = part.astype(bf16)
        gain_acc[...] += jnp.sum((part * x_hat).reshape(chunk // 8, 8, D), axis=0)

    def one_tile(i, carry):
        cols = pl.ds(pl.multiple_of(i * GIN, GIN), GIN)
        gin_s[:, cols] = lax.dot_general(
            normed_s[...], d_pre_s[:, cols], tn, preferred_element_type=f32
        ).astype(bf16)
        return carry

    lax.fori_loop(0, HALF // GIN, one_tile, 0)
    g_bias = jnp.sum(bias_acc[...], axis=0, keepdims=True)
    g_gain = jnp.sum(gain_acc[...], axis=0, keepdims=True)
    for r in range(HALF // LANES):
        vec_s[r : r + 1, :] = g_bias[:, r * LANES : (r + 1) * LANES]
    for r in range(D // LANES):
        vec_s[8 + r : 9 + r, :] = g_gain[:, r * LANES : (r + 1) * LANES]
    for shift, ref in enumerate(ring_refs):
        to = lax.rem(place[1] + shift, 4)
        cols = pl.ds(pl.multiple_of(to * 256, 256), 256)
        g_out = lax.dot_general(
            hidden_s[:, cols], d_out_s[...], tn, preferred_element_type=f32
        ).astype(bf16)
        for b in range(4):
            rows = pl.ds(pl.multiple_of(to * 128 + b * 32, 32), 32)
            for y in range(N_Y):
                at = b * N_BLOCK + y * 128
                ref[at : at + 64, :] = g_out[b * 64 : b * 64 + 64, y * LANES : (y + 1) * LANES]
                for p in range(2):
                    lane = (y * 2 + p) * LANES
                    ref[at + 64 + p * 32 : at + 96 + p * 32, :] = gin_s[rows, lane : lane + LANES]
        vec = [vec_s[pl.ds(to * 3 + r, 1), :] for r in range(3)] + [jnp.zeros((13, LANES), f32)]
        ref[4 * N_BLOCK :, :] = jnp.concatenate(vec, axis=0).astype(bf16)


def block(place, slot_own, slot_other, got_own, got_other, cot_own, cot_other, gain, w_in, bias, w_out):
    return pl.pallas_call(
        block_kernel,
        in_specs=[SCALARS] + [NEAR] * 4 + [FAR] * 2 + [NEAR, FAR, NEAR, FAR],
        out_specs=[NEAR] * 6,
        scratch_shapes=[
            pltpu.VMEM((2, 2 * N_SLOTS, D), bf16),
            pltpu.VMEM((2 * TOK, D), bf16),
            pltpu.VMEM((2 * TOK, HALF), bf16),
            pltpu.VMEM((2 * TOK, HALF), bf16),
            pltpu.VMEM((8, HALF), f32),
            pltpu.VMEM((8, D), f32),
            pltpu.VMEM((2 * TOK, D), bf16),
            pltpu.VMEM((D, HALF), bf16),
            pltpu.VMEM((16, LANES), f32),
            pltpu.VMEM((D, HALF), bf16),
            pltpu.VMEM((HALF, D), bf16),
            pltpu.SemaphoreType.DMA((4,)),
        ],
        out_shape=[jax.ShapeDtypeStruct((2 * TOK, D), bf16)] * 2
        + [jax.ShapeDtypeStruct((N_RING, LANES), bf16)] * 4,
        compiler_params=params(BLOCK_MIB),
        name="block",
    )(place, slot_own, slot_other, got_own, got_other, cot_own, cot_other, gain, w_in, bias, w_out)


def pack_kernel(slot_ref, part_ref, other_ref, emb_ref, gain_ref, cot_own, cot_other, out_ref):
    gain = gain_ref[...]
    slot_ids = lax.broadcasted_iota(i32, (N_SLOTS, TOK), 0)
    for j in range(2):
        rows = slice(j * TOK, (j + 1) * TOK)
        theirs = slice((1 - j) * TOK, (2 - j) * TOK)
        emb = emb_ref[rows, :].astype(f32)
        inv_rms = lax.rsqrt(jnp.mean(emb * emb, axis=-1, keepdims=True) + norm_eps)
        x_hat = emb * inv_rms
        scaled = (part_ref[rows, :].astype(f32) + other_ref[theirs, :].astype(f32)) * gain
        d_out = (cot_own if j == 0 else cot_other)[...].astype(f32)
        d_embed = (
            inv_rms * (scaled - x_hat * jnp.mean(scaled * x_hat, axis=-1, keepdims=True)) + d_out
        ).astype(bf16)
        hit = (slot_ids == slot_ref[j : j + 1, :]).astype(f32).astype(bf16)
        grads = jnp.dot(hit, d_embed, preferred_element_type=f32).astype(bf16)
        for y in range(N_Y):
            out_ref[:, y, j * CAP : (j + 1) * CAP, :] = grads[
                :, y * LANES : (y + 1) * LANES
            ].reshape(N_XZ, CAP, LANES)


def pack(slot_row, part, other, emb, gain, cot_own, cot_other):
    return pl.pallas_call(
        pack_kernel,
        out_shape=jax.ShapeDtypeStruct((N_XZ, N_Y, PAIR_CAP, LANES), bf16),
        compiler_params=params(32),
        cost_estimate=pl.CostEstimate(flops=2 * 10**9, bytes_accessed=10**7, transcendentals=0),
        name="pack",
    )(slot_row, part, other, emb, gain, cot_own, cot_other)


N_ACC = 8
SCATTER_MIB = 48


def scatter_kernel(asked, arrived_ref, out_ref, grads, *accs):
    zero = jnp.zeros((512, LANES), f32)

    def clear(i, carry):
        rows = pl.ds(pl.multiple_of(i * 512, 512), 512)
        for acc in (out_ref,) + accs:
            acc[rows, :] = zero
        return carry

    lax.fori_loop(0, ROWS // 512, clear, 0)

    def widen(i, carry):
        rows = pl.ds(pl.multiple_of(i * 512, 512), 512)
        grads[rows, :] = arrived_ref[pl.ds(i * 8, 8)].astype(f32).reshape(512, LANES)
        return carry

    lax.fori_loop(0, N_REQ // 512, widen, 0)
    unroll = 8
    share = N_REQ // N_ACC

    def add(i, carry):
        base = pl.multiple_of(i * unroll, unroll)
        for u in range(unroll):
            for a, acc in enumerate((out_ref,) + accs):
                row = base + (a * share + u)
                at = pl.ds(asked[request_at(base) + (a * share * LANES // PAIR_CAP + u)], 1)
                acc[at, :] = acc[at, :] + grads[pl.ds(row, 1), :]
        return carry

    lax.fori_loop(0, share // unroll, add, 0)

    def merge(i, carry):
        rows = pl.ds(pl.multiple_of(i * 512, 512), 512)
        total = out_ref[rows, :]
        for acc in accs:
            total = total + acc[rows, :]
        out_ref[rows, :] = total
        return carry

    lax.fori_loop(0, ROWS // 512, merge, 0)


def scatter_rows(asked, arrived):
    return pl.pallas_call(
        scatter_kernel,
        in_specs=[SCALARS, NEAR],
        out_specs=NEAR,
        scratch_shapes=[pltpu.VMEM((N_REQ, LANES), f32)]
        + [pltpu.VMEM((ROWS, LANES), f32)] * (N_ACC - 1),
        out_shape=jax.ShapeDtypeStruct((ROWS, LANES), f32),
        compiler_params=params(SCATTER_MIB),
        cost_estimate=pl.CostEstimate(flops=10**10, bytes_accessed=10**7, transcendentals=0),
        name="scatter_rows",
    )(asked, arrived)


def ring_add(here, back_1, back_2, back_3, rows):
    first = here[rows, :].astype(f32) + back_2[rows, :].astype(f32)
    return first + (back_1[rows, :].astype(f32) + back_3[rows, :].astype(f32))


def sum_split_kernel(place, here, back_1, back_2, back_3, *outs):
    vec = ring_add(here, back_1, back_2, back_3, slice(4 * N_BLOCK, N_RING)).astype(bf16)
    for shift, out in enumerate(outs):
        to = lax.rem(place[2] + shift, 4)
        for part in range(4):
            step = N_BLOCK // 4
            rows = pl.ds(pl.multiple_of(to * N_BLOCK + part * step, step), step)
            out[part * step : (part + 1) * step, :] = ring_add(
                here, back_1, back_2, back_3, rows
            ).astype(bf16)
        out[N_BLOCK:, :] = vec


def sum_split(place, pieces):
    return pl.pallas_call(
        sum_split_kernel,
        in_specs=[SCALARS] + [NEAR] * 4,
        out_specs=[NEAR] * 4,
        out_shape=[jax.ShapeDtypeStruct((N_BLOCK + N_VEC, LANES), bf16)] * 4,
        compiler_params=params(8),
        cost_estimate=pl.CostEstimate(flops=2*10**9, bytes_accessed=10**6, transcendentals=0),
        name="sum_split",
    )(place, *pieces)


def sum_kernel(here, back_1, back_2, back_3, out):
    n = N_BLOCK + N_VEC
    for at in range(0, n, 88):
        rows = slice(at, min(at + 88, n))
        out[rows, :] = ring_add(here, back_1, back_2, back_3, rows).astype(bf16)


def sum_four(pieces):
    return pl.pallas_call(
        sum_kernel,
        out_shape=jax.ShapeDtypeStruct((N_BLOCK + N_VEC, LANES), bf16),
        compiler_params=params(4),
        cost_estimate=pl.CostEstimate(flops=2*10**9, bytes_accessed=10**6, transcendentals=0),
        name="sum_four",
    )(*pieces)


def join_kernel(here, back_1, back_2, back_3, out):
    for i, ref in enumerate((here, back_1, back_2, back_3)):
        out[i * N_BLOCK : (i + 1) * N_BLOCK, :] = ref[:N_BLOCK, :]
    out[4 * N_BLOCK :, :] = here[N_BLOCK:, :]


def join_four(pieces):
    return pl.pallas_call(
        join_kernel,
        out_shape=jax.ShapeDtypeStruct((N_RING, LANES), bf16),
        compiler_params=params(4),
        cost_estimate=pl.CostEstimate(flops=2*10**9, bytes_accessed=10**6, transcendentals=0),
        name="join_four",
    )(*pieces)


def write_pieces(scale, place, a_at, b_at, pieces, out_ref, in_ref, vec_s):
    for s in range(4):

        @pl.when(pl.program_id(0) == s)
        def _(ref=pieces[s], s=s):
            a = lax.rem(place[a_at] + (4 - s), 4)
            for j in range(4):
                b = lax.rem(place[b_at] + (4 - j), 4)
                rows_out = pl.ds(pl.multiple_of(b * 64, 64), 64)
                rows_in = pl.ds(pl.multiple_of(b * 32, 32), 32)
                for y in range(N_Y):
                    at = j * N_BLOCK + y * 128
                    out_ref[rows_out, y * LANES : (y + 1) * LANES] = (
                        ref[at : at + 64, :].astype(f32) * scale
                    )
                    for p in range(2):
                        lane = (y * 2 + p) * LANES
                        in_ref[rows_in, lane : lane + LANES] = (
                            ref[at + 64 + p * 32 : at + 96 + p * 32, :].astype(f32) * scale
                        )
            vec = ref[4 * N_BLOCK :, :].astype(f32) * scale
            for r in range(3):
                vec_s[pl.ds(a * 3 + r, 1), :] = vec[r : r + 1, :]


def finish_own_kernel(scale, place, *refs):
    write_pieces(scale, place, 1, 2, refs[:4], *refs[4:])


def finish_other_kernel(scale, place, *refs):
    own_vec, out_ref, in_ref, bias_ref, gain_ref, vec_s = refs[4:5] + refs[7:]
    write_pieces(scale, place, 3, 4, refs[:4], out_ref, in_ref, vec_s)

    @pl.when(pl.program_id(0) == 3)
    def _():
        bias_ref[pl.ds(pl.multiple_of(place[0] * 8, 8), 8), :] = own_vec[:8, :]
        bias_ref[pl.ds(pl.multiple_of((1 - place[0]) * 8, 8), 8), :] = vec_s[:8, :]
        gain_ref[...] = own_vec[8:12, :] + vec_s[8:12, :]


def finish(place, own, other, scale):
    results = [
        jax.ShapeDtypeStruct((2 * HALF, D), f32),
        jax.ShapeDtypeStruct((D, 2 * HALF), f32),
    ]
    piece_specs = [whole((N_RING, LANES))] * 4

    def blocks(half_of, a_at):
        def row_of(s, c):
            return lax.rem(c[a_at] + 4 - s, 4)

        return [
            pl.BlockSpec((256, D), lambda s, c: (half_of(c) * 4 + row_of(s, c), 0)),
            pl.BlockSpec((128, HALF), lambda s, c: (row_of(s, c), half_of(c))),
        ]

    g_out, g_in, vec = pl.pallas_call(
        lambda *refs: finish_own_kernel(scale, *refs),
        grid_spec=pltpu.PrefetchScalarGridSpec(
            num_scalar_prefetch=1,
            grid=(4,),
            in_specs=piece_specs,
            out_specs=blocks(lambda c: c[0], 1) + [whole((16, LANES))],
        ),
        out_shape=results + [jax.ShapeDtypeStruct((16, LANES), f32)],
        compiler_params=params(12),
        cost_estimate=pl.CostEstimate(flops=6 * 10**9, bytes_accessed=10**7, transcendentals=0),
        name="finish_own",
    )(place, *own)
    return pl.pallas_call(
        lambda *refs: finish_other_kernel(scale, *refs),
        grid_spec=pltpu.PrefetchScalarGridSpec(
            num_scalar_prefetch=1,
            grid=(4,),
            in_specs=piece_specs + [whole((16, LANES))] + [pl.BlockSpec(memory_space=pl.ANY)] * 2,
            out_specs=blocks(lambda c: 1 - c[0], 3) + [whole((16, LANES)), whole((4, LANES))],
            scratch_shapes=[pltpu.VMEM((16, LANES), f32)],
        ),
        out_shape=results
        + [jax.ShapeDtypeStruct((16, LANES), f32), jax.ShapeDtypeStruct((4, LANES), f32)],
        input_output_aliases={6: 0, 7: 1},
        compiler_params=params(12),
        name="finish_other",
    )(place, *other, vec, g_out, g_in)


def local(table, item_ids, cotangent, norm_gain, w_in, bias_in, w_out):
    core = lax.axis_index("core").astype(i32)
    x, y, z = (lax.axis_index(name).astype(i32) for name in "xyz")
    is_first = core == 0
    place = jnp.stack(
        [
            core,
            jnp.where(is_first, x, y),
            jnp.where(is_first, y, z),
            jnp.where(is_first, y, x),
            jnp.where(is_first, z, y),
        ]
    )
    own_ids = item_ids.reshape(-1)
    cot_own = cotangent.reshape(TOK, D)
    cot_other = swap(cot_own)
    ids = jnp.stack([own_ids, swap(own_ids)])

    owners = ids // ROWS
    offsets = ids - owners * ROWS
    range_ids = jnp.arange(N_XZ * N_CORE, dtype=i32)
    onehot = (owners[:, :, None] == range_ids).astype(bf16)
    tok_ids = jnp.arange(TOK, dtype=i32)
    lower = (tok_ids[:, None] >= tok_ids[None, :]).astype(bf16)
    running = jnp.einsum("ts,jsr->jtr", lower, onehot, preferred_element_type=f32)
    rank = (jnp.sum(running * onehot.astype(f32), axis=2) - 1.0).astype(i32)
    slot = (owners // 2) * CAP + rank
    is_own = owners % 2 == core
    slot_own = jnp.where(is_own, slot, -1)
    slot_other = jnp.where(is_own, -1, slot)
    slot_ids = jnp.arange(N_SLOTS, dtype=i32)
    wanted = jnp.sum(
        jnp.where(slot_own[:, :, None] == slot_ids, offsets[:, :, None], 0), axis=1
    )
    wanted = jnp.transpose(wanted.reshape(2, N_XZ, CAP), (1, 0, 2))
    wanted = jnp.pad(wanted.reshape(N_XZ, 1, PAIR_CAP), ((0, 0), (0, 0), (0, LANES - PAIR_CAP)))
    requests = jnp.broadcast_to(wanted, (N_XZ, N_Y, LANES)).reshape(N_PEERS, 1, LANES)
    requests, cot_other, slot_own, slot_other = lax.optimization_barrier(
        (requests, cot_other, slot_own, slot_other)
    )
    asked = exchange(requests).reshape(-1)
    fetched = exchange(gather_rows(asked, table)).reshape(N_XZ, N_Y, PAIR_CAP, LANES)
    gain_row = norm_gain.reshape(1, D)
    emb, send, *ring = block(
        place,
        slot_own.reshape(2 * TOK, 1),
        slot_other.reshape(2 * TOK, 1),
        fetched,
        swap(fetched),
        cot_own,
        cot_other,
        gain_row,
        w_in,
        bias_in.reshape(1, 2 * HALF),
        w_out,
    )
    other = swap(send)
    ring_got = [along(0, ring[s], s) for s in (1, 2, 3)]
    payload = pack(slot_own, send, other, emb, gain_row, cot_own, cot_other)
    place_late, payload = lax.optimization_barrier((place, payload))
    split = list(sum_split(place_late, ring[:1] + ring_got))
    arrived = exchange(payload.reshape(N_PEERS, PAIR_CAP, LANES))
    mine = sum_four(split[:1] + [along(1, split[s], s) for s in (1, 2, 3)])
    total = sum_four([mine] + [along(2, mine, s) for s in (1, 2, 3)])
    joined = join_four([total] + [along(1, total, s) for s in (1, 2, 3)])
    pieces = [joined] + [along(0, joined, s) for s in (1, 2, 3)]
    table_grad = scatter_rows(asked, arrived)
    *late, table_grad = lax.optimization_barrier((*pieces, table_grad))
    others = [swap(p) for p in late]
    scale = 1.0 / math.sqrt(TOK * N_PEERS * N_CORE)
    g_out, g_in, g_bias, g_gain = finish(place, late, others, scale)
    return (table_grad, g_in, g_bias.reshape(-1), g_out, g_gain.reshape(-1))


def solution(mesh):
    pairs = Mesh(mesh.devices.reshape(N_X, N_Z, N_CORE, N_Y), EVERY)
    rows = ("x", "z", "core")
    return jax.shard_map(
        local,
        mesh=pairs,
        in_specs=(
            P(rows, "y"),
            P(EVERY, None),
            P(EVERY, None, None),
            P(),
            P(),
            P(),
            P(),
        ),
        out_specs=(P(rows, "y"), P(), P(), P(), P()),
        check_vma=False,
    )
```

```python
import math

import jax
import jax.numpy as jnp
from jax import lax
from jax.experimental import pallas as pl
from jax.experimental.pallas import tpu as pltpu
from jax.sharding import Mesh
from jax.sharding import PartitionSpec as P

norm_eps = 1e-06
gelu_coef = 0.7978845608
bf16 = jnp.bfloat16
f32 = jnp.float32
i32 = jnp.int32

N_X, N_Z, N_CORE, N_Y = 4, 4, 2, 4
N_XZ = N_X * N_Z
PEERS = ("x", "z", "y")
N_PEERS = N_XZ * N_Y
EVERY = ("x", "z", "core", "y")

TOK = 512
D = 512
HALF = 1024
LANES = 128
CAP = 32
PAIR_CAP = 2 * CAP
N_SLOTS = N_XZ * CAP
ROWS = 8192
N_REQ = N_PEERS * PAIR_CAP
N_BLOCK = 512
N_VEC = 16
N_RING = 4 * N_BLOCK + N_VEC


def swap(a):
    return lax.ppermute(a, "core", [(0, 1), (1, 0)])


def exchange(a):
    return lax.all_to_all(a, PEERS, split_axis=0, concat_axis=0, tiled=True)


def device(x, z, core, y):
    return ((x * N_Z + z) * N_CORE + core) * N_Y + y


def rings(of_core):
    found = []
    for core in range(N_CORE):
        for i in range(4):
            for j in range(4):
                at = [{"x": (k, i, j), "y": (i, k, j), "z": (i, j, k)}[of_core[core]] for k in range(4)]
                found.append([device(x, z, core, y) for x, y, z in at])
    return found


RING = (rings("xy"), rings("yz"), rings("zx"))


def along(stage, a, shift):
    pairs = [(ring[i], ring[(i + shift) % 4]) for ring in RING[stage] for i in range(4)]
    return lax.ppermute(a, EVERY, pairs)


def params(mib):
    return pltpu.CompilerParams(vmem_limit_bytes=mib << 20)


def whole(shape, space=pltpu.VMEM):
    return pl.BlockSpec(shape, lambda *_: (0,) * len(shape), memory_space=space)


SCALARS = pl.BlockSpec(memory_space=pltpu.SMEM)
NEAR = pl.BlockSpec(memory_space=pltpu.VMEM)
FAR = pl.BlockSpec(memory_space=pltpu.HBM)


GATHER_MIB = 54


def request_at(row):
    return lax.shift_left(lax.shift_right_logical(row, 6), 7) + lax.bitwise_and(row, 63)


def gather_kernel(asked, table_ref, out_ref, near, sems, wide, picked):
    step = ROWS // 8
    copies = [
        pltpu.make_async_copy(
            table_ref.at[pl.ds(i * step, step)], near.at[pl.ds(i * step, step)], sems.at[i]
        )
        for i in range(8)
    ]
    for copy in copies:
        copy.start()
    for i, copy in enumerate(copies):
        copy.wait()
        rows = slice(i * step, (i + 1) * step)
        wide[rows, :] = near[rows, :].astype(f32)

    def pick(i, carry):
        for u in range(PAIR_CAP):
            picked[pl.ds(i * PAIR_CAP + u, 1), :] = wide[pl.ds(asked[i * LANES + u], 1), :]
        rows = pl.ds(pl.multiple_of(i * PAIR_CAP, PAIR_CAP), PAIR_CAP)
        out_ref[i] = picked[rows, :].astype(bf16)
        return carry

    lax.fori_loop(0, N_PEERS, pick, 0)


def gather_rows(asked, table):
    return pl.pallas_call(
        gather_kernel,
        in_specs=[SCALARS, FAR],
        out_specs=NEAR,
        scratch_shapes=[
            pltpu.VMEM((ROWS, LANES), bf16),
            pltpu.SemaphoreType.DMA((8,)),
            pltpu.VMEM((ROWS, LANES), f32),
            pltpu.VMEM((N_REQ, LANES), f32),
        ],
        out_shape=jax.ShapeDtypeStruct((N_PEERS, PAIR_CAP, LANES), bf16),
        compiler_params=params(GATHER_MIB),
        name="gather_rows",
    )(asked, table)


CHUNK = 512
GIN = 1024
BLOCK_MIB = 46


def block_kernel(
    place,
    slot_own,
    slot_other,
    got_own,
    got_other,
    cot_own,
    cot_other,
    gain_ref,
    w_in_far,
    bias_ref,
    w_out_far,
    emb_ref,
    send_ref,
    ring_0,
    ring_1,
    ring_2,
    ring_3,
    by_slot,
    normed_s,
    hidden_s,
    d_pre_s,
    bias_acc,
    gain_acc,
    d_out_s,
    gin_s,
    vec_s,
    w_in,
    w_out,
    sems,
):
    ring_refs = (ring_0, ring_1, ring_2, ring_3)
    own_half = pl.ds(pl.multiple_of(place[0] * HALF, HALF), HALF)
    w_in_copy = pltpu.make_async_copy(w_in_far.at[:, own_half], w_in, sems.at[0])
    late_copies = [
        pltpu.make_async_copy(w_out_far.at[own_half, :], w_out, sems.at[1]),
        pltpu.make_async_copy(cot_own, d_out_s.at[pl.ds(0, TOK)], sems.at[2]),
        pltpu.make_async_copy(cot_other, d_out_s.at[pl.ds(TOK, TOK)], sems.at[3]),
    ]
    w_in_copy.start()
    for copy in late_copies:
        copy.start()
    for j in range(2):
        for y in range(N_Y):
            lanes = slice(y * LANES, (y + 1) * LANES)
            by_slot[j, :N_SLOTS, lanes] = got_own[:, y, j * CAP : (j + 1) * CAP, :].reshape(
                N_SLOTS, LANES
            )
            k = 1 - j
            by_slot[j, N_SLOTS:, lanes] = got_other[:, y, k * CAP : (k + 1) * CAP, :].reshape(
                N_SLOTS, LANES
            )
    bias_acc[...] = jnp.zeros_like(bias_acc)
    gain_acc[...] = jnp.zeros_like(gain_acc)
    gain = gain_ref[...]
    bias = bias_ref[:, own_half]
    chunk = CHUNK
    nt = (((1,), (1,)), ((), ()))
    tn = (((0,), (0,)), ((), ()))
    slot_ids = lax.broadcasted_iota(i32, (chunk, N_SLOTS), 1)

    for i in range(2 * TOK // chunk):
        rows = slice(i * chunk, (i + 1) * chunk)
        hit_own = (slot_own[rows, :] == slot_ids).astype(f32).astype(bf16)
        hit_other = (slot_other[rows, :] == slot_ids).astype(f32).astype(bf16)
        j = i // (TOK // chunk)
        emb = jnp.dot(hit_own, by_slot[j, :N_SLOTS, :], preferred_element_type=f32) + jnp.dot(
            hit_other, by_slot[j, N_SLOTS:, :], preferred_element_type=f32
        )
        emb_ref[rows, :] = emb.astype(bf16)
        inv_rms = lax.rsqrt(jnp.mean(emb * emb, axis=-1, keepdims=True) + norm_eps)
        x_hat = emb * inv_rms
        normed = (x_hat * gain).astype(bf16)
        normed_s[rows, :] = normed
        if i == 0:
            w_in_copy.wait()
        pre = jnp.dot(normed, w_in[...], preferred_element_type=f32) + bias
        square = pre * pre
        tanh_part = jnp.tanh(gelu_coef * (pre + 0.044715 * (square * pre)))
        gate = 0.5 * (1.0 + tanh_part)
        hidden_s[rows, :] = (pre * gate).astype(bf16)
        slope = gate + 0.5 * pre * (1.0 - tanh_part * tanh_part) * (
            gelu_coef + (gelu_coef * 3.0 * 0.044715) * square
        )
        if i == 0:
            for copy in late_copies:
                copy.wait()
        d_act = lax.dot_general(d_out_s[rows, :], w_out[...], nt, preferred_element_type=f32)
        d_pre = d_act * slope
        d_pre_bf = d_pre.astype(bf16)
        d_pre_s[rows, :] = d_pre_bf
        bias_acc[...] += jnp.sum(d_pre.reshape(chunk // 8, 8, HALF), axis=0)
        part = lax.dot_general(d_pre_bf, w_in[...], nt, preferred_element_type=f32)
        send_ref[rows, :] = part.astype(bf16)
        gain_acc[...] += jnp.sum((part * x_hat).reshape(chunk // 8, 8, D), axis=0)

    def one_tile(i, carry):
        cols = pl.ds(pl.multiple_of(i * GIN, GIN), GIN)
        gin_s[:, cols] = lax.dot_general(
            normed_s[...], d_pre_s[:, cols], tn, preferred_element_type=f32
        ).astype(bf16)
        return carry

    lax.fori_loop(0, HALF // GIN, one_tile, 0)
    g_bias = jnp.sum(bias_acc[...], axis=0, keepdims=True)
    g_gain = jnp.sum(gain_acc[...], axis=0, keepdims=True)
    for r in range(HALF // LANES):
        vec_s[r : r + 1, :] = g_bias[:, r * LANES : (r + 1) * LANES]
    for r in range(D // LANES):
        vec_s[8 + r : 9 + r, :] = g_gain[:, r * LANES : (r + 1) * LANES]
    for shift, ref in enumerate(ring_refs):
        to = lax.rem(place[1] + shift, 4)
        cols = pl.ds(pl.multiple_of(to * 256, 256), 256)
        g_out = lax.dot_general(
            hidden_s[:, cols], d_out_s[...], tn, preferred_element_type=f32
        ).astype(bf16)
        for b in range(4):
            rows = pl.ds(pl.multiple_of(to * 128 + b * 32, 32), 32)
            for y in range(N_Y):
                at = b * N_BLOCK + y * 128
                ref[at : at + 64, :] = g_out[b * 64 : b * 64 + 64, y * LANES : (y + 1) * LANES]
                for p in range(2):
                    lane = (y * 2 + p) * LANES
                    ref[at + 64 + p * 32 : at + 96 + p * 32, :] = gin_s[rows, lane : lane + LANES]
        vec = [vec_s[pl.ds(to * 3 + r, 1), :] for r in range(3)] + [jnp.zeros((13, LANES), f32)]
        ref[4 * N_BLOCK :, :] = jnp.concatenate(vec, axis=0).astype(bf16)


def block(place, slot_own, slot_other, got_own, got_other, cot_own, cot_other, gain, w_in, bias, w_out):
    return pl.pallas_call(
        block_kernel,
        in_specs=[SCALARS] + [NEAR] * 4 + [FAR] * 2 + [NEAR, FAR, NEAR, FAR],
        out_specs=[NEAR] * 6,
        scratch_shapes=[
            pltpu.VMEM((2, 2 * N_SLOTS, D), bf16),
            pltpu.VMEM((2 * TOK, D), bf16),
            pltpu.VMEM((2 * TOK, HALF), bf16),
            pltpu.VMEM((2 * TOK, HALF), bf16),
            pltpu.VMEM((8, HALF), f32),
            pltpu.VMEM((8, D), f32),
            pltpu.VMEM((2 * TOK, D), bf16),
            pltpu.VMEM((D, HALF), bf16),
            pltpu.VMEM((16, LANES), f32),
            pltpu.VMEM((D, HALF), bf16),
            pltpu.VMEM((HALF, D), bf16),
            pltpu.SemaphoreType.DMA((4,)),
        ],
        out_shape=[jax.ShapeDtypeStruct((2 * TOK, D), bf16)] * 2
        + [jax.ShapeDtypeStruct((N_RING, LANES), bf16)] * 4,
        compiler_params=params(BLOCK_MIB),
        name="block",
    )(place, slot_own, slot_other, got_own, got_other, cot_own, cot_other, gain, w_in, bias, w_out)


def pack_kernel(slot_ref, part_ref, other_ref, emb_ref, gain_ref, cot_own, cot_other, out_ref):
    gain = gain_ref[...]
    slot_ids = lax.broadcasted_iota(i32, (N_SLOTS, TOK), 0)
    for j in range(2):
        rows = slice(j * TOK, (j + 1) * TOK)
        theirs = slice((1 - j) * TOK, (2 - j) * TOK)
        emb = emb_ref[rows, :].astype(f32)
        inv_rms = lax.rsqrt(jnp.mean(emb * emb, axis=-1, keepdims=True) + norm_eps)
        x_hat = emb * inv_rms
        scaled = (part_ref[rows, :].astype(f32) + other_ref[theirs, :].astype(f32)) * gain
        d_out = (cot_own if j == 0 else cot_other)[...].astype(f32)
        d_embed = (
            inv_rms * (scaled - x_hat * jnp.mean(scaled * x_hat, axis=-1, keepdims=True)) + d_out
        ).astype(bf16)
        hit = (slot_ids == slot_ref[j : j + 1, :]).astype(f32).astype(bf16)
        grads = jnp.dot(hit, d_embed, preferred_element_type=f32).astype(bf16)
        for y in range(N_Y):
            out_ref[:, y, j * CAP : (j + 1) * CAP, :] = grads[
                :, y * LANES : (y + 1) * LANES
            ].reshape(N_XZ, CAP, LANES)


def pack(slot_row, part, other, emb, gain, cot_own, cot_other):
    return pl.pallas_call(
        pack_kernel,
        out_shape=jax.ShapeDtypeStruct((N_XZ, N_Y, PAIR_CAP, LANES), bf16),
        compiler_params=params(32),
        cost_estimate=pl.CostEstimate(flops=2 * 10**9, bytes_accessed=10**7, transcendentals=0),
        name="pack",
    )(slot_row, part, other, emb, gain, cot_own, cot_other)


N_ACC = 8
SCATTER_MIB = 48


def scatter_kernel(asked, arrived_ref, out_ref, grads, *accs):
    zero = jnp.zeros((512, LANES), f32)

    def clear(i, carry):
        rows = pl.ds(pl.multiple_of(i * 512, 512), 512)
        for acc in (out_ref,) + accs:
            acc[rows, :] = zero
        return carry

    lax.fori_loop(0, ROWS // 512, clear, 0)

    def widen(i, carry):
        rows = pl.ds(pl.multiple_of(i * 512, 512), 512)
        grads[rows, :] = arrived_ref[pl.ds(i * 8, 8)].astype(f32).reshape(512, LANES)
        return carry

    lax.fori_loop(0, N_REQ // 512, widen, 0)
    unroll = 8
    share = N_REQ // N_ACC

    def add(i, carry):
        base = pl.multiple_of(i * unroll, unroll)
        for u in range(unroll):
            for a, acc in enumerate((out_ref,) + accs):
                row = base + (a * share + u)
                at = pl.ds(asked[request_at(base) + (a * share * LANES // PAIR_CAP + u)], 1)
                acc[at, :] = acc[at, :] + grads[pl.ds(row, 1), :]
        return carry

    lax.fori_loop(0, share // unroll, add, 0)

    def merge(i, carry):
        rows = pl.ds(pl.multiple_of(i * 512, 512), 512)
        total = out_ref[rows, :]
        for acc in accs:
            total = total + acc[rows, :]
        out_ref[rows, :] = total
        return carry

    lax.fori_loop(0, ROWS // 512, merge, 0)


def scatter_rows(asked, arrived):
    return pl.pallas_call(
        scatter_kernel,
        in_specs=[SCALARS, NEAR],
        out_specs=NEAR,
        scratch_shapes=[pltpu.VMEM((N_REQ, LANES), f32)]
        + [pltpu.VMEM((ROWS, LANES), f32)] * (N_ACC - 1),
        out_shape=jax.ShapeDtypeStruct((ROWS, LANES), f32),
        compiler_params=params(SCATTER_MIB),
        cost_estimate=pl.CostEstimate(flops=10**10, bytes_accessed=10**7, transcendentals=0),
        name="scatter_rows",
    )(asked, arrived)


def ring_add(here, back_1, back_2, back_3, rows):
    first = here[rows, :].astype(f32) + back_2[rows, :].astype(f32)
    return first + (back_1[rows, :].astype(f32) + back_3[rows, :].astype(f32))


def sum_split_kernel(place, here, back_1, back_2, back_3, *outs):
    vec = ring_add(here, back_1, back_2, back_3, slice(4 * N_BLOCK, N_RING)).astype(bf16)
    for shift, out in enumerate(outs):
        to = lax.rem(place[2] + shift, 4)
        for part in range(4):
            step = N_BLOCK // 4
            rows = pl.ds(pl.multiple_of(to * N_BLOCK + part * step, step), step)
            out[part * step : (part + 1) * step, :] = ring_add(
                here, back_1, back_2, back_3, rows
            ).astype(bf16)
        out[N_BLOCK:, :] = vec


def sum_split(place, pieces):
    return pl.pallas_call(
        sum_split_kernel,
        in_specs=[SCALARS] + [NEAR] * 4,
        out_specs=[NEAR] * 4,
        out_shape=[jax.ShapeDtypeStruct((N_BLOCK + N_VEC, LANES), bf16)] * 4,
        compiler_params=params(8),
        cost_estimate=pl.CostEstimate(flops=4 * 10**9, bytes_accessed=10**6, transcendentals=0),
        name="sum_split",
    )(place, *pieces)


def sum_kernel(here, back_1, back_2, back_3, out):
    n = N_BLOCK + N_VEC
    for at in range(0, n, 88):
        rows = slice(at, min(at + 88, n))
        out[rows, :] = ring_add(here, back_1, back_2, back_3, rows).astype(bf16)


def sum_four(pieces):
    return pl.pallas_call(
        sum_kernel,
        out_shape=jax.ShapeDtypeStruct((N_BLOCK + N_VEC, LANES), bf16),
        compiler_params=params(4),
        cost_estimate=pl.CostEstimate(flops=4 * 10**9, bytes_accessed=10**6, transcendentals=0),
        name="sum_four",
    )(*pieces)


def join_kernel(here, back_1, back_2, back_3, out):
    for i, ref in enumerate((here, back_1, back_2, back_3)):
        out[i * N_BLOCK : (i + 1) * N_BLOCK, :] = ref[:N_BLOCK, :]
    out[4 * N_BLOCK :, :] = here[N_BLOCK:, :]


def join_four(pieces):
    return pl.pallas_call(
        join_kernel,
        out_shape=jax.ShapeDtypeStruct((N_RING, LANES), bf16),
        compiler_params=params(4),
        cost_estimate=pl.CostEstimate(flops=4 * 10**9, bytes_accessed=10**6, transcendentals=0),
        name="join_four",
    )(*pieces)


def write_pieces(scale, place, a_at, b_at, pieces, out_ref, in_ref, vec_s):
    for s in range(4):

        @pl.when(pl.program_id(0) == s)
        def _(ref=pieces[s], s=s):
            a = lax.rem(place[a_at] + (4 - s), 4)
            for j in range(4):
                b = lax.rem(place[b_at] + (4 - j), 4)
                rows_out = pl.ds(pl.multiple_of(b * 64, 64), 64)
                rows_in = pl.ds(pl.multiple_of(b * 32, 32), 32)
                for y in range(N_Y):
                    at = j * N_BLOCK + y * 128
                    out_ref[rows_out, y * LANES : (y + 1) * LANES] = (
                        ref[at : at + 64, :].astype(f32) * scale
                    )
                    for p in range(2):
                        lane = (y * 2 + p) * LANES
                        in_ref[rows_in, lane : lane + LANES] = (
                            ref[at + 64 + p * 32 : at + 96 + p * 32, :].astype(f32) * scale
                        )
            vec = ref[4 * N_BLOCK :, :].astype(f32) * scale
            for r in range(3):
                vec_s[pl.ds(a * 3 + r, 1), :] = vec[r : r + 1, :]


def finish_own_kernel(scale, place, *refs):
    write_pieces(scale, place, 1, 2, refs[:4], *refs[4:])


def finish_other_kernel(scale, place, *refs):
    own_vec, out_ref, in_ref, bias_ref, gain_ref, vec_s = refs[4:5] + refs[7:]
    write_pieces(scale, place, 3, 4, refs[:4], out_ref, in_ref, vec_s)

    @pl.when(pl.program_id(0) == 3)
    def _():
        bias_ref[pl.ds(pl.multiple_of(place[0] * 8, 8), 8), :] = own_vec[:8, :]
        bias_ref[pl.ds(pl.multiple_of((1 - place[0]) * 8, 8), 8), :] = vec_s[:8, :]
        gain_ref[...] = own_vec[8:12, :] + vec_s[8:12, :]


def finish(place, own, other, scale):
    results = [
        jax.ShapeDtypeStruct((2 * HALF, D), f32),
        jax.ShapeDtypeStruct((D, 2 * HALF), f32),
    ]
    piece_specs = [whole((N_RING, LANES))] * 4

    def blocks(half_of, a_at):
        def row_of(s, c):
            return lax.rem(c[a_at] + 4 - s, 4)

        return [
            pl.BlockSpec((256, D), lambda s, c: (half_of(c) * 4 + row_of(s, c), 0)),
            pl.BlockSpec((128, HALF), lambda s, c: (row_of(s, c), half_of(c))),
        ]

    g_out, g_in, vec = pl.pallas_call(
        lambda *refs: finish_own_kernel(scale, *refs),
        grid_spec=pltpu.PrefetchScalarGridSpec(
            num_scalar_prefetch=1,
            grid=(4,),
            in_specs=piece_specs,
            out_specs=blocks(lambda c: c[0], 1) + [whole((16, LANES))],
        ),
        out_shape=results + [jax.ShapeDtypeStruct((16, LANES), f32)],
        compiler_params=params(12),
        cost_estimate=pl.CostEstimate(flops=6 * 10**9, bytes_accessed=10**7, transcendentals=0),
        name="finish_own",
    )(place, *own)
    return pl.pallas_call(
        lambda *refs: finish_other_kernel(scale, *refs),
        grid_spec=pltpu.PrefetchScalarGridSpec(
            num_scalar_prefetch=1,
            grid=(4,),
            in_specs=piece_specs + [whole((16, LANES))] + [pl.BlockSpec(memory_space=pl.ANY)] * 2,
            out_specs=blocks(lambda c: 1 - c[0], 3) + [whole((16, LANES)), whole((4, LANES))],
            scratch_shapes=[pltpu.VMEM((16, LANES), f32)],
        ),
        out_shape=results
        + [jax.ShapeDtypeStruct((16, LANES), f32), jax.ShapeDtypeStruct((4, LANES), f32)],
        input_output_aliases={6: 0, 7: 1},
        compiler_params=params(12),
        name="finish_other",
    )(place, *other, vec, g_out, g_in)


def local(table, item_ids, cotangent, norm_gain, w_in, bias_in, w_out):
    core = lax.axis_index("core").astype(i32)
    x, y, z = (lax.axis_index(name).astype(i32) for name in "xyz")
    is_first = core == 0
    place = jnp.stack(
        [
            core,
            jnp.where(is_first, x, y),
            jnp.where(is_first, y, z),
            jnp.where(is_first, y, x),
            jnp.where(is_first, z, y),
        ]
    )
    own_ids = item_ids.reshape(-1)
    cot_own = cotangent.reshape(TOK, D)
    cot_other = swap(cot_own)
    ids = jnp.stack([own_ids, swap(own_ids)])

    owners = ids // ROWS
    offsets = ids - owners * ROWS
    range_ids = jnp.arange(N_XZ * N_CORE, dtype=i32)
    onehot = (owners[:, :, None] == range_ids).astype(bf16)
    tok_ids = jnp.arange(TOK, dtype=i32)
    lower = (tok_ids[:, None] >= tok_ids[None, :]).astype(bf16)
    running = jnp.einsum("ts,jsr->jtr", lower, onehot, preferred_element_type=f32)
    rank = (jnp.sum(running * onehot.astype(f32), axis=2) - 1.0).astype(i32)
    slot = (owners // 2) * CAP + rank
    is_own = owners % 2 == core
    slot_own = jnp.where(is_own, slot, -1)
    slot_other = jnp.where(is_own, -1, slot)
    slot_ids = jnp.arange(N_SLOTS, dtype=i32)
    wanted = jnp.sum(
        jnp.where(slot_own[:, :, None] == slot_ids, offsets[:, :, None], 0), axis=1
    )
    wanted = jnp.transpose(wanted.reshape(2, N_XZ, CAP), (1, 0, 2))
    wanted = jnp.pad(wanted.reshape(N_XZ, 1, PAIR_CAP), ((0, 0), (0, 0), (0, LANES - PAIR_CAP)))
    requests = jnp.broadcast_to(wanted, (N_XZ, N_Y, LANES)).reshape(N_PEERS, 1, LANES)
    requests, cot_other, slot_own, slot_other = lax.optimization_barrier(
        (requests, cot_other, slot_own, slot_other)
    )
    asked = exchange(requests).reshape(-1)
    fetched = exchange(gather_rows(asked, table)).reshape(N_XZ, N_Y, PAIR_CAP, LANES)
    gain_row = norm_gain.reshape(1, D)
    emb, send, *ring = block(
        place,
        slot_own.reshape(2 * TOK, 1),
        slot_other.reshape(2 * TOK, 1),
        fetched,
        swap(fetched),
        cot_own,
        cot_other,
        gain_row,
        w_in,
        bias_in.reshape(1, 2 * HALF),
        w_out,
    )
    other = swap(send)
    ring_got = [along(0, ring[s], s) for s in (1, 2, 3)]
    payload = pack(slot_own, send, other, emb, gain_row, cot_own, cot_other)
    place_late, payload = lax.optimization_barrier((place, payload))
    split = list(sum_split(place_late, ring[:1] + ring_got))
    arrived = exchange(payload.reshape(N_PEERS, PAIR_CAP, LANES))
    mine = sum_four(split[:1] + [along(1, split[s], s) for s in (1, 2, 3)])
    total = sum_four([mine] + [along(2, mine, s) for s in (1, 2, 3)])
    joined = join_four([total] + [along(1, total, s) for s in (1, 2, 3)])
    pieces = [joined] + [along(0, joined, s) for s in (1, 2, 3)]
    table_grad = scatter_rows(asked, arrived)
    *late, table_grad = lax.optimization_barrier((*pieces, table_grad))
    others = [swap(p) for p in late]
    scale = 1.0 / math.sqrt(TOK * N_PEERS * N_CORE)
    g_out, g_in, g_bias, g_gain = finish(place, late, others, scale)
    return (table_grad, g_in, g_bias.reshape(-1), g_out, g_gain.reshape(-1))


def solution(mesh):
    pairs = Mesh(mesh.devices.reshape(N_X, N_Z, N_CORE, N_Y), EVERY)
    rows = ("x", "z", "core")
    return jax.shard_map(
        local,
        mesh=pairs,
        in_specs=(
            P(rows, "y"),
            P(EVERY, None),
            P(EVERY, None, None),
            P(),
            P(),
            P(),
            P(),
        ),
        out_specs=(P(rows, "y"), P(), P(), P(), P()),
        check_vma=False,
    )
```

```python
import math

import jax
import jax.numpy as jnp
from jax import lax
from jax.experimental import pallas as pl
from jax.experimental.pallas import tpu as pltpu
from jax.sharding import Mesh
from jax.sharding import PartitionSpec as P

norm_eps = 1e-06
gelu_coef = 0.7978845608
bf16 = jnp.bfloat16
f32 = jnp.float32
i32 = jnp.int32

N_X, N_Z, N_CORE, N_Y = 4, 4, 2, 4
N_XZ = N_X * N_Z
PEERS = ("z", "x", "y")
N_PEERS = N_XZ * N_Y
EVERY = ("x", "z", "core", "y")

TOK = 512
D = 512
HALF = 1024
LANES = 128
CAP = 32
PAIR_CAP = 2 * CAP
N_SLOTS = N_XZ * CAP
ROWS = 8192
N_REQ = N_PEERS * PAIR_CAP
N_BLOCK = 512
N_VEC = 16
N_RING = 4 * N_BLOCK + N_VEC


def swap(a):
    return lax.ppermute(a, "core", [(0, 1), (1, 0)])


def exchange(a):
    return lax.all_to_all(a, PEERS, split_axis=0, concat_axis=0, tiled=True)


def device(x, z, core, y):
    return ((x * N_Z + z) * N_CORE + core) * N_Y + y


def rings(of_core):
    found = []
    for core in range(N_CORE):
        for i in range(4):
            for j in range(4):
                at = [{"x": (k, i, j), "y": (i, k, j), "z": (i, j, k)}[of_core[core]] for k in range(4)]
                found.append([device(x, z, core, y) for x, y, z in at])
    return found


RING = (rings("xy"), rings("yz"), rings("zx"))


def along(stage, a, shift):
    pairs = [(ring[i], ring[(i + shift) % 4]) for ring in RING[stage] for i in range(4)]
    return lax.ppermute(a, EVERY, pairs)


def params(mib):
    return pltpu.CompilerParams(vmem_limit_bytes=mib << 20)


def whole(shape, space=pltpu.VMEM):
    return pl.BlockSpec(shape, lambda *_: (0,) * len(shape), memory_space=space)


SCALARS = pl.BlockSpec(memory_space=pltpu.SMEM)
NEAR = pl.BlockSpec(memory_space=pltpu.VMEM)
FAR = pl.BlockSpec(memory_space=pltpu.HBM)


GATHER_MIB = 54


def request_at(row):
    return lax.shift_left(lax.shift_right_logical(row, 6), 7) + lax.bitwise_and(row, 63)


def gather_kernel(asked, table_ref, out_ref, near, sems, wide, picked):
    step = ROWS // 8
    copies = [
        pltpu.make_async_copy(
            table_ref.at[pl.ds(i * step, step)], near.at[pl.ds(i * step, step)], sems.at[i]
        )
        for i in range(8)
    ]
    for copy in copies:
        copy.start()
    for i, copy in enumerate(copies):
        copy.wait()
        rows = slice(i * step, (i + 1) * step)
        wide[rows, :] = near[rows, :].astype(f32)

    def pick(i, carry):
        for u in range(PAIR_CAP):
            picked[pl.ds(i * PAIR_CAP + u, 1), :] = wide[pl.ds(asked[i * LANES + u], 1), :]
        rows = pl.ds(pl.multiple_of(i * PAIR_CAP, PAIR_CAP), PAIR_CAP)
        out_ref[i] = picked[rows, :].astype(bf16)
        return carry

    lax.fori_loop(0, N_PEERS, pick, 0)


def gather_rows(asked, table):
    return pl.pallas_call(
        gather_kernel,
        in_specs=[SCALARS, FAR],
        out_specs=NEAR,
        scratch_shapes=[
            pltpu.VMEM((ROWS, LANES), bf16),
            pltpu.SemaphoreType.DMA((8,)),
            pltpu.VMEM((ROWS, LANES), f32),
            pltpu.VMEM((N_REQ, LANES), f32),
        ],
        out_shape=jax.ShapeDtypeStruct((N_PEERS, PAIR_CAP, LANES), bf16),
        compiler_params=params(GATHER_MIB),
        name="gather_rows",
    )(asked, table)


CHUNK = 512
GIN = 1024
BLOCK_MIB = 46


def block_kernel(
    place,
    slot_own,
    slot_other,
    got_own,
    got_other,
    cot_own,
    cot_other,
    gain_ref,
    w_in_far,
    bias_ref,
    w_out_far,
    emb_ref,
    send_ref,
    ring_0,
    ring_1,
    ring_2,
    ring_3,
    by_slot,
    normed_s,
    hidden_s,
    d_pre_s,
    bias_acc,
    gain_acc,
    d_out_s,
    gin_s,
    vec_s,
    w_in,
    w_out,
    sems,
):
    ring_refs = (ring_0, ring_1, ring_2, ring_3)
    own_half = pl.ds(pl.multiple_of(place[0] * HALF, HALF), HALF)
    w_in_copy = pltpu.make_async_copy(w_in_far.at[:, own_half], w_in, sems.at[0])
    late_copies = [
        pltpu.make_async_copy(w_out_far.at[own_half, :], w_out, sems.at[1]),
        pltpu.make_async_copy(cot_own, d_out_s.at[pl.ds(0, TOK)], sems.at[2]),
        pltpu.make_async_copy(cot_other, d_out_s.at[pl.ds(TOK, TOK)], sems.at[3]),
    ]
    w_in_copy.start()
    for copy in late_copies:
        copy.start()
    for j in range(2):
        for y in range(N_Y):
            lanes = slice(y * LANES, (y + 1) * LANES)
            by_slot[j, :N_SLOTS, lanes] = got_own[:, y, j * CAP : (j + 1) * CAP, :].reshape(
                N_SLOTS, LANES
            )
            k = 1 - j
            by_slot[j, N_SLOTS:, lanes] = got_other[:, y, k * CAP : (k + 1) * CAP, :].reshape(
                N_SLOTS, LANES
            )
    bias_acc[...] = jnp.zeros_like(bias_acc)
    gain_acc[...] = jnp.zeros_like(gain_acc)
    gain = gain_ref[...]
    bias = bias_ref[:, own_half]
    chunk = CHUNK
    nt = (((1,), (1,)), ((), ()))
    tn = (((0,), (0,)), ((), ()))
    slot_ids = lax.broadcasted_iota(i32, (chunk, N_SLOTS), 1)

    for i in range(2 * TOK // chunk):
        rows = slice(i * chunk, (i + 1) * chunk)
        hit_own = (slot_own[rows, :] == slot_ids).astype(f32).astype(bf16)
        hit_other = (slot_other[rows, :] == slot_ids).astype(f32).astype(bf16)
        j = i // (TOK // chunk)
        emb = jnp.dot(hit_own, by_slot[j, :N_SLOTS, :], preferred_element_type=f32) + jnp.dot(
            hit_other, by_slot[j, N_SLOTS:, :], preferred_element_type=f32
        )
        emb_ref[rows, :] = emb.astype(bf16)
        inv_rms = lax.rsqrt(jnp.mean(emb * emb, axis=-1, keepdims=True) + norm_eps)
        x_hat = emb * inv_rms
        normed = (x_hat * gain).astype(bf16)
        normed_s[rows, :] = normed
        if i == 0:
            w_in_copy.wait()
        pre = jnp.dot(normed, w_in[...], preferred_element_type=f32) + bias
        square = pre * pre
        tanh_part = jnp.tanh(gelu_coef * (pre + 0.044715 * (square * pre)))
        gate = 0.5 * (1.0 + tanh_part)
        hidden_s[rows, :] = (pre * gate).astype(bf16)
        slope = gate + 0.5 * pre * (1.0 - tanh_part * tanh_part) * (
            gelu_coef + (gelu_coef * 3.0 * 0.044715) * square
        )
        if i == 0:
            for copy in late_copies:
                copy.wait()
        d_act = lax.dot_general(d_out_s[rows, :], w_out[...], nt, preferred_element_type=f32)
        d_pre = d_act * slope
        d_pre_bf = d_pre.astype(bf16)
        d_pre_s[rows, :] = d_pre_bf
        bias_acc[...] += jnp.sum(d_pre.reshape(chunk // 8, 8, HALF), axis=0)
        part = lax.dot_general(d_pre_bf, w_in[...], nt, preferred_element_type=f32)
        send_ref[rows, :] = part.astype(bf16)
        gain_acc[...] += jnp.sum((part * x_hat).reshape(chunk // 8, 8, D), axis=0)

    def one_tile(i, carry):
        cols = pl.ds(pl.multiple_of(i * GIN, GIN), GIN)
        gin_s[:, cols] = lax.dot_general(
            normed_s[...], d_pre_s[:, cols], tn, preferred_element_type=f32
        ).astype(bf16)
        return carry

    lax.fori_loop(0, HALF // GIN, one_tile, 0)
    g_bias = jnp.sum(bias_acc[...], axis=0, keepdims=True)
    g_gain = jnp.sum(gain_acc[...], axis=0, keepdims=True)
    for r in range(HALF // LANES):
        vec_s[r : r + 1, :] = g_bias[:, r * LANES : (r + 1) * LANES]
    for r in range(D // LANES):
        vec_s[8 + r : 9 + r, :] = g_gain[:, r * LANES : (r + 1) * LANES]
    for shift, ref in enumerate(ring_refs):
        to = lax.rem(place[1] + shift, 4)
        cols = pl.ds(pl.multiple_of(to * 256, 256), 256)
        g_out = lax.dot_general(
            hidden_s[:, cols], d_out_s[...], tn, preferred_element_type=f32
        ).astype(bf16)
        for b in range(4):
            rows = pl.ds(pl.multiple_of(to * 128 + b * 32, 32), 32)
            for y in range(N_Y):
                at = b * N_BLOCK + y * 128
                ref[at : at + 64, :] = g_out[b * 64 : b * 64 + 64, y * LANES : (y + 1) * LANES]
                for p in range(2):
                    lane = (y * 2 + p) * LANES
                    ref[at + 64 + p * 32 : at + 96 + p * 32, :] = gin_s[rows, lane : lane + LANES]
        vec = [vec_s[pl.ds(to * 3 + r, 1), :] for r in range(3)] + [jnp.zeros((13, LANES), f32)]
        ref[4 * N_BLOCK :, :] = jnp.concatenate(vec, axis=0).astype(bf16)


def block(place, slot_own, slot_other, got_own, got_other, cot_own, cot_other, gain, w_in, bias, w_out):
    return pl.pallas_call(
        block_kernel,
        in_specs=[SCALARS] + [NEAR] * 4 + [FAR] * 2 + [NEAR, FAR, NEAR, FAR],
        out_specs=[NEAR] * 6,
        scratch_shapes=[
            pltpu.VMEM((2, 2 * N_SLOTS, D), bf16),
            pltpu.VMEM((2 * TOK, D), bf16),
            pltpu.VMEM((2 * TOK, HALF), bf16),
            pltpu.VMEM((2 * TOK, HALF), bf16),
            pltpu.VMEM((8, HALF), f32),
            pltpu.VMEM((8, D), f32),
            pltpu.VMEM((2 * TOK, D), bf16),
            pltpu.VMEM((D, HALF), bf16),
            pltpu.VMEM((16, LANES), f32),
            pltpu.VMEM((D, HALF), bf16),
            pltpu.VMEM((HALF, D), bf16),
            pltpu.SemaphoreType.DMA((4,)),
        ],
        out_shape=[jax.ShapeDtypeStruct((2 * TOK, D), bf16)] * 2
        + [jax.ShapeDtypeStruct((N_RING, LANES), bf16)] * 4,
        compiler_params=params(BLOCK_MIB),
        name="block",
    )(place, slot_own, slot_other, got_own, got_other, cot_own, cot_other, gain, w_in, bias, w_out)


def pack_kernel(slot_ref, part_ref, other_ref, emb_ref, gain_ref, cot_own, cot_other, out_ref):
    gain = gain_ref[...]
    slot_ids = lax.broadcasted_iota(i32, (N_SLOTS, TOK), 0)
    for j in range(2):
        rows = slice(j * TOK, (j + 1) * TOK)
        theirs = slice((1 - j) * TOK, (2 - j) * TOK)
        emb = emb_ref[rows, :].astype(f32)
        inv_rms = lax.rsqrt(jnp.mean(emb * emb, axis=-1, keepdims=True) + norm_eps)
        x_hat = emb * inv_rms
        scaled = (part_ref[rows, :].astype(f32) + other_ref[theirs, :].astype(f32)) * gain
        d_out = (cot_own if j == 0 else cot_other)[...].astype(f32)
        d_embed = (
            inv_rms * (scaled - x_hat * jnp.mean(scaled * x_hat, axis=-1, keepdims=True)) + d_out
        ).astype(bf16)
        hit = (slot_ids == slot_ref[j : j + 1, :]).astype(f32).astype(bf16)
        grads = jnp.dot(hit, d_embed, preferred_element_type=f32).astype(bf16)
        for y in range(N_Y):
            out_ref[:, y, j * CAP : (j + 1) * CAP, :] = grads[
                :, y * LANES : (y + 1) * LANES
            ].reshape(N_XZ, CAP, LANES)


def pack(slot_row, part, other, emb, gain, cot_own, cot_other):
    return pl.pallas_call(
        pack_kernel,
        out_shape=jax.ShapeDtypeStruct((N_XZ, N_Y, PAIR_CAP, LANES), bf16),
        compiler_params=params(32),
        cost_estimate=pl.CostEstimate(flops=2 * 10**9, bytes_accessed=10**7, transcendentals=0),
        name="pack",
    )(slot_row, part, other, emb, gain, cot_own, cot_other)


N_ACC = 8
SCATTER_MIB = 48


def scatter_kernel(asked, arrived_ref, out_ref, grads, *accs):
    zero = jnp.zeros((512, LANES), f32)

    def clear(i, carry):
        rows = pl.ds(pl.multiple_of(i * 512, 512), 512)
        for acc in (out_ref,) + accs:
            acc[rows, :] = zero
        return carry

    lax.fori_loop(0, ROWS // 512, clear, 0)

    def widen(i, carry):
        rows = pl.ds(pl.multiple_of(i * 512, 512), 512)
        grads[rows, :] = arrived_ref[pl.ds(i * 8, 8)].astype(f32).reshape(512, LANES)
        return carry

    lax.fori_loop(0, N_REQ // 512, widen, 0)
    unroll = 8
    share = N_REQ // N_ACC

    def add(i, carry):
        base = pl.multiple_of(i * unroll, unroll)
        for u in range(unroll):
            for a, acc in enumerate((out_ref,) + accs):
                row = base + (a * share + u)
                at = pl.ds(asked[request_at(base) + (a * share * LANES // PAIR_CAP + u)], 1)
                acc[at, :] = acc[at, :] + grads[pl.ds(row, 1), :]
        return carry

    lax.fori_loop(0, share // unroll, add, 0)

    def merge(i, carry):
        rows = pl.ds(pl.multiple_of(i * 512, 512), 512)
        total = out_ref[rows, :]
        for acc in accs:
            total = total + acc[rows, :]
        out_ref[rows, :] = total
        return carry

    lax.fori_loop(0, ROWS // 512, merge, 0)


def scatter_rows(asked, arrived):
    return pl.pallas_call(
        scatter_kernel,
        in_specs=[SCALARS, NEAR],
        out_specs=NEAR,
        scratch_shapes=[pltpu.VMEM((N_REQ, LANES), f32)]
        + [pltpu.VMEM((ROWS, LANES), f32)] * (N_ACC - 1),
        out_shape=jax.ShapeDtypeStruct((ROWS, LANES), f32),
        compiler_params=params(SCATTER_MIB),
        cost_estimate=pl.CostEstimate(flops=10**10, bytes_accessed=10**7, transcendentals=0),
        name="scatter_rows",
    )(asked, arrived)


def ring_add(here, back_1, back_2, back_3, rows):
    first = here[rows, :].astype(f32) + back_2[rows, :].astype(f32)
    return first + (back_1[rows, :].astype(f32) + back_3[rows, :].astype(f32))


def sum_split_kernel(place, here, back_1, back_2, back_3, *outs):
    vec = ring_add(here, back_1, back_2, back_3, slice(4 * N_BLOCK, N_RING)).astype(bf16)
    for shift, out in enumerate(outs):
        to = lax.rem(place[2] + shift, 4)
        for part in range(4):
            step = N_BLOCK // 4
            rows = pl.ds(pl.multiple_of(to * N_BLOCK + part * step, step), step)
            out[part * step : (part + 1) * step, :] = ring_add(
                here, back_1, back_2, back_3, rows
            ).astype(bf16)
        out[N_BLOCK:, :] = vec


def sum_split(place, pieces):
    return pl.pallas_call(
        sum_split_kernel,
        in_specs=[SCALARS] + [NEAR] * 4,
        out_specs=[NEAR] * 4,
        out_shape=[jax.ShapeDtypeStruct((N_BLOCK + N_VEC, LANES), bf16)] * 4,
        compiler_params=params(8),
        cost_estimate=pl.CostEstimate(flops=2*10**9, bytes_accessed=10**6, transcendentals=0),
        name="sum_split",
    )(place, *pieces)


def sum_kernel(here, back_1, back_2, back_3, out):
    n = N_BLOCK + N_VEC
    for at in range(0, n, 88):
        rows = slice(at, min(at + 88, n))
        out[rows, :] = ring_add(here, back_1, back_2, back_3, rows).astype(bf16)


def sum_four(pieces):
    return pl.pallas_call(
        sum_kernel,
        out_shape=jax.ShapeDtypeStruct((N_BLOCK + N_VEC, LANES), bf16),
        compiler_params=params(4),
        cost_estimate=pl.CostEstimate(flops=2*10**9, bytes_accessed=10**6, transcendentals=0),
        name="sum_four",
    )(*pieces)


def join_kernel(here, back_1, back_2, back_3, out):
    for i, ref in enumerate((here, back_1, back_2, back_3)):
        out[i * N_BLOCK : (i + 1) * N_BLOCK, :] = ref[:N_BLOCK, :]
    out[4 * N_BLOCK :, :] = here[N_BLOCK:, :]


def join_four(pieces):
    return pl.pallas_call(
        join_kernel,
        out_shape=jax.ShapeDtypeStruct((N_RING, LANES), bf16),
        compiler_params=params(4),
        cost_estimate=pl.CostEstimate(flops=2*10**9, bytes_accessed=10**6, transcendentals=0),
        name="join_four",
    )(*pieces)


def write_pieces(scale, place, a_at, b_at, pieces, out_ref, in_ref, vec_s):
    for s in range(4):

        @pl.when(pl.program_id(0) == s)
        def _(ref=pieces[s], s=s):
            a = lax.rem(place[a_at] + (4 - s), 4)
            for j in range(4):
                b = lax.rem(place[b_at] + (4 - j), 4)
                rows_out = pl.ds(pl.multiple_of(b * 64, 64), 64)
                rows_in = pl.ds(pl.multiple_of(b * 32, 32), 32)
                for y in range(N_Y):
                    at = j * N_BLOCK + y * 128
                    out_ref[rows_out, y * LANES : (y + 1) * LANES] = (
                        ref[at : at + 64, :].astype(f32) * scale
                    )
                    for p in range(2):
                        lane = (y * 2 + p) * LANES
                        in_ref[rows_in, lane : lane + LANES] = (
                            ref[at + 64 + p * 32 : at + 96 + p * 32, :].astype(f32) * scale
                        )
            vec = ref[4 * N_BLOCK :, :].astype(f32) * scale
            for r in range(3):
                vec_s[pl.ds(a * 3 + r, 1), :] = vec[r : r + 1, :]


def finish_own_kernel(scale, place, *refs):
    write_pieces(scale, place, 1, 2, refs[:4], *refs[4:])


def finish_other_kernel(scale, place, *refs):
    own_vec, out_ref, in_ref, bias_ref, gain_ref, vec_s = refs[4:5] + refs[7:]
    write_pieces(scale, place, 3, 4, refs[:4], out_ref, in_ref, vec_s)

    @pl.when(pl.program_id(0) == 3)
    def _():
        bias_ref[pl.ds(pl.multiple_of(place[0] * 8, 8), 8), :] = own_vec[:8, :]
        bias_ref[pl.ds(pl.multiple_of((1 - place[0]) * 8, 8), 8), :] = vec_s[:8, :]
        gain_ref[...] = own_vec[8:12, :] + vec_s[8:12, :]


def finish(place, own, other, scale):
    results = [
        jax.ShapeDtypeStruct((2 * HALF, D), f32),
        jax.ShapeDtypeStruct((D, 2 * HALF), f32),
    ]
    piece_specs = [whole((N_RING, LANES))] * 4

    def blocks(half_of, a_at):
        def row_of(s, c):
            return lax.rem(c[a_at] + 4 - s, 4)

        return [
            pl.BlockSpec((256, D), lambda s, c: (half_of(c) * 4 + row_of(s, c), 0)),
            pl.BlockSpec((128, HALF), lambda s, c: (row_of(s, c), half_of(c))),
        ]

    g_out, g_in, vec = pl.pallas_call(
        lambda *refs: finish_own_kernel(scale, *refs),
        grid_spec=pltpu.PrefetchScalarGridSpec(
            num_scalar_prefetch=1,
            grid=(4,),
            in_specs=piece_specs,
            out_specs=blocks(lambda c: c[0], 1) + [whole((16, LANES))],
        ),
        out_shape=results + [jax.ShapeDtypeStruct((16, LANES), f32)],
        compiler_params=params(12),
        cost_estimate=pl.CostEstimate(flops=6 * 10**9, bytes_accessed=10**7, transcendentals=0),
        name="finish_own",
    )(place, *own)
    return pl.pallas_call(
        lambda *refs: finish_other_kernel(scale, *refs),
        grid_spec=pltpu.PrefetchScalarGridSpec(
            num_scalar_prefetch=1,
            grid=(4,),
            in_specs=piece_specs + [whole((16, LANES))] + [pl.BlockSpec(memory_space=pl.ANY)] * 2,
            out_specs=blocks(lambda c: 1 - c[0], 3) + [whole((16, LANES)), whole((4, LANES))],
            scratch_shapes=[pltpu.VMEM((16, LANES), f32)],
        ),
        out_shape=results
        + [jax.ShapeDtypeStruct((16, LANES), f32), jax.ShapeDtypeStruct((4, LANES), f32)],
        input_output_aliases={6: 0, 7: 1},
        compiler_params=params(12),
        name="finish_other",
    )(place, *other, vec, g_out, g_in)


def local(table, item_ids, cotangent, norm_gain, w_in, bias_in, w_out):
    core = lax.axis_index("core").astype(i32)
    x, y, z = (lax.axis_index(name).astype(i32) for name in "xyz")
    is_first = core == 0
    place = jnp.stack(
        [
            core,
            jnp.where(is_first, x, y),
            jnp.where(is_first, y, z),
            jnp.where(is_first, y, x),
            jnp.where(is_first, z, y),
        ]
    )
    own_ids = item_ids.reshape(-1)
    cot_own = cotangent.reshape(TOK, D)
    cot_other = swap(cot_own)
    ids = jnp.stack([own_ids, swap(own_ids)])

    owners = ids // ROWS
    offsets = ids - owners * ROWS
    range_ids = jnp.arange(N_XZ * N_CORE, dtype=i32)
    onehot = (owners[:, :, None] == range_ids).astype(bf16)
    tok_ids = jnp.arange(TOK, dtype=i32)
    lower = (tok_ids[:, None] >= tok_ids[None, :]).astype(bf16)
    running = jnp.einsum("ts,jsr->jtr", lower, onehot, preferred_element_type=f32)
    rank = (jnp.sum(running * onehot.astype(f32), axis=2) - 1.0).astype(i32)
    column = owners // 2
    slot = (column % N_Z * N_X + column // N_Z) * CAP + rank
    is_own = owners % 2 == core
    slot_own = jnp.where(is_own, slot, -1)
    slot_other = jnp.where(is_own, -1, slot)
    slot_ids = jnp.arange(N_SLOTS, dtype=i32)
    wanted = jnp.sum(
        jnp.where(slot_own[:, :, None] == slot_ids, offsets[:, :, None], 0), axis=1
    )
    wanted = jnp.transpose(wanted.reshape(2, N_XZ, CAP), (1, 0, 2))
    wanted = jnp.pad(wanted.reshape(N_XZ, 1, PAIR_CAP), ((0, 0), (0, 0), (0, LANES - PAIR_CAP)))
    requests = jnp.broadcast_to(wanted, (N_XZ, N_Y, LANES)).reshape(N_PEERS, 1, LANES)
    requests, cot_other, slot_own, slot_other = lax.optimization_barrier(
        (requests, cot_other, slot_own, slot_other)
    )
    asked = exchange(requests).reshape(-1)
    fetched = exchange(gather_rows(asked, table)).reshape(N_XZ, N_Y, PAIR_CAP, LANES)
    gain_row = norm_gain.reshape(1, D)
    emb, send, *ring = block(
        place,
        slot_own.reshape(2 * TOK, 1),
        slot_other.reshape(2 * TOK, 1),
        fetched,
        swap(fetched),
        cot_own,
        cot_other,
        gain_row,
        w_in,
        bias_in.reshape(1, 2 * HALF),
        w_out,
    )
    other = swap(send)
    ring_got = [along(0, ring[s], s) for s in (1, 2, 3)]
    payload = pack(slot_own, send, other, emb, gain_row, cot_own, cot_other)
    place_late, payload = lax.optimization_barrier((place, payload))
    split = list(sum_split(place_late, ring[:1] + ring_got))
    arrived = exchange(payload.reshape(N_PEERS, PAIR_CAP, LANES))
    mine = sum_four(split[:1] + [along(1, split[s], s) for s in (1, 2, 3)])
    total = sum_four([mine] + [along(2, mine, s) for s in (1, 2, 3)])
    joined = join_four([total] + [along(1, total, s) for s in (1, 2, 3)])
    pieces = [joined] + [along(0, joined, s) for s in (1, 2, 3)]
    table_grad = scatter_rows(asked, arrived)
    *late, table_grad = lax.optimization_barrier((*pieces, table_grad))
    others = [swap(p) for p in late]
    scale = 1.0 / math.sqrt(TOK * N_PEERS * N_CORE)
    g_out, g_in, g_bias, g_gain = finish(place, late, others, scale)
    return (table_grad, g_in, g_bias.reshape(-1), g_out, g_gain.reshape(-1))


def solution(mesh):
    pairs = Mesh(mesh.devices.reshape(N_X, N_Z, N_CORE, N_Y), EVERY)
    rows = ("x", "z", "core")
    return jax.shard_map(
        local,
        mesh=pairs,
        in_specs=(
            P(rows, "y"),
            P(EVERY, None),
            P(EVERY, None, None),
            P(),
            P(),
            P(),
            P(),
        ),
        out_specs=(P(rows, "y"), P(), P(), P(), P()),
        check_vma=False,
    )
```

```python
import math

import jax
import jax.numpy as jnp
from jax import lax
from jax.experimental import pallas as pl
from jax.experimental.pallas import tpu as pltpu
from jax.sharding import Mesh
from jax.sharding import PartitionSpec as P

norm_eps = 1e-06
gelu_coef = 0.7978845608
bf16 = jnp.bfloat16
f32 = jnp.float32
i32 = jnp.int32

N_X, N_Z, N_CORE, N_Y = 4, 4, 2, 4
N_XZ = N_X * N_Z
PEERS = ("x", "z", "y")
N_PEERS = N_XZ * N_Y
EVERY = ("x", "z", "core", "y")

TOK = 512
D = 512
HALF = 1024
LANES = 128
CAP = 32
PAIR_CAP = 2 * CAP
N_SLOTS = N_XZ * CAP
ROWS = 8192
N_REQ = N_PEERS * PAIR_CAP
N_BLOCK = 512
N_VEC = 16
N_RING = 4 * N_BLOCK + N_VEC


def swap(a):
    return lax.ppermute(a, "core", [(0, 1), (1, 0)])


def exchange(a):
    return lax.all_to_all(a, PEERS, split_axis=0, concat_axis=0, tiled=True)


def device(x, z, core, y):
    return ((x * N_Z + z) * N_CORE + core) * N_Y + y


def rings(of_core):
    found = []
    for core in range(N_CORE):
        for i in range(4):
            for j in range(4):
                at = [{"x": (k, i, j), "y": (i, k, j), "z": (i, j, k)}[of_core[core]] for k in range(4)]
                found.append([device(x, z, core, y) for x, y, z in at])
    return found


RING = (rings("xy"), rings("yz"), rings("zx"))


def along(stage, a, shift):
    pairs = [(ring[i], ring[(i + shift) % 4]) for ring in RING[stage] for i in range(4)]
    return lax.ppermute(a, EVERY, pairs)


def params(mib):
    return pltpu.CompilerParams(vmem_limit_bytes=mib << 20)


def whole(shape, space=pltpu.VMEM):
    return pl.BlockSpec(shape, lambda *_: (0,) * len(shape), memory_space=space)


SCALARS = pl.BlockSpec(memory_space=pltpu.SMEM)
NEAR = pl.BlockSpec(memory_space=pltpu.VMEM)
FAR = pl.BlockSpec(memory_space=pltpu.HBM)


GATHER_MIB = 54


def request_at(row):
    return lax.shift_left(lax.shift_right_logical(row, 6), 7) + lax.bitwise_and(row, 63)


def gather_kernel(asked, table_ref, out_ref, near, sems, wide, picked):
    step = ROWS // 8
    copies = [
        pltpu.make_async_copy(
            table_ref.at[pl.ds(i * step, step)], near.at[pl.ds(i * step, step)], sems.at[i]
        )
        for i in range(8)
    ]
    for copy in copies:
        copy.start()
    for i, copy in enumerate(copies):
        copy.wait()
        rows = slice(i * step, (i + 1) * step)
        wide[rows, :] = near[rows, :].astype(f32)

    def pick(i, carry):
        for u in range(PAIR_CAP):
            picked[pl.ds(i * PAIR_CAP + u, 1), :] = wide[pl.ds(asked[i * LANES + u], 1), :]
        rows = pl.ds(pl.multiple_of(i * PAIR_CAP, PAIR_CAP), PAIR_CAP)
        out_ref[i] = picked[rows, :].astype(bf16)
        return carry

    lax.fori_loop(0, N_PEERS, pick, 0)


def gather_rows(asked, table):
    return pl.pallas_call(
        gather_kernel,
        in_specs=[SCALARS, FAR],
        out_specs=NEAR,
        scratch_shapes=[
            pltpu.VMEM((ROWS, LANES), bf16),
            pltpu.SemaphoreType.DMA((8,)),
            pltpu.VMEM((ROWS, LANES), f32),
            pltpu.VMEM((N_REQ, LANES), f32),
        ],
        out_shape=jax.ShapeDtypeStruct((N_PEERS, PAIR_CAP, LANES), bf16),
        compiler_params=params(GATHER_MIB),
        name="gather_rows",
    )(asked, table)


CHUNK = 512
GIN = 1024
BLOCK_MIB = 46


def block_kernel(
    place,
    slot_own,
    slot_other,
    got_own,
    got_other,
    cot_own,
    cot_other,
    gain_ref,
    w_in_far,
    bias_ref,
    w_out_far,
    emb_ref,
    send_ref,
    ring_0,
    ring_1,
    ring_2,
    ring_3,
    by_slot,
    normed_s,
    hidden_s,
    d_pre_s,
    bias_acc,
    gain_acc,
    d_out_s,
    gin_s,
    vec_s,
    w_in,
    w_out,
    sems,
):
    ring_refs = (ring_0, ring_1, ring_2, ring_3)
    own_half = pl.ds(pl.multiple_of(place[0] * HALF, HALF), HALF)
    w_in_copy = pltpu.make_async_copy(w_in_far.at[:, own_half], w_in, sems.at[0])
    late_copies = [
        pltpu.make_async_copy(w_out_far.at[own_half, :], w_out, sems.at[1]),
        pltpu.make_async_copy(cot_own, d_out_s.at[pl.ds(0, TOK)], sems.at[2]),
        pltpu.make_async_copy(cot_other, d_out_s.at[pl.ds(TOK, TOK)], sems.at[3]),
    ]
    w_in_copy.start()
    for copy in late_copies:
        copy.start()
    for j in range(2):
        for y in range(N_Y):
            lanes = slice(y * LANES, (y + 1) * LANES)
            by_slot[j, :N_SLOTS, lanes] = got_own[:, y, j * CAP : (j + 1) * CAP, :].reshape(
                N_SLOTS, LANES
            )
            k = 1 - j
            by_slot[j, N_SLOTS:, lanes] = got_other[:, y, k * CAP : (k + 1) * CAP, :].reshape(
                N_SLOTS, LANES
            )
    bias_acc[...] = jnp.zeros_like(bias_acc)
    gain_acc[...] = jnp.zeros_like(gain_acc)
    gain = gain_ref[...]
    bias = bias_ref[:, own_half]
    chunk = CHUNK
    nt = (((1,), (1,)), ((), ()))
    tn = (((0,), (0,)), ((), ()))
    slot_ids = lax.broadcasted_iota(i32, (chunk, N_SLOTS), 1)

    for i in range(2 * TOK // chunk):
        rows = slice(i * chunk, (i + 1) * chunk)
        hit_own = (slot_own[rows, :] == slot_ids).astype(f32).astype(bf16)
        hit_other = (slot_other[rows, :] == slot_ids).astype(f32).astype(bf16)
        j = i // (TOK // chunk)
        emb = jnp.dot(hit_own, by_slot[j, :N_SLOTS, :], preferred_element_type=f32) + jnp.dot(
            hit_other, by_slot[j, N_SLOTS:, :], preferred_element_type=f32
        )
        emb_ref[rows, :] = emb.astype(bf16)
        inv_rms = lax.rsqrt(jnp.mean(emb * emb, axis=-1, keepdims=True) + norm_eps)
        x_hat = emb * inv_rms
        normed = (x_hat * gain).astype(bf16)
        normed_s[rows, :] = normed
        if i == 0:
            w_in_copy.wait()
        pre = jnp.dot(normed, w_in[...], preferred_element_type=f32) + bias
        square = pre * pre
        tanh_part = jnp.tanh(gelu_coef * (pre + 0.044715 * (square * pre)))
        gate = 0.5 * (1.0 + tanh_part)
        hidden_s[rows, :] = (pre * gate).astype(bf16)
        slope = gate + 0.5 * pre * (1.0 - tanh_part * tanh_part) * (
            gelu_coef + (gelu_coef * 3.0 * 0.044715) * square
        )
        if i == 0:
            for copy in late_copies:
                copy.wait()
        d_act = lax.dot_general(d_out_s[rows, :], w_out[...], nt, preferred_element_type=f32)
        d_pre = d_act * slope
        d_pre_bf = d_pre.astype(bf16)
        d_pre_s[rows, :] = d_pre_bf
        bias_acc[...] += jnp.sum(d_pre.reshape(chunk // 8, 8, HALF), axis=0)
        part = lax.dot_general(d_pre_bf, w_in[...], nt, preferred_element_type=f32)
        send_ref[rows, :] = part.astype(bf16)
        gain_acc[...] += jnp.sum((part * x_hat).reshape(chunk // 8, 8, D), axis=0)

    def one_tile(i, carry):
        cols = pl.ds(pl.multiple_of(i * GIN, GIN), GIN)
        gin_s[:, cols] = lax.dot_general(
            normed_s[...], d_pre_s[:, cols], tn, preferred_element_type=f32
        ).astype(bf16)
        return carry

    lax.fori_loop(0, HALF // GIN, one_tile, 0)
    g_bias = jnp.sum(bias_acc[...], axis=0, keepdims=True)
    g_gain = jnp.sum(gain_acc[...], axis=0, keepdims=True)
    for r in range(HALF // LANES):
        vec_s[r : r + 1, :] = g_bias[:, r * LANES : (r + 1) * LANES]
    for r in range(D // LANES):
        vec_s[8 + r : 9 + r, :] = g_gain[:, r * LANES : (r + 1) * LANES]
    for shift, ref in enumerate(ring_refs):
        to = lax.rem(place[1] + shift, 4)
        cols = pl.ds(pl.multiple_of(to * 256, 256), 256)
        g_out = lax.dot_general(
            hidden_s[:, cols], d_out_s[...], tn, preferred_element_type=f32
        ).astype(bf16)
        for b in range(4):
            rows = pl.ds(pl.multiple_of(to * 128 + b * 32, 32), 32)
            for y in range(N_Y):
                at = b * N_BLOCK + y * 128
                ref[at : at + 64, :] = g_out[b * 64 : b * 64 + 64, y * LANES : (y + 1) * LANES]
                for p in range(2):
                    lane = (y * 2 + p) * LANES
                    ref[at + 64 + p * 32 : at + 96 + p * 32, :] = gin_s[rows, lane : lane + LANES]
        vec = [vec_s[pl.ds(to * 3 + r, 1), :] for r in range(3)] + [jnp.zeros((13, LANES), f32)]
        ref[4 * N_BLOCK :, :] = jnp.concatenate(vec, axis=0).astype(bf16)


def block(place, slot_own, slot_other, got_own, got_other, cot_own, cot_other, gain, w_in, bias, w_out):
    return pl.pallas_call(
        block_kernel,
        in_specs=[SCALARS] + [NEAR] * 4 + [FAR] * 2 + [NEAR, FAR, NEAR, FAR],
        out_specs=[NEAR] * 6,
        scratch_shapes=[
            pltpu.VMEM((2, 2 * N_SLOTS, D), bf16),
            pltpu.VMEM((2 * TOK, D), bf16),
            pltpu.VMEM((2 * TOK, HALF), bf16),
            pltpu.VMEM((2 * TOK, HALF), bf16),
            pltpu.VMEM((8, HALF), f32),
            pltpu.VMEM((8, D), f32),
            pltpu.VMEM((2 * TOK, D), bf16),
            pltpu.VMEM((D, HALF), bf16),
            pltpu.VMEM((16, LANES), f32),
            pltpu.VMEM((D, HALF), bf16),
            pltpu.VMEM((HALF, D), bf16),
            pltpu.SemaphoreType.DMA((4,)),
        ],
        out_shape=[jax.ShapeDtypeStruct((2 * TOK, D), bf16)] * 2
        + [jax.ShapeDtypeStruct((N_RING, LANES), bf16)] * 4,
        compiler_params=params(BLOCK_MIB),
        name="block",
    )(place, slot_own, slot_other, got_own, got_other, cot_own, cot_other, gain, w_in, bias, w_out)


def pack_kernel(slot_ref, part_ref, other_ref, emb_ref, gain_ref, cot_own, cot_other, out_ref):
    gain = gain_ref[...]
    slot_ids = lax.broadcasted_iota(i32, (N_SLOTS, TOK), 0)
    for j in range(2):
        rows = slice(j * TOK, (j + 1) * TOK)
        theirs = slice((1 - j) * TOK, (2 - j) * TOK)
        emb = emb_ref[rows, :].astype(f32)
        inv_rms = lax.rsqrt(jnp.mean(emb * emb, axis=-1, keepdims=True) + norm_eps)
        x_hat = emb * inv_rms
        scaled = (part_ref[rows, :].astype(f32) + other_ref[theirs, :].astype(f32)) * gain
        d_out = (cot_own if j == 0 else cot_other)[...].astype(f32)
        d_embed = (
            inv_rms * (scaled - x_hat * jnp.mean(scaled * x_hat, axis=-1, keepdims=True)) + d_out
        ).astype(bf16)
        hit = (slot_ids == slot_ref[j : j + 1, :]).astype(f32).astype(bf16)
        grads = jnp.dot(hit, d_embed, preferred_element_type=f32).astype(bf16)
        for y in range(N_Y):
            out_ref[:, y, j * CAP : (j + 1) * CAP, :] = grads[
                :, y * LANES : (y + 1) * LANES
            ].reshape(N_XZ, CAP, LANES)


def pack(slot_row, part, other, emb, gain, cot_own, cot_other):
    return pl.pallas_call(
        pack_kernel,
        out_shape=jax.ShapeDtypeStruct((N_XZ, N_Y, PAIR_CAP, LANES), bf16),
        compiler_params=params(32),
        cost_estimate=pl.CostEstimate(flops=2 * 10**9, bytes_accessed=10**7, transcendentals=0),
        name="pack",
    )(slot_row, part, other, emb, gain, cot_own, cot_other)


N_ACC = 8
SCATTER_MIB = 48


def scatter_kernel(asked, arrived_ref, out_ref, grads, *accs):
    zero = jnp.zeros((512, LANES), f32)

    def clear(i, carry):
        rows = pl.ds(pl.multiple_of(i * 512, 512), 512)
        for acc in (out_ref,) + accs:
            acc[rows, :] = zero
        return carry

    lax.fori_loop(0, ROWS // 512, clear, 0)

    def widen(i, carry):
        rows = pl.ds(pl.multiple_of(i * 512, 512), 512)
        grads[rows, :] = arrived_ref[pl.ds(i * 8, 8)].astype(f32).reshape(512, LANES)
        return carry

    lax.fori_loop(0, N_REQ // 512, widen, 0)
    unroll = 8
    share = N_REQ // N_ACC

    def add(i, carry):
        base = pl.multiple_of(i * unroll, unroll)
        for u in range(unroll):
            for a, acc in enumerate((out_ref,) + accs):
                row = base + (a * share + u)
                at = pl.ds(asked[request_at(base) + (a * share * LANES // PAIR_CAP + u)], 1)
                acc[at, :] = acc[at, :] + grads[pl.ds(row, 1), :]
        return carry

    lax.fori_loop(0, share // unroll, add, 0)

    def merge(i, carry):
        rows = pl.ds(pl.multiple_of(i * 512, 512), 512)
        total = out_ref[rows, :]
        for acc in accs:
            total = total + acc[rows, :]
        out_ref[rows, :] = total
        return carry

    lax.fori_loop(0, ROWS // 512, merge, 0)


def scatter_rows(asked, arrived):
    return pl.pallas_call(
        scatter_kernel,
        in_specs=[SCALARS, NEAR],
        out_specs=NEAR,
        scratch_shapes=[pltpu.VMEM((N_REQ, LANES), f32)]
        + [pltpu.VMEM((ROWS, LANES), f32)] * (N_ACC - 1),
        out_shape=jax.ShapeDtypeStruct((ROWS, LANES), f32),
        compiler_params=params(SCATTER_MIB),
        cost_estimate=pl.CostEstimate(flops=10**10, bytes_accessed=10**7, transcendentals=0),
        name="scatter_rows",
    )(asked, arrived)


def ring_add(here, back_1, back_2, back_3, rows):
    first = here[rows, :].astype(f32) + back_2[rows, :].astype(f32)
    return first + (back_1[rows, :].astype(f32) + back_3[rows, :].astype(f32))


def sum_split_kernel(place, here, back_1, back_2, back_3, *outs):
    vec = ring_add(here, back_1, back_2, back_3, slice(4 * N_BLOCK, N_RING)).astype(bf16)
    for shift, out in enumerate(outs):
        to = lax.rem(place[2] + shift, 4)
        for part in range(4):
            step = N_BLOCK // 4
            rows = pl.ds(pl.multiple_of(to * N_BLOCK + part * step, step), step)
            out[part * step : (part + 1) * step, :] = ring_add(
                here, back_1, back_2, back_3, rows
            ).astype(bf16)
        out[N_BLOCK:, :] = vec


def sum_split(place, pieces):
    return pl.pallas_call(
        sum_split_kernel,
        in_specs=[SCALARS] + [NEAR] * 4,
        out_specs=[NEAR] * 4,
        out_shape=[jax.ShapeDtypeStruct((N_BLOCK + N_VEC, LANES), bf16)] * 4,
        compiler_params=params(8),
        cost_estimate=pl.CostEstimate(flops=6 * 10**9, bytes_accessed=10**6, transcendentals=0),
        name="sum_split",
    )(place, *pieces)


def sum_kernel(here, back_1, back_2, back_3, out):
    n = N_BLOCK + N_VEC
    for at in range(0, n, 88):
        rows = slice(at, min(at + 88, n))
        out[rows, :] = ring_add(here, back_1, back_2, back_3, rows).astype(bf16)


def sum_four(pieces):
    return pl.pallas_call(
        sum_kernel,
        out_shape=jax.ShapeDtypeStruct((N_BLOCK + N_VEC, LANES), bf16),
        compiler_params=params(4),
        cost_estimate=pl.CostEstimate(flops=6 * 10**9, bytes_accessed=10**6, transcendentals=0),
        name="sum_four",
    )(*pieces)


def join_kernel(here, back_1, back_2, back_3, out):
    for i, ref in enumerate((here, back_1, back_2, back_3)):
        out[i * N_BLOCK : (i + 1) * N_BLOCK, :] = ref[:N_BLOCK, :]
    out[4 * N_BLOCK :, :] = here[N_BLOCK:, :]


def join_four(pieces):
    return pl.pallas_call(
        join_kernel,
        out_shape=jax.ShapeDtypeStruct((N_RING, LANES), bf16),
        compiler_params=params(4),
        cost_estimate=pl.CostEstimate(flops=6 * 10**9, bytes_accessed=10**6, transcendentals=0),
        name="join_four",
    )(*pieces)


def write_pieces(scale, place, a_at, b_at, pieces, out_ref, in_ref, vec_s):
    for s in range(4):

        @pl.when(pl.program_id(0) == s)
        def _(ref=pieces[s], s=s):
            a = lax.rem(place[a_at] + (4 - s), 4)
            for j in range(4):
                b = lax.rem(place[b_at] + (4 - j), 4)
                rows_out = pl.ds(pl.multiple_of(b * 64, 64), 64)
                rows_in = pl.ds(pl.multiple_of(b * 32, 32), 32)
                for y in range(N_Y):
                    at = j * N_BLOCK + y * 128
                    out_ref[rows_out, y * LANES : (y + 1) * LANES] = (
                        ref[at : at + 64, :].astype(f32) * scale
                    )
                    for p in range(2):
                        lane = (y * 2 + p) * LANES
                        in_ref[rows_in, lane : lane + LANES] = (
                            ref[at + 64 + p * 32 : at + 96 + p * 32, :].astype(f32) * scale
                        )
            vec = ref[4 * N_BLOCK :, :].astype(f32) * scale
            for r in range(3):
                vec_s[pl.ds(a * 3 + r, 1), :] = vec[r : r + 1, :]


def finish_own_kernel(scale, place, *refs):
    write_pieces(scale, place, 1, 2, refs[:4], *refs[4:])


def finish_other_kernel(scale, place, *refs):
    own_vec, out_ref, in_ref, bias_ref, gain_ref, vec_s = refs[4:5] + refs[7:]
    write_pieces(scale, place, 3, 4, refs[:4], out_ref, in_ref, vec_s)

    @pl.when(pl.program_id(0) == 3)
    def _():
        bias_ref[pl.ds(pl.multiple_of(place[0] * 8, 8), 8), :] = own_vec[:8, :]
        bias_ref[pl.ds(pl.multiple_of((1 - place[0]) * 8, 8), 8), :] = vec_s[:8, :]
        gain_ref[...] = own_vec[8:12, :] + vec_s[8:12, :]


def finish(place, own, other, scale):
    results = [
        jax.ShapeDtypeStruct((2 * HALF, D), f32),
        jax.ShapeDtypeStruct((D, 2 * HALF), f32),
    ]
    piece_specs = [whole((N_RING, LANES))] * 4

    def blocks(half_of, a_at):
        def row_of(s, c):
            return lax.rem(c[a_at] + 4 - s, 4)

        return [
            pl.BlockSpec((256, D), lambda s, c: (half_of(c) * 4 + row_of(s, c), 0)),
            pl.BlockSpec((128, HALF), lambda s, c: (row_of(s, c), half_of(c))),
        ]

    g_out, g_in, vec = pl.pallas_call(
        lambda *refs: finish_own_kernel(scale, *refs),
        grid_spec=pltpu.PrefetchScalarGridSpec(
            num_scalar_prefetch=1,
            grid=(4,),
            in_specs=piece_specs,
            out_specs=blocks(lambda c: c[0], 1) + [whole((16, LANES))],
        ),
        out_shape=results + [jax.ShapeDtypeStruct((16, LANES), f32)],
        compiler_params=params(12),
        cost_estimate=pl.CostEstimate(flops=6 * 10**9, bytes_accessed=10**7, transcendentals=0),
        name="finish_own",
    )(place, *own)
    return pl.pallas_call(
        lambda *refs: finish_other_kernel(scale, *refs),
        grid_spec=pltpu.PrefetchScalarGridSpec(
            num_scalar_prefetch=1,
            grid=(4,),
            in_specs=piece_specs + [whole((16, LANES))] + [pl.BlockSpec(memory_space=pl.ANY)] * 2,
            out_specs=blocks(lambda c: 1 - c[0], 3) + [whole((16, LANES)), whole((4, LANES))],
            scratch_shapes=[pltpu.VMEM((16, LANES), f32)],
        ),
        out_shape=results
        + [jax.ShapeDtypeStruct((16, LANES), f32), jax.ShapeDtypeStruct((4, LANES), f32)],
        input_output_aliases={6: 0, 7: 1},
        compiler_params=params(12),
        name="finish_other",
    )(place, *other, vec, g_out, g_in)


def local(table, item_ids, cotangent, norm_gain, w_in, bias_in, w_out):
    core = lax.axis_index("core").astype(i32)
    x, y, z = (lax.axis_index(name).astype(i32) for name in "xyz")
    is_first = core == 0
    place = jnp.stack(
        [
            core,
            jnp.where(is_first, x, y),
            jnp.where(is_first, y, z),
            jnp.where(is_first, y, x),
            jnp.where(is_first, z, y),
        ]
    )
    own_ids = item_ids.reshape(-1)
    cot_own = cotangent.reshape(TOK, D)
    cot_other = swap(cot_own)
    ids = jnp.stack([own_ids, swap(own_ids)])

    owners = ids // ROWS
    offsets = ids - owners * ROWS
    range_ids = jnp.arange(N_XZ * N_CORE, dtype=i32)
    onehot = (owners[:, :, None] == range_ids).astype(bf16)
    tok_ids = jnp.arange(TOK, dtype=i32)
    lower = (tok_ids[:, None] >= tok_ids[None, :]).astype(bf16)
    running = jnp.einsum("ts,jsr->jtr", lower, onehot, preferred_element_type=f32)
    rank = (jnp.sum(running * onehot.astype(f32), axis=2) - 1.0).astype(i32)
    slot = (owners // 2) * CAP + rank
    is_own = owners % 2 == core
    slot_own = jnp.where(is_own, slot, -1)
    slot_other = jnp.where(is_own, -1, slot)
    slot_ids = jnp.arange(N_SLOTS, dtype=i32)
    wanted = jnp.sum(
        jnp.where(slot_own[:, :, None] == slot_ids, offsets[:, :, None], 0), axis=1
    )
    wanted = jnp.transpose(wanted.reshape(2, N_XZ, CAP), (1, 0, 2))
    wanted = jnp.pad(wanted.reshape(N_XZ, 1, PAIR_CAP), ((0, 0), (0, 0), (0, LANES - PAIR_CAP)))
    requests = jnp.broadcast_to(wanted, (N_XZ, N_Y, LANES)).reshape(N_PEERS, 1, LANES)
    requests, cot_other, slot_own, slot_other = lax.optimization_barrier(
        (requests, cot_other, slot_own, slot_other)
    )
    asked = exchange(requests).reshape(-1)
    fetched = exchange(gather_rows(asked, table)).reshape(N_XZ, N_Y, PAIR_CAP, LANES)
    gain_row = norm_gain.reshape(1, D)
    emb, send, *ring = block(
        place,
        slot_own.reshape(2 * TOK, 1),
        slot_other.reshape(2 * TOK, 1),
        fetched,
        swap(fetched),
        cot_own,
        cot_other,
        gain_row,
        w_in,
        bias_in.reshape(1, 2 * HALF),
        w_out,
    )
    other = swap(send)
    ring_got = [along(0, ring[s], s) for s in (1, 2, 3)]
    payload = pack(slot_own, send, other, emb, gain_row, cot_own, cot_other)
    place_late, payload = lax.optimization_barrier((place, payload))
    split = list(sum_split(place_late, ring[:1] + ring_got))
    arrived = exchange(payload.reshape(N_PEERS, PAIR_CAP, LANES))
    mine = sum_four(split[:1] + [along(1, split[s], s) for s in (1, 2, 3)])
    total = sum_four([mine] + [along(2, mine, s) for s in (1, 2, 3)])
    joined = join_four([total] + [along(1, total, s) for s in (1, 2, 3)])
    pieces = [joined] + [along(0, joined, s) for s in (1, 2, 3)]
    table_grad = scatter_rows(asked, arrived)
    *late, table_grad = lax.optimization_barrier((*pieces, table_grad))
    others = [swap(p) for p in late]
    scale = 1.0 / math.sqrt(TOK * N_PEERS * N_CORE)
    g_out, g_in, g_bias, g_gain = finish(place, late, others, scale)
    return (table_grad, g_in, g_bias.reshape(-1), g_out, g_gain.reshape(-1))


def solution(mesh):
    pairs = Mesh(mesh.devices.reshape(N_X, N_Z, N_CORE, N_Y), EVERY)
    rows = ("x", "z", "core")
    return jax.shard_map(
        local,
        mesh=pairs,
        in_specs=(
            P(rows, "y"),
            P(EVERY, None),
            P(EVERY, None, None),
            P(),
            P(),
            P(),
            P(),
        ),
        out_specs=(P(rows, "y"), P(), P(), P(), P()),
        check_vma=False,
    )
```

```python
import math

import jax
import jax.numpy as jnp
from jax import lax
from jax.experimental import pallas as pl
from jax.experimental.pallas import tpu as pltpu
from jax.sharding import Mesh
from jax.sharding import PartitionSpec as P

norm_eps = 1e-06
gelu_coef = 0.7978845608
bf16 = jnp.bfloat16
f32 = jnp.float32
i32 = jnp.int32

N_X, N_Z, N_CORE, N_Y = 4, 4, 2, 4
N_XZ = N_X * N_Z
PEERS = ("x", "z", "y")
N_PEERS = N_XZ * N_Y
EVERY = ("x", "z", "core", "y")

TOK = 512
D = 512
HALF = 1024
LANES = 128
CAP = 32
PAIR_CAP = 2 * CAP
N_SLOTS = N_XZ * CAP
ROWS = 8192
N_REQ = N_PEERS * PAIR_CAP
N_BLOCK = 512
N_VEC = 16
N_RING = 4 * N_BLOCK + N_VEC


def swap(a):
    return lax.ppermute(a, "core", [(0, 1), (1, 0)])


def exchange(a):
    return lax.all_to_all(a, PEERS, split_axis=0, concat_axis=0, tiled=True)


def device(x, z, core, y):
    return ((x * N_Z + z) * N_CORE + core) * N_Y + y


def rings(of_core):
    found = []
    for core in range(N_CORE):
        for i in range(4):
            for j in range(4):
                at = [{"x": (k, i, j), "y": (i, k, j), "z": (i, j, k)}[of_core[core]] for k in range(4)]
                found.append([device(x, z, core, y) for x, y, z in at])
    return found


RING = (rings("xy"), rings("yz"), rings("zx"))


def along(stage, a, shift):
    pairs = [(ring[i], ring[(i + shift) % 4]) for ring in RING[stage] for i in range(4)]
    return lax.ppermute(a, EVERY, pairs)


def params(mib):
    return pltpu.CompilerParams(vmem_limit_bytes=mib << 20)


def whole(shape, space=pltpu.VMEM):
    return pl.BlockSpec(shape, lambda *_: (0,) * len(shape), memory_space=space)


SCALARS = pl.BlockSpec(memory_space=pltpu.SMEM)
NEAR = pl.BlockSpec(memory_space=pltpu.VMEM)
FAR = pl.BlockSpec(memory_space=pltpu.HBM)


GATHER_MIB = 54


def request_at(row):
    return lax.shift_left(lax.shift_right_logical(row, 6), 7) + lax.bitwise_and(row, 63)


def gather_kernel(asked, table_ref, out_ref, near, sems, wide, picked):
    step = ROWS // 8
    copies = [
        pltpu.make_async_copy(
            table_ref.at[pl.ds(i * step, step)], near.at[pl.ds(i * step, step)], sems.at[i]
        )
        for i in range(8)
    ]
    for copy in copies:
        copy.start()
    for i, copy in enumerate(copies):
        copy.wait()
        rows = slice(i * step, (i + 1) * step)
        wide[rows, :] = near[rows, :].astype(f32)

    def pick(i, carry):
        for u in range(PAIR_CAP):
            picked[pl.ds(i * PAIR_CAP + u, 1), :] = wide[pl.ds(asked[i * LANES + u], 1), :]
        rows = pl.ds(pl.multiple_of(i * PAIR_CAP, PAIR_CAP), PAIR_CAP)
        out_ref[i] = picked[rows, :].astype(bf16)
        return carry

    lax.fori_loop(0, N_PEERS, pick, 0)


def gather_rows(asked, table):
    return pl.pallas_call(
        gather_kernel,
        in_specs=[SCALARS, FAR],
        out_specs=NEAR,
        scratch_shapes=[
            pltpu.VMEM((ROWS, LANES), bf16),
            pltpu.SemaphoreType.DMA((8,)),
            pltpu.VMEM((ROWS, LANES), f32),
            pltpu.VMEM((N_REQ, LANES), f32),
        ],
        out_shape=jax.ShapeDtypeStruct((N_PEERS, PAIR_CAP, LANES), bf16),
        compiler_params=params(GATHER_MIB),
        name="gather_rows",
    )(asked, table)


CHUNK = 512
GIN = 1024
BLOCK_MIB = 46


def block_kernel(
    place,
    slot_own,
    slot_other,
    got_own,
    got_other,
    cot_own,
    cot_other,
    gain_ref,
    w_in_far,
    bias_ref,
    w_out_far,
    emb_ref,
    send_ref,
    ring_0,
    ring_1,
    ring_2,
    ring_3,
    by_slot,
    normed_s,
    hidden_s,
    d_pre_s,
    bias_acc,
    gain_acc,
    d_out_s,
    gin_s,
    vec_s,
    w_in,
    w_out,
    sems,
):
    ring_refs = (ring_0, ring_1, ring_2, ring_3)
    own_half = pl.ds(pl.multiple_of(place[0] * HALF, HALF), HALF)
    w_in_copy = pltpu.make_async_copy(w_in_far.at[:, own_half], w_in, sems.at[0])
    late_copies = [
        pltpu.make_async_copy(w_out_far.at[own_half, :], w_out, sems.at[1]),
        pltpu.make_async_copy(cot_own, d_out_s.at[pl.ds(0, TOK)], sems.at[2]),
        pltpu.make_async_copy(cot_other, d_out_s.at[pl.ds(TOK, TOK)], sems.at[3]),
    ]
    w_in_copy.start()
    for copy in late_copies:
        copy.start()
    for j in range(2):
        for y in range(N_Y):
            lanes = slice(y * LANES, (y + 1) * LANES)
            by_slot[j, :N_SLOTS, lanes] = got_own[:, y, j * CAP : (j + 1) * CAP, :].reshape(
                N_SLOTS, LANES
            )
            k = 1 - j
            by_slot[j, N_SLOTS:, lanes] = got_other[:, y, k * CAP : (k + 1) * CAP, :].reshape(
                N_SLOTS, LANES
            )
    bias_acc[...] = jnp.zeros_like(bias_acc)
    gain_acc[...] = jnp.zeros_like(gain_acc)
    gain = gain_ref[...]
    bias = bias_ref[:, own_half]
    chunk = CHUNK
    nt = (((1,), (1,)), ((), ()))
    tn = (((0,), (0,)), ((), ()))
    slot_ids = lax.broadcasted_iota(i32, (chunk, N_SLOTS), 1)

    for i in range(2 * TOK // chunk):
        rows = slice(i * chunk, (i + 1) * chunk)
        hit_own = (slot_own[rows, :] == slot_ids).astype(f32).astype(bf16)
        hit_other = (slot_other[rows, :] == slot_ids).astype(f32).astype(bf16)
        j = i // (TOK // chunk)
        emb = jnp.dot(hit_own, by_slot[j, :N_SLOTS, :], preferred_element_type=f32) + jnp.dot(
            hit_other, by_slot[j, N_SLOTS:, :], preferred_element_type=f32
        )
        emb_ref[rows, :] = emb.astype(bf16)
        inv_rms = lax.rsqrt(jnp.mean(emb * emb, axis=-1, keepdims=True) + norm_eps)
        x_hat = emb * inv_rms
        normed = (x_hat * gain).astype(bf16)
        normed_s[rows, :] = normed
        if i == 0:
            w_in_copy.wait()
        pre = jnp.dot(normed, w_in[...], preferred_element_type=f32) + bias
        square = pre * pre
        tanh_part = jnp.tanh(gelu_coef * (pre + 0.044715 * (square * pre)))
        gate = 0.5 * (1.0 + tanh_part)
        hidden_s[rows, :] = (pre * gate).astype(bf16)
        slope = gate + 0.5 * pre * (1.0 - tanh_part * tanh_part) * (
            gelu_coef + (gelu_coef * 3.0 * 0.044715) * square
        )
        if i == 0:
            for copy in late_copies:
                copy.wait()
        d_act = lax.dot_general(d_out_s[rows, :], w_out[...], nt, preferred_element_type=f32)
        d_pre = d_act * slope
        d_pre_bf = d_pre.astype(bf16)
        d_pre_s[rows, :] = d_pre_bf
        bias_acc[...] += jnp.sum(d_pre.reshape(chunk // 8, 8, HALF), axis=0)
        part = lax.dot_general(d_pre_bf, w_in[...], nt, preferred_element_type=f32)
        send_ref[rows, :] = part.astype(bf16)
        gain_acc[...] += jnp.sum((part * x_hat).reshape(chunk // 8, 8, D), axis=0)

    def one_tile(i, carry):
        cols = pl.ds(pl.multiple_of(i * GIN, GIN), GIN)
        gin_s[:, cols] = lax.dot_general(
            normed_s[...], d_pre_s[:, cols], tn, preferred_element_type=f32
        ).astype(bf16)
        return carry

    lax.fori_loop(0, HALF // GIN, one_tile, 0)
    g_bias = jnp.sum(bias_acc[...], axis=0, keepdims=True)
    g_gain = jnp.sum(gain_acc[...], axis=0, keepdims=True)
    for r in range(HALF // LANES):
        vec_s[r : r + 1, :] = g_bias[:, r * LANES : (r + 1) * LANES]
    for r in range(D // LANES):
        vec_s[8 + r : 9 + r, :] = g_gain[:, r * LANES : (r + 1) * LANES]
    for shift, ref in enumerate(ring_refs):
        to = lax.rem(place[1] + shift, 4)
        cols = pl.ds(pl.multiple_of(to * 256, 256), 256)
        g_out = lax.dot_general(
            hidden_s[:, cols], d_out_s[...], tn, preferred_element_type=f32
        ).astype(bf16)
        for b in range(4):
            rows = pl.ds(pl.multiple_of(to * 128 + b * 32, 32), 32)
            for y in range(N_Y):
                at = b * N_BLOCK + y * 128
                ref[at : at + 64, :] = g_out[b * 64 : b * 64 + 64, y * LANES : (y + 1) * LANES]
                for p in range(2):
                    lane = (y * 2 + p) * LANES
                    ref[at + 64 + p * 32 : at + 96 + p * 32, :] = gin_s[rows, lane : lane + LANES]
        vec = [vec_s[pl.ds(to * 3 + r, 1), :] for r in range(3)] + [jnp.zeros((13, LANES), f32)]
        ref[4 * N_BLOCK :, :] = jnp.concatenate(vec, axis=0).astype(bf16)


def block(place, slot_own, slot_other, got_own, got_other, cot_own, cot_other, gain, w_in, bias, w_out):
    return pl.pallas_call(
        block_kernel,
        in_specs=[SCALARS] + [NEAR] * 4 + [FAR] * 2 + [NEAR, FAR, NEAR, FAR],
        out_specs=[NEAR] * 6,
        scratch_shapes=[
            pltpu.VMEM((2, 2 * N_SLOTS, D), bf16),
            pltpu.VMEM((2 * TOK, D), bf16),
            pltpu.VMEM((2 * TOK, HALF), bf16),
            pltpu.VMEM((2 * TOK, HALF), bf16),
            pltpu.VMEM((8, HALF), f32),
            pltpu.VMEM((8, D), f32),
            pltpu.VMEM((2 * TOK, D), bf16),
            pltpu.VMEM((D, HALF), bf16),
            pltpu.VMEM((16, LANES), f32),
            pltpu.VMEM((D, HALF), bf16),
            pltpu.VMEM((HALF, D), bf16),
            pltpu.SemaphoreType.DMA((4,)),
        ],
        out_shape=[jax.ShapeDtypeStruct((2 * TOK, D), bf16)] * 2
        + [jax.ShapeDtypeStruct((N_RING, LANES), bf16)] * 4,
        compiler_params=params(BLOCK_MIB),
        name="block",
    )(place, slot_own, slot_other, got_own, got_other, cot_own, cot_other, gain, w_in, bias, w_out)


def pack_kernel(slot_ref, part_ref, other_ref, emb_ref, gain_ref, cot_own, cot_other, out_ref):
    gain = gain_ref[...]
    slot_ids = lax.broadcasted_iota(i32, (N_SLOTS, TOK), 0)
    for j in range(2):
        rows = slice(j * TOK, (j + 1) * TOK)
        theirs = slice((1 - j) * TOK, (2 - j) * TOK)
        emb = emb_ref[rows, :].astype(f32)
        inv_rms = lax.rsqrt(jnp.mean(emb * emb, axis=-1, keepdims=True) + norm_eps)
        x_hat = emb * inv_rms
        scaled = (part_ref[rows, :].astype(f32) + other_ref[theirs, :].astype(f32)) * gain
        d_out = (cot_own if j == 0 else cot_other)[...].astype(f32)
        d_embed = (
            inv_rms * (scaled - x_hat * jnp.mean(scaled * x_hat, axis=-1, keepdims=True)) + d_out
        ).astype(bf16)
        hit = (slot_ids == slot_ref[j : j + 1, :]).astype(f32).astype(bf16)
        grads = jnp.dot(hit, d_embed, preferred_element_type=f32).astype(bf16)
        for y in range(N_Y):
            out_ref[:, y, j * CAP : (j + 1) * CAP, :] = grads[
                :, y * LANES : (y + 1) * LANES
            ].reshape(N_XZ, CAP, LANES)


def pack(slot_row, part, other, emb, gain, cot_own, cot_other):
    return pl.pallas_call(
        pack_kernel,
        out_shape=jax.ShapeDtypeStruct((N_XZ, N_Y, PAIR_CAP, LANES), bf16),
        compiler_params=params(32),
        cost_estimate=pl.CostEstimate(flops=2 * 10**9, bytes_accessed=10**7, transcendentals=0),
        name="pack",
    )(slot_row, part, other, emb, gain, cot_own, cot_other)


N_ACC = 8
SCATTER_MIB = 48


def scatter_kernel(asked, arrived_ref, out_ref, grads, *accs):
    zero = jnp.zeros((512, LANES), f32)

    def clear(i, carry):
        rows = pl.ds(pl.multiple_of(i * 512, 512), 512)
        for acc in (out_ref,) + accs:
            acc[rows, :] = zero
        return carry

    lax.fori_loop(0, ROWS // 512, clear, 0)

    def widen(i, carry):
        rows = pl.ds(pl.multiple_of(i * 512, 512), 512)
        grads[rows, :] = arrived_ref[pl.ds(i * 8, 8)].astype(f32).reshape(512, LANES)
        return carry

    lax.fori_loop(0, N_REQ // 512, widen, 0)
    unroll = 8
    share = N_REQ // N_ACC

    def add(i, carry):
        base = pl.multiple_of(i * unroll, unroll)
        for u in range(unroll):
            for a, acc in enumerate((out_ref,) + accs):
                row = base + (a * share + u)
                at = pl.ds(asked[request_at(base) + (a * share * LANES // PAIR_CAP + u)], 1)
                acc[at, :] = acc[at, :] + grads[pl.ds(row, 1), :]
        return carry

    lax.fori_loop(0, share // unroll, add, 0)

    def merge(i, carry):
        rows = pl.ds(pl.multiple_of(i * 512, 512), 512)
        total = out_ref[rows, :]
        for acc in accs:
            total = total + acc[rows, :]
        out_ref[rows, :] = total
        return carry

    lax.fori_loop(0, ROWS // 512, merge, 0)


def scatter_rows(asked, arrived):
    return pl.pallas_call(
        scatter_kernel,
        in_specs=[SCALARS, NEAR],
        out_specs=NEAR,
        scratch_shapes=[pltpu.VMEM((N_REQ, LANES), f32)]
        + [pltpu.VMEM((ROWS, LANES), f32)] * (N_ACC - 1),
        out_shape=jax.ShapeDtypeStruct((ROWS, LANES), f32),
        compiler_params=params(SCATTER_MIB),
        cost_estimate=pl.CostEstimate(flops=10**10, bytes_accessed=10**7, transcendentals=0),
        name="scatter_rows",
    )(asked, arrived)


def ring_add(here, back_1, back_2, back_3, rows):
    first = here[rows, :].astype(f32) + back_2[rows, :].astype(f32)
    return first + (back_1[rows, :].astype(f32) + back_3[rows, :].astype(f32))


def sum_split_kernel(place, here, back_1, back_2, back_3, *outs):
    vec = ring_add(here, back_1, back_2, back_3, slice(4 * N_BLOCK, N_RING)).astype(bf16)
    for shift, out in enumerate(outs):
        to = lax.rem(place[2] + shift, 4)
        for part in range(4):
            step = N_BLOCK // 4
            rows = pl.ds(pl.multiple_of(to * N_BLOCK + part * step, step), step)
            out[part * step : (part + 1) * step, :] = ring_add(
                here, back_1, back_2, back_3, rows
            ).astype(bf16)
        out[N_BLOCK:, :] = vec


def sum_split(place, pieces):
    return pl.pallas_call(
        sum_split_kernel,
        in_specs=[SCALARS] + [NEAR] * 4,
        out_specs=[NEAR] * 4,
        out_shape=[jax.ShapeDtypeStruct((N_BLOCK + N_VEC, LANES), bf16)] * 4,
        compiler_params=params(8),
        cost_estimate=pl.CostEstimate(flops=10 * 10**9, bytes_accessed=10**6, transcendentals=0),
        name="sum_split",
    )(place, *pieces)


def sum_kernel(here, back_1, back_2, back_3, out):
    n = N_BLOCK + N_VEC
    for at in range(0, n, 88):
        rows = slice(at, min(at + 88, n))
        out[rows, :] = ring_add(here, back_1, back_2, back_3, rows).astype(bf16)


def sum_four(pieces):
    return pl.pallas_call(
        sum_kernel,
        out_shape=jax.ShapeDtypeStruct((N_BLOCK + N_VEC, LANES), bf16),
        compiler_params=params(4),
        cost_estimate=pl.CostEstimate(flops=10 * 10**9, bytes_accessed=10**6, transcendentals=0),
        name="sum_four",
    )(*pieces)


def join_kernel(here, back_1, back_2, back_3, out):
    for i, ref in enumerate((here, back_1, back_2, back_3)):
        out[i * N_BLOCK : (i + 1) * N_BLOCK, :] = ref[:N_BLOCK, :]
    out[4 * N_BLOCK :, :] = here[N_BLOCK:, :]


def join_four(pieces):
    return pl.pallas_call(
        join_kernel,
        out_shape=jax.ShapeDtypeStruct((N_RING, LANES), bf16),
        compiler_params=params(4),
        cost_estimate=pl.CostEstimate(flops=10 * 10**9, bytes_accessed=10**6, transcendentals=0),
        name="join_four",
    )(*pieces)


def write_pieces(scale, place, a_at, b_at, pieces, out_ref, in_ref, vec_s):
    for s in range(4):

        @pl.when(pl.program_id(0) == s)
        def _(ref=pieces[s], s=s):
            a = lax.rem(place[a_at] + (4 - s), 4)
            for j in range(4):
                b = lax.rem(place[b_at] + (4 - j), 4)
                rows_out = pl.ds(pl.multiple_of(b * 64, 64), 64)
                rows_in = pl.ds(pl.multiple_of(b * 32, 32), 32)
                for y in range(N_Y):
                    at = j * N_BLOCK + y * 128
                    out_ref[rows_out, y * LANES : (y + 1) * LANES] = (
                        ref[at : at + 64, :].astype(f32) * scale
                    )
                    for p in range(2):
                        lane = (y * 2 + p) * LANES
                        in_ref[rows_in, lane : lane + LANES] = (
                            ref[at + 64 + p * 32 : at + 96 + p * 32, :].astype(f32) * scale
                        )
            vec = ref[4 * N_BLOCK :, :].astype(f32) * scale
            for r in range(3):
                vec_s[pl.ds(a * 3 + r, 1), :] = vec[r : r + 1, :]


def finish_own_kernel(scale, place, *refs):
    write_pieces(scale, place, 1, 2, refs[:4], *refs[4:])


def finish_other_kernel(scale, place, *refs):
    own_vec, out_ref, in_ref, bias_ref, gain_ref, vec_s = refs[4:5] + refs[7:]
    write_pieces(scale, place, 3, 4, refs[:4], out_ref, in_ref, vec_s)

    @pl.when(pl.program_id(0) == 3)
    def _():
        bias_ref[pl.ds(pl.multiple_of(place[0] * 8, 8), 8), :] = own_vec[:8, :]
        bias_ref[pl.ds(pl.multiple_of((1 - place[0]) * 8, 8), 8), :] = vec_s[:8, :]
        gain_ref[...] = own_vec[8:12, :] + vec_s[8:12, :]


def finish(place, own, other, scale):
    results = [
        jax.ShapeDtypeStruct((2 * HALF, D), f32),
        jax.ShapeDtypeStruct((D, 2 * HALF), f32),
    ]
    piece_specs = [whole((N_RING, LANES))] * 4

    def blocks(half_of, a_at):
        def row_of(s, c):
            return lax.rem(c[a_at] + 4 - s, 4)

        return [
            pl.BlockSpec((256, D), lambda s, c: (half_of(c) * 4 + row_of(s, c), 0)),
            pl.BlockSpec((128, HALF), lambda s, c: (row_of(s, c), half_of(c))),
        ]

    g_out, g_in, vec = pl.pallas_call(
        lambda *refs: finish_own_kernel(scale, *refs),
        grid_spec=pltpu.PrefetchScalarGridSpec(
            num_scalar_prefetch=1,
            grid=(4,),
            in_specs=piece_specs,
            out_specs=blocks(lambda c: c[0], 1) + [whole((16, LANES))],
        ),
        out_shape=results + [jax.ShapeDtypeStruct((16, LANES), f32)],
        compiler_params=params(12),
        cost_estimate=pl.CostEstimate(flops=6 * 10**9, bytes_accessed=10**7, transcendentals=0),
        name="finish_own",
    )(place, *own)
    return pl.pallas_call(
        lambda *refs: finish_other_kernel(scale, *refs),
        grid_spec=pltpu.PrefetchScalarGridSpec(
            num_scalar_prefetch=1,
            grid=(4,),
            in_specs=piece_specs + [whole((16, LANES))] + [pl.BlockSpec(memory_space=pl.ANY)] * 2,
            out_specs=blocks(lambda c: 1 - c[0], 3) + [whole((16, LANES)), whole((4, LANES))],
            scratch_shapes=[pltpu.VMEM((16, LANES), f32)],
        ),
        out_shape=results
        + [jax.ShapeDtypeStruct((16, LANES), f32), jax.ShapeDtypeStruct((4, LANES), f32)],
        input_output_aliases={6: 0, 7: 1},
        compiler_params=params(12),
        name="finish_other",
    )(place, *other, vec, g_out, g_in)


def local(table, item_ids, cotangent, norm_gain, w_in, bias_in, w_out):
    core = lax.axis_index("core").astype(i32)
    x, y, z = (lax.axis_index(name).astype(i32) for name in "xyz")
    is_first = core == 0
    place = jnp.stack(
        [
            core,
            jnp.where(is_first, x, y),
            jnp.where(is_first, y, z),
            jnp.where(is_first, y, x),
            jnp.where(is_first, z, y),
        ]
    )
    own_ids = item_ids.reshape(-1)
    cot_own = cotangent.reshape(TOK, D)
    cot_other = swap(cot_own)
    ids = jnp.stack([own_ids, swap(own_ids)])

    owners = ids // ROWS
    offsets = ids - owners * ROWS
    range_ids = jnp.arange(N_XZ * N_CORE, dtype=i32)
    onehot = (owners[:, :, None] == range_ids).astype(bf16)
    tok_ids = jnp.arange(TOK, dtype=i32)
    lower = (tok_ids[:, None] >= tok_ids[None, :]).astype(bf16)
    running = jnp.einsum("ts,jsr->jtr", lower, onehot, preferred_element_type=f32)
    rank = (jnp.sum(running * onehot.astype(f32), axis=2) - 1.0).astype(i32)
    slot = (owners // 2) * CAP + rank
    is_own = owners % 2 == core
    slot_own = jnp.where(is_own, slot, -1)
    slot_other = jnp.where(is_own, -1, slot)
    slot_ids = jnp.arange(N_SLOTS, dtype=i32)
    wanted = jnp.sum(
        jnp.where(slot_own[:, :, None] == slot_ids, offsets[:, :, None], 0), axis=1
    )
    wanted = jnp.transpose(wanted.reshape(2, N_XZ, CAP), (1, 0, 2))
    wanted = jnp.pad(wanted.reshape(N_XZ, 1, PAIR_CAP), ((0, 0), (0, 0), (0, LANES - PAIR_CAP)))
    requests = jnp.broadcast_to(wanted, (N_XZ, N_Y, LANES)).reshape(N_PEERS, 1, LANES)
    requests, cot_other, slot_own, slot_other = lax.optimization_barrier(
        (requests, cot_other, slot_own, slot_other)
    )
    asked = exchange(requests).reshape(-1)
    fetched = exchange(gather_rows(asked, table)).reshape(N_XZ, N_Y, PAIR_CAP, LANES)
    gain_row = norm_gain.reshape(1, D)
    emb, send, *ring = block(
        place,
        slot_own.reshape(2 * TOK, 1),
        slot_other.reshape(2 * TOK, 1),
        fetched,
        swap(fetched),
        cot_own,
        cot_other,
        gain_row,
        w_in,
        bias_in.reshape(1, 2 * HALF),
        w_out,
    )
    other = swap(send)
    ring_got = [along(0, ring[s], s) for s in (1, 2, 3)]
    payload = pack(slot_own, send, other, emb, gain_row, cot_own, cot_other)
    place_late, payload = lax.optimization_barrier((place, payload))
    split = list(sum_split(place_late, ring[:1] + ring_got))
    arrived = exchange(payload.reshape(N_PEERS, PAIR_CAP, LANES))
    mine = sum_four(split[:1] + [along(1, split[s], s) for s in (1, 2, 3)])
    total = sum_four([mine] + [along(2, mine, s) for s in (1, 2, 3)])
    joined = join_four([total] + [along(1, total, s) for s in (1, 2, 3)])
    pieces = [joined] + [along(0, joined, s) for s in (1, 2, 3)]
    table_grad = scatter_rows(asked, arrived)
    *late, table_grad = lax.optimization_barrier((*pieces, table_grad))
    others = [swap(p) for p in late]
    scale = 1.0 / math.sqrt(TOK * N_PEERS * N_CORE)
    g_out, g_in, g_bias, g_gain = finish(place, late, others, scale)
    return (table_grad, g_in, g_bias.reshape(-1), g_out, g_gain.reshape(-1))


def solution(mesh):
    pairs = Mesh(mesh.devices.reshape(N_X, N_Z, N_CORE, N_Y), EVERY)
    rows = ("x", "z", "core")
    return jax.shard_map(
        local,
        mesh=pairs,
        in_specs=(
            P(rows, "y"),
            P(EVERY, None),
            P(EVERY, None, None),
            P(),
            P(),
            P(),
            P(),
        ),
        out_specs=(P(rows, "y"), P(), P(), P(), P()),
        check_vma=False,
    )
```

```python
import math

import jax
import jax.numpy as jnp
from jax import lax
from jax.experimental import pallas as pl
from jax.experimental.pallas import tpu as pltpu
from jax.sharding import Mesh
from jax.sharding import PartitionSpec as P

norm_eps = 1e-06
gelu_coef = 0.7978845608
bf16 = jnp.bfloat16
f32 = jnp.float32
i32 = jnp.int32

N_X, N_Z, N_CORE, N_Y = 4, 4, 2, 4
N_XZ = N_X * N_Z
PEERS = ("x", "z", "y")
N_PEERS = N_XZ * N_Y
EVERY = ("x", "z", "core", "y")

TOK = 512
D = 512
HALF = 1024
LANES = 128
CAP = 32
PAIR_CAP = 2 * CAP
N_SLOTS = N_XZ * CAP
ROWS = 8192
N_REQ = N_PEERS * PAIR_CAP
N_BLOCK = 512
N_VEC = 16
N_RING = 4 * N_BLOCK + N_VEC


def swap(a):
    return lax.ppermute(a, "core", [(0, 1), (1, 0)])


def exchange(a):
    return lax.all_to_all(a, PEERS, split_axis=0, concat_axis=0, tiled=True)


def device(x, z, core, y):
    return ((x * N_Z + z) * N_CORE + core) * N_Y + y


def rings(of_core):
    found = []
    for core in range(N_CORE):
        for i in range(4):
            for j in range(4):
                at = [{"x": (k, i, j), "y": (i, k, j), "z": (i, j, k)}[of_core[core]] for k in range(4)]
                found.append([device(x, z, core, y) for x, y, z in at])
    return found


RING = (rings("xy"), rings("yz"), rings("zx"))


def along(stage, a, shift):
    pairs = [(ring[i], ring[(i + shift) % 4]) for ring in RING[stage] for i in range(4)]
    return lax.ppermute(a, EVERY, pairs)


def params(mib):
    return pltpu.CompilerParams(vmem_limit_bytes=mib << 20)


def whole(shape, space=pltpu.VMEM):
    return pl.BlockSpec(shape, lambda *_: (0,) * len(shape), memory_space=space)


SCALARS = pl.BlockSpec(memory_space=pltpu.SMEM)
NEAR = pl.BlockSpec(memory_space=pltpu.VMEM)
FAR = pl.BlockSpec(memory_space=pltpu.HBM)


GATHER_MIB = 54


def request_at(row):
    return lax.shift_left(lax.shift_right_logical(row, 6), 7) + lax.bitwise_and(row, 63)


def gather_kernel(asked, table_ref, out_ref, near, sems, wide, picked):
    step = ROWS // 8
    copies = [
        pltpu.make_async_copy(
            table_ref.at[pl.ds(i * step, step)], near.at[pl.ds(i * step, step)], sems.at[i]
        )
        for i in range(8)
    ]
    for copy in copies:
        copy.start()
    for i, copy in enumerate(copies):
        copy.wait()
        rows = slice(i * step, (i + 1) * step)
        wide[rows, :] = near[rows, :].astype(f32)

    def pick(i, carry):
        for u in range(PAIR_CAP):
            picked[pl.ds(i * PAIR_CAP + u, 1), :] = wide[pl.ds(asked[i * LANES + u], 1), :]
        rows = pl.ds(pl.multiple_of(i * PAIR_CAP, PAIR_CAP), PAIR_CAP)
        out_ref[i] = picked[rows, :].astype(bf16)
        return carry

    lax.fori_loop(0, N_PEERS, pick, 0)


def gather_rows(asked, table):
    return pl.pallas_call(
        gather_kernel,
        in_specs=[SCALARS, FAR],
        out_specs=NEAR,
        scratch_shapes=[
            pltpu.VMEM((ROWS, LANES), bf16),
            pltpu.SemaphoreType.DMA((8,)),
            pltpu.VMEM((ROWS, LANES), f32),
            pltpu.VMEM((N_REQ, LANES), f32),
        ],
        out_shape=jax.ShapeDtypeStruct((N_PEERS, PAIR_CAP, LANES), bf16),
        compiler_params=params(GATHER_MIB),
        name="gather_rows",
    )(asked, table)


CHUNK = 512
GIN = 1024
BLOCK_MIB = 46


def block_kernel(
    place,
    slot_own,
    slot_other,
    got_own,
    got_other,
    cot_own,
    cot_other,
    gain_ref,
    w_in_far,
    bias_ref,
    w_out_far,
    emb_ref,
    send_ref,
    ring_0,
    ring_1,
    ring_2,
    ring_3,
    by_slot,
    normed_s,
    hidden_s,
    d_pre_s,
    bias_acc,
    gain_acc,
    d_out_s,
    gin_s,
    vec_s,
    w_in,
    w_out,
    sems,
):
    ring_refs = (ring_0, ring_1, ring_2, ring_3)
    own_half = pl.ds(pl.multiple_of(place[0] * HALF, HALF), HALF)
    w_in_copy = pltpu.make_async_copy(w_in_far.at[:, own_half], w_in, sems.at[0])
    late_copies = [
        pltpu.make_async_copy(w_out_far.at[own_half, :], w_out, sems.at[1]),
        pltpu.make_async_copy(cot_own, d_out_s.at[pl.ds(0, TOK)], sems.at[2]),
        pltpu.make_async_copy(cot_other, d_out_s.at[pl.ds(TOK, TOK)], sems.at[3]),
    ]
    w_in_copy.start()
    for copy in late_copies:
        copy.start()
    for j in range(2):
        for y in range(N_Y):
            lanes = slice(y * LANES, (y + 1) * LANES)
            by_slot[j, :N_SLOTS, lanes] = got_own[:, y, j * CAP : (j + 1) * CAP, :].reshape(
                N_SLOTS, LANES
            )
            k = 1 - j
            by_slot[j, N_SLOTS:, lanes] = got_other[:, y, k * CAP : (k + 1) * CAP, :].reshape(
                N_SLOTS, LANES
            )
    bias_acc[...] = jnp.zeros_like(bias_acc)
    gain_acc[...] = jnp.zeros_like(gain_acc)
    gain = gain_ref[...]
    bias = bias_ref[:, own_half]
    chunk = CHUNK
    nt = (((1,), (1,)), ((), ()))
    tn = (((0,), (0,)), ((), ()))
    slot_ids = lax.broadcasted_iota(i32, (chunk, N_SLOTS), 1)

    for i in range(2 * TOK // chunk):
        rows = slice(i * chunk, (i + 1) * chunk)
        hit_own = (slot_own[rows, :] == slot_ids).astype(f32).astype(bf16)
        hit_other = (slot_other[rows, :] == slot_ids).astype(f32).astype(bf16)
        j = i // (TOK // chunk)
        emb = jnp.dot(hit_own, by_slot[j, :N_SLOTS, :], preferred_element_type=f32) + jnp.dot(
            hit_other, by_slot[j, N_SLOTS:, :], preferred_element_type=f32
        )
        emb_ref[rows, :] = emb.astype(bf16)
        inv_rms = lax.rsqrt(jnp.mean(emb * emb, axis=-1, keepdims=True) + norm_eps)
        x_hat = emb * inv_rms
        normed = (x_hat * gain).astype(bf16)
        normed_s[rows, :] = normed
        if i == 0:
            w_in_copy.wait()
        pre = jnp.dot(normed, w_in[...], preferred_element_type=f32) + bias
        square = pre * pre
        tanh_part = jnp.tanh(gelu_coef * (pre + 0.044715 * (square * pre)))
        gate = 0.5 * (1.0 + tanh_part)
        hidden_s[rows, :] = (pre * gate).astype(bf16)
        slope = gate + 0.5 * pre * (1.0 - tanh_part * tanh_part) * (
            gelu_coef + (gelu_coef * 3.0 * 0.044715) * square
        )
        if i == 0:
            for copy in late_copies:
                copy.wait()
        d_act = lax.dot_general(d_out_s[rows, :], w_out[...], nt, preferred_element_type=f32)
        d_pre = d_act * slope
        d_pre_bf = d_pre.astype(bf16)
        d_pre_s[rows, :] = d_pre_bf
        bias_acc[...] += jnp.sum(d_pre.reshape(chunk // 8, 8, HALF), axis=0)
        part = lax.dot_general(d_pre_bf, w_in[...], nt, preferred_element_type=f32)
        send_ref[rows, :] = part.astype(bf16)
        gain_acc[...] += jnp.sum((part * x_hat).reshape(chunk // 8, 8, D), axis=0)

    def one_tile(i, carry):
        cols = pl.ds(pl.multiple_of(i * GIN, GIN), GIN)
        gin_s[:, cols] = lax.dot_general(
            normed_s[...], d_pre_s[:, cols], tn, preferred_element_type=f32
        ).astype(bf16)
        return carry

    lax.fori_loop(0, HALF // GIN, one_tile, 0)
    g_bias = jnp.sum(bias_acc[...], axis=0, keepdims=True)
    g_gain = jnp.sum(gain_acc[...], axis=0, keepdims=True)
    for r in range(HALF // LANES):
        vec_s[r : r + 1, :] = g_bias[:, r * LANES : (r + 1) * LANES]
    for r in range(D // LANES):
        vec_s[8 + r : 9 + r, :] = g_gain[:, r * LANES : (r + 1) * LANES]
    for shift, ref in enumerate(ring_refs):
        to = lax.rem(place[1] + shift, 4)
        cols = pl.ds(pl.multiple_of(to * 256, 256), 256)
        g_out = lax.dot_general(
            hidden_s[:, cols], d_out_s[...], tn, preferred_element_type=f32
        ).astype(bf16)
        for b in range(4):
            rows = pl.ds(pl.multiple_of(to * 128 + b * 32, 32), 32)
            for y in range(N_Y):
                at = b * N_BLOCK + y * 128
                ref[at : at + 64, :] = g_out[b * 64 : b * 64 + 64, y * LANES : (y + 1) * LANES]
                for p in range(2):
                    lane = (y * 2 + p) * LANES
                    ref[at + 64 + p * 32 : at + 96 + p * 32, :] = gin_s[rows, lane : lane + LANES]
        vec = [vec_s[pl.ds(to * 3 + r, 1), :] for r in range(3)] + [jnp.zeros((13, LANES), f32)]
        ref[4 * N_BLOCK :, :] = jnp.concatenate(vec, axis=0).astype(bf16)


def block(place, slot_own, slot_other, got_own, got_other, cot_own, cot_other, gain, w_in, bias, w_out):
    return pl.pallas_call(
        block_kernel,
        in_specs=[SCALARS] + [NEAR] * 4 + [FAR] * 2 + [NEAR, FAR, NEAR, FAR],
        out_specs=[NEAR] * 6,
        scratch_shapes=[
            pltpu.VMEM((2, 2 * N_SLOTS, D), bf16),
            pltpu.VMEM((2 * TOK, D), bf16),
            pltpu.VMEM((2 * TOK, HALF), bf16),
            pltpu.VMEM((2 * TOK, HALF), bf16),
            pltpu.VMEM((8, HALF), f32),
            pltpu.VMEM((8, D), f32),
            pltpu.VMEM((2 * TOK, D), bf16),
            pltpu.VMEM((D, HALF), bf16),
            pltpu.VMEM((16, LANES), f32),
            pltpu.VMEM((D, HALF), bf16),
            pltpu.VMEM((HALF, D), bf16),
            pltpu.SemaphoreType.DMA((4,)),
        ],
        out_shape=[jax.ShapeDtypeStruct((2 * TOK, D), bf16)] * 2
        + [jax.ShapeDtypeStruct((N_RING, LANES), bf16)] * 4,
        compiler_params=params(BLOCK_MIB),
        name="block",
    )(place, slot_own, slot_other, got_own, got_other, cot_own, cot_other, gain, w_in, bias, w_out)


def pack_kernel(slot_ref, part_ref, other_ref, emb_ref, gain_ref, cot_own, cot_other, out_ref):
    gain = gain_ref[...]
    slot_ids = lax.broadcasted_iota(i32, (N_SLOTS, TOK), 0)
    for j in range(2):
        rows = slice(j * TOK, (j + 1) * TOK)
        theirs = slice((1 - j) * TOK, (2 - j) * TOK)
        emb = emb_ref[rows, :].astype(f32)
        inv_rms = lax.rsqrt(jnp.mean(emb * emb, axis=-1, keepdims=True) + norm_eps)
        x_hat = emb * inv_rms
        scaled = (part_ref[rows, :].astype(f32) + other_ref[theirs, :].astype(f32)) * gain
        d_out = (cot_own if j == 0 else cot_other)[...].astype(f32)
        d_embed = (
            inv_rms * (scaled - x_hat * jnp.mean(scaled * x_hat, axis=-1, keepdims=True)) + d_out
        ).astype(bf16)
        hit = (slot_ids == slot_ref[j : j + 1, :]).astype(f32).astype(bf16)
        grads = jnp.dot(hit, d_embed, preferred_element_type=f32).astype(bf16)
        for y in range(N_Y):
            out_ref[:, y, j * CAP : (j + 1) * CAP, :] = grads[
                :, y * LANES : (y + 1) * LANES
            ].reshape(N_XZ, CAP, LANES)


def pack(slot_row, part, other, emb, gain, cot_own, cot_other):
    return pl.pallas_call(
        pack_kernel,
        out_shape=jax.ShapeDtypeStruct((N_XZ, N_Y, PAIR_CAP, LANES), bf16),
        compiler_params=params(32),
        cost_estimate=pl.CostEstimate(flops=2 * 10**9, bytes_accessed=10**7, transcendentals=0),
        name="pack",
    )(slot_row, part, other, emb, gain, cot_own, cot_other)


N_ACC = 8
SCATTER_MIB = 48


def scatter_kernel(asked, arrived_ref, out_ref, grads, *accs):
    zero = jnp.zeros((512, LANES), f32)

    def clear(i, carry):
        rows = pl.ds(pl.multiple_of(i * 512, 512), 512)
        for acc in (out_ref,) + accs:
            acc[rows, :] = zero
        return carry

    lax.fori_loop(0, ROWS // 512, clear, 0)

    def widen(i, carry):
        rows = pl.ds(pl.multiple_of(i * 512, 512), 512)
        grads[rows, :] = arrived_ref[pl.ds(i * 8, 8)].astype(f32).reshape(512, LANES)
        return carry

    lax.fori_loop(0, N_REQ // 512, widen, 0)
    unroll = 8
    share = N_REQ // N_ACC

    def add(i, carry):
        base = pl.multiple_of(i * unroll, unroll)
        for u in range(unroll):
            for a, acc in enumerate((out_ref,) + accs):
                row = base + (a * share + u)
                at = pl.ds(asked[request_at(base) + (a * share * LANES // PAIR_CAP + u)], 1)
                acc[at, :] = acc[at, :] + grads[pl.ds(row, 1), :]
        return carry

    lax.fori_loop(0, share // unroll, add, 0)

    def merge(i, carry):
        rows = pl.ds(pl.multiple_of(i * 512, 512), 512)
        total = out_ref[rows, :]
        for acc in accs:
            total = total + acc[rows, :]
        out_ref[rows, :] = total
        return carry

    lax.fori_loop(0, ROWS // 512, merge, 0)


def scatter_rows(asked, arrived):
    return pl.pallas_call(
        scatter_kernel,
        in_specs=[SCALARS, NEAR],
        out_specs=NEAR,
        scratch_shapes=[pltpu.VMEM((N_REQ, LANES), f32)]
        + [pltpu.VMEM((ROWS, LANES), f32)] * (N_ACC - 1),
        out_shape=jax.ShapeDtypeStruct((ROWS, LANES), f32),
        compiler_params=params(SCATTER_MIB),
        cost_estimate=pl.CostEstimate(flops=10**10, bytes_accessed=10**7, transcendentals=0),
        name="scatter_rows",
    )(asked, arrived)


def ring_add(here, back_1, back_2, back_3, rows):
    first = here[rows, :].astype(f32) + back_2[rows, :].astype(f32)
    return first + (back_1[rows, :].astype(f32) + back_3[rows, :].astype(f32))


def sum_split_kernel(place, here, back_1, back_2, back_3, *outs):
    vec = ring_add(here, back_1, back_2, back_3, slice(4 * N_BLOCK, N_RING)).astype(bf16)
    for shift, out in enumerate(outs):
        to = lax.rem(place[2] + shift, 4)
        for part in range(4):
            step = N_BLOCK // 4
            rows = pl.ds(pl.multiple_of(to * N_BLOCK + part * step, step), step)
            out[part * step : (part + 1) * step, :] = ring_add(
                here, back_1, back_2, back_3, rows
            ).astype(bf16)
        out[N_BLOCK:, :] = vec


def sum_split(place, pieces):
    return pl.pallas_call(
        sum_split_kernel,
        in_specs=[SCALARS] + [NEAR] * 4,
        out_specs=[NEAR] * 4,
        out_shape=[jax.ShapeDtypeStruct((N_BLOCK + N_VEC, LANES), bf16)] * 4,
        compiler_params=params(8),
        cost_estimate=pl.CostEstimate(flops=6 * 10**9, bytes_accessed=10**6, transcendentals=0),
        name="sum_split",
    )(place, *pieces)


def sum_kernel(here, back_1, back_2, back_3, out):
    n = N_BLOCK + N_VEC
    for at in range(0, n, 88):
        rows = slice(at, min(at + 88, n))
        out[rows, :] = ring_add(here, back_1, back_2, back_3, rows).astype(bf16)


def sum_four(pieces):
    return pl.pallas_call(
        sum_kernel,
        out_shape=jax.ShapeDtypeStruct((N_BLOCK + N_VEC, LANES), bf16),
        compiler_params=params(4),
        cost_estimate=pl.CostEstimate(flops=6 * 10**9, bytes_accessed=10**6, transcendentals=0),
        name="sum_four",
    )(*pieces)


def join_kernel(here, back_1, back_2, back_3, out):
    for i, ref in enumerate((here, back_1, back_2, back_3)):
        out[i * N_BLOCK : (i + 1) * N_BLOCK, :] = ref[:N_BLOCK, :]
    out[4 * N_BLOCK :, :] = here[N_BLOCK:, :]


def join_four(pieces):
    return pl.pallas_call(
        join_kernel,
        out_shape=jax.ShapeDtypeStruct((N_RING, LANES), bf16),
        compiler_params=params(4),
        cost_estimate=pl.CostEstimate(flops=6 * 10**9, bytes_accessed=10**6, transcendentals=0),
        name="join_four",
    )(*pieces)


def write_pieces(scale, place, a_at, b_at, shifts, pieces, out_ref, in_ref, vec_s):
    for step, s in enumerate(shifts):

        @pl.when(pl.program_id(0) == step)
        def _(ref=pieces[step], s=s):
            a = lax.rem(place[a_at] + (4 - s), 4)
            for j in range(4):
                b = lax.rem(place[b_at] + (4 - j), 4)
                rows_out = pl.ds(pl.multiple_of(b * 64, 64), 64)
                rows_in = pl.ds(pl.multiple_of(b * 32, 32), 32)
                for y in range(N_Y):
                    at = j * N_BLOCK + y * 128
                    out_ref[rows_out, y * LANES : (y + 1) * LANES] = (
                        ref[at : at + 64, :].astype(f32) * scale
                    )
                    for p in range(2):
                        lane = (y * 2 + p) * LANES
                        in_ref[rows_in, lane : lane + LANES] = (
                            ref[at + 64 + p * 32 : at + 96 + p * 32, :].astype(f32) * scale
                        )
            vec = ref[4 * N_BLOCK :, :].astype(f32) * scale
            for r in range(3):
                vec_s[pl.ds(a * 3 + r, 1), :] = vec[r : r + 1, :]


def finish_first_kernel(scale, place, piece, out_ref, in_ref, vec_ref):
    vec_ref[...] = jnp.zeros_like(vec_ref)
    write_pieces(scale, place, 1, 2, (0,), [piece], out_ref, in_ref, vec_ref)


def finish_own_kernel(scale, place, *refs):
    vec_before, out_ref, in_ref, vec_ref = refs[3:4] + refs[6:]

    @pl.when(pl.program_id(0) == 0)
    def _():
        vec_ref[...] = vec_before[...]

    write_pieces(scale, place, 1, 2, (1, 2, 3), refs[:3], out_ref, in_ref, vec_ref)


def finish_other_kernel(scale, place, *refs):
    own_vec, out_ref, in_ref, bias_ref, gain_ref, vec_s = refs[4:5] + refs[7:]
    write_pieces(scale, place, 3, 4, (0, 1, 2, 3), refs[:4], out_ref, in_ref, vec_s)

    @pl.when(pl.program_id(0) == 3)
    def _():
        bias_ref[pl.ds(pl.multiple_of(place[0] * 8, 8), 8), :] = own_vec[:8, :]
        bias_ref[pl.ds(pl.multiple_of((1 - place[0]) * 8, 8), 8), :] = vec_s[:8, :]
        gain_ref[...] = own_vec[8:12, :] + vec_s[8:12, :]


RESULTS = [
    jax.ShapeDtypeStruct((2 * HALF, D), f32),
    jax.ShapeDtypeStruct((D, 2 * HALF), f32),
]
VECTORS = [jax.ShapeDtypeStruct((16, LANES), f32), jax.ShapeDtypeStruct((4, LANES), f32)]


def finish_part(kernel, name, scale, place, half_of, a_at, first, pieces, before, n_vectors, scratch):
    n = len(pieces)

    def row_of(s, c):
        return lax.rem(c[a_at] + 4 - first - s, 4)

    in_specs = [whole((N_RING, LANES))] * n
    aliases = {}
    if before:
        in_specs += [whole((16, LANES))] + [pl.BlockSpec(memory_space=pl.ANY)] * 2
        aliases = {n + 2: 0, n + 3: 1}
    return pl.pallas_call(
        lambda *refs: kernel(scale, *refs),
        grid_spec=pltpu.PrefetchScalarGridSpec(
            num_scalar_prefetch=1,
            grid=(n,),
            in_specs=in_specs,
            out_specs=[
                pl.BlockSpec((256, D), lambda s, c: (half_of(c) * 4 + row_of(s, c), 0)),
                pl.BlockSpec((128, HALF), lambda s, c: (row_of(s, c), half_of(c))),
            ]
            + [whole(v.shape) for v in VECTORS[:n_vectors]],
            scratch_shapes=scratch,
        ),
        out_shape=RESULTS + VECTORS[:n_vectors],
        input_output_aliases=aliases,
        compiler_params=params(12),
        cost_estimate=pl.CostEstimate(
            flops=n * 15 * 10**8, bytes_accessed=n * 10**6, transcendentals=0
        ),
        name=name,
    )(place, *pieces, *before)


def local(table, item_ids, cotangent, norm_gain, w_in, bias_in, w_out):
    core = lax.axis_index("core").astype(i32)
    x, y, z = (lax.axis_index(name).astype(i32) for name in "xyz")
    is_first = core == 0
    place = jnp.stack(
        [
            core,
            jnp.where(is_first, x, y),
            jnp.where(is_first, y, z),
            jnp.where(is_first, y, x),
            jnp.where(is_first, z, y),
        ]
    )
    own_ids = item_ids.reshape(-1)
    cot_own = cotangent.reshape(TOK, D)
    cot_other = swap(cot_own)
    ids = jnp.stack([own_ids, swap(own_ids)])

    owners = ids // ROWS
    offsets = ids - owners * ROWS
    range_ids = jnp.arange(N_XZ * N_CORE, dtype=i32)
    onehot = (owners[:, :, None] == range_ids).astype(bf16)
    tok_ids = jnp.arange(TOK, dtype=i32)
    lower = (tok_ids[:, None] >= tok_ids[None, :]).astype(bf16)
    running = jnp.einsum("ts,jsr->jtr", lower, onehot, preferred_element_type=f32)
    rank = (jnp.sum(running * onehot.astype(f32), axis=2) - 1.0).astype(i32)
    slot = (owners // 2) * CAP + rank
    is_own = owners % 2 == core
    slot_own = jnp.where(is_own, slot, -1)
    slot_other = jnp.where(is_own, -1, slot)
    slot_ids = jnp.arange(N_SLOTS, dtype=i32)
    wanted = jnp.sum(
        jnp.where(slot_own[:, :, None] == slot_ids, offsets[:, :, None], 0), axis=1
    )
    wanted = jnp.transpose(wanted.reshape(2, N_XZ, CAP), (1, 0, 2))
    wanted = jnp.pad(wanted.reshape(N_XZ, 1, PAIR_CAP), ((0, 0), (0, 0), (0, LANES - PAIR_CAP)))
    requests = jnp.broadcast_to(wanted, (N_XZ, N_Y, LANES)).reshape(N_PEERS, 1, LANES)
    requests, cot_other, slot_own, slot_other = lax.optimization_barrier(
        (requests, cot_other, slot_own, slot_other)
    )
    asked = exchange(requests).reshape(-1)
    fetched = exchange(gather_rows(asked, table)).reshape(N_XZ, N_Y, PAIR_CAP, LANES)
    gain_row = norm_gain.reshape(1, D)
    emb, send, *ring = block(
        place,
        slot_own.reshape(2 * TOK, 1),
        slot_other.reshape(2 * TOK, 1),
        fetched,
        swap(fetched),
        cot_own,
        cot_other,
        gain_row,
        w_in,
        bias_in.reshape(1, 2 * HALF),
        w_out,
    )
    other = swap(send)
    ring_got = [along(0, ring[s], s) for s in (1, 2, 3)]
    payload = pack(slot_own, send, other, emb, gain_row, cot_own, cot_other)
    place_late, payload = lax.optimization_barrier((place, payload))
    split = list(sum_split(place_late, ring[:1] + ring_got))
    arrived = exchange(payload.reshape(N_PEERS, PAIR_CAP, LANES))
    mine = sum_four(split[:1] + [along(1, split[s], s) for s in (1, 2, 3)])
    total = sum_four([mine] + [along(2, mine, s) for s in (1, 2, 3)])
    joined = join_four([total] + [along(1, total, s) for s in (1, 2, 3)])
    pieces = [joined] + [along(0, joined, s) for s in (1, 2, 3)]
    table_grad = scatter_rows(asked, arrived)
    scale = 1.0 / math.sqrt(TOK * N_PEERS * N_CORE)
    other_first = swap(joined)
    g_out, g_in, vec = finish_part(
        finish_first_kernel, "finish_first", scale, place, lambda c: c[0], 1, 0, [joined], (), 1, []
    )
    *late, table_grad, g_out, g_in, vec = lax.optimization_barrier(
        (*pieces[1:], table_grad, g_out, g_in, vec)
    )
    others = [other_first] + [swap(p) for p in late]
    g_out, g_in, vec = finish_part(
        finish_own_kernel, "finish_own", scale, place, lambda c: c[0], 1, 1, late, (vec, g_out, g_in), 1, []
    )
    g_out, g_in, g_bias, g_gain = finish_part(
        finish_other_kernel,
        "finish_other",
        scale,
        place,
        lambda c: 1 - c[0],
        3,
        0,
        others,
        (vec, g_out, g_in),
        2,
        [pltpu.VMEM((16, LANES), f32)],
    )
    return (table_grad, g_in, g_bias.reshape(-1), g_out, g_gain.reshape(-1))


def solution(mesh):
    pairs = Mesh(mesh.devices.reshape(N_X, N_Z, N_CORE, N_Y), EVERY)
    rows = ("x", "z", "core")
    return jax.shard_map(
        local,
        mesh=pairs,
        in_specs=(
            P(rows, "y"),
            P(EVERY, None),
            P(EVERY, None, None),
            P(),
            P(),
            P(),
            P(),
        ),
        out_specs=(P(rows, "y"), P(), P(), P(), P()),
        check_vma=False,
    )
```

```python
import math

import jax
import jax.numpy as jnp
from jax import lax
from jax.experimental import pallas as pl
from jax.experimental.pallas import tpu as pltpu
from jax.sharding import Mesh
from jax.sharding import PartitionSpec as P

norm_eps = 1e-06
gelu_coef = 0.7978845608
bf16 = jnp.bfloat16
f32 = jnp.float32
i32 = jnp.int32

N_X, N_Z, N_CORE, N_Y = 4, 4, 2, 4
N_XZ = N_X * N_Z
PEERS = ("x", "z", "y")
N_PEERS = N_XZ * N_Y
EVERY = ("x", "z", "core", "y")

TOK = 512
D = 512
HALF = 1024
LANES = 128
CAP = 32
PAIR_CAP = 2 * CAP
N_SLOTS = N_XZ * CAP
ROWS = 8192
N_REQ = N_PEERS * PAIR_CAP
N_BLOCK = 512
N_VEC = 16
N_RING = 4 * N_BLOCK + N_VEC


def swap(a):
    return lax.ppermute(a, "core", [(0, 1), (1, 0)])


def exchange(a):
    return lax.all_to_all(a, PEERS, split_axis=0, concat_axis=0, tiled=True)


def device(x, z, core, y):
    return ((x * N_Z + z) * N_CORE + core) * N_Y + y


def rings(of_core):
    found = []
    for core in range(N_CORE):
        for i in range(4):
            for j in range(4):
                at = [{"x": (k, i, j), "y": (i, k, j), "z": (i, j, k)}[of_core[core]] for k in range(4)]
                found.append([device(x, z, core, y) for x, y, z in at])
    return found


RING = (rings("xy"), rings("yz"), rings("zx"))


def along(stage, a, shift):
    pairs = [(ring[i], ring[(i + shift) % 4]) for ring in RING[stage] for i in range(4)]
    return lax.ppermute(a, EVERY, pairs)


def params(mib):
    return pltpu.CompilerParams(vmem_limit_bytes=mib << 20)


def whole(shape, space=pltpu.VMEM):
    return pl.BlockSpec(shape, lambda *_: (0,) * len(shape), memory_space=space)


SCALARS = pl.BlockSpec(memory_space=pltpu.SMEM)
NEAR = pl.BlockSpec(memory_space=pltpu.VMEM)
FAR = pl.BlockSpec(memory_space=pltpu.HBM)


GATHER_MIB = 54


def request_at(row):
    return lax.shift_left(lax.shift_right_logical(row, 6), 7) + lax.bitwise_and(row, 63)


def gather_kernel(asked, table_ref, out_ref, near, sems, wide, picked):
    step = ROWS // 8
    copies = [
        pltpu.make_async_copy(
            table_ref.at[pl.ds(i * step, step)], near.at[pl.ds(i * step, step)], sems.at[i]
        )
        for i in range(8)
    ]
    for copy in copies:
        copy.start()
    for i, copy in enumerate(copies):
        copy.wait()
        rows = slice(i * step, (i + 1) * step)
        wide[rows, :] = near[rows, :].astype(f32)

    def pick(i, carry):
        for u in range(PAIR_CAP):
            picked[pl.ds(i * PAIR_CAP + u, 1), :] = wide[pl.ds(asked[i * LANES + u], 1), :]
        rows = pl.ds(pl.multiple_of(i * PAIR_CAP, PAIR_CAP), PAIR_CAP)
        out_ref[i] = picked[rows, :].astype(bf16)
        return carry

    lax.fori_loop(0, N_PEERS, pick, 0)


def gather_rows(asked, table):
    return pl.pallas_call(
        gather_kernel,
        in_specs=[SCALARS, FAR],
        out_specs=NEAR,
        scratch_shapes=[
            pltpu.VMEM((ROWS, LANES), bf16),
            pltpu.SemaphoreType.DMA((8,)),
            pltpu.VMEM((ROWS, LANES), f32),
            pltpu.VMEM((N_REQ, LANES), f32),
        ],
        out_shape=jax.ShapeDtypeStruct((N_PEERS, PAIR_CAP, LANES), bf16),
        compiler_params=params(GATHER_MIB),
        name="gather_rows",
    )(asked, table)


CHUNK = 512
GIN = 1024
BLOCK_MIB = 46


def block_kernel(
    place,
    slot_own,
    slot_other,
    got_own,
    got_other,
    cot_own,
    cot_other,
    gain_ref,
    w_in_far,
    bias_ref,
    w_out_far,
    emb_ref,
    send_ref,
    ring_0,
    ring_1,
    ring_2,
    ring_3,
    by_slot,
    normed_s,
    hidden_s,
    d_pre_s,
    bias_acc,
    gain_acc,
    d_out_s,
    gin_s,
    vec_s,
    w_in,
    w_out,
    sems,
):
    ring_refs = (ring_0, ring_1, ring_2, ring_3)
    own_half = pl.ds(pl.multiple_of(place[0] * HALF, HALF), HALF)
    w_in_copy = pltpu.make_async_copy(w_in_far.at[:, own_half], w_in, sems.at[0])
    late_copies = [
        pltpu.make_async_copy(w_out_far.at[own_half, :], w_out, sems.at[1]),
        pltpu.make_async_copy(cot_own, d_out_s.at[pl.ds(0, TOK)], sems.at[2]),
        pltpu.make_async_copy(cot_other, d_out_s.at[pl.ds(TOK, TOK)], sems.at[3]),
    ]
    w_in_copy.start()
    for copy in late_copies:
        copy.start()
    for j in range(2):
        for y in range(N_Y):
            lanes = slice(y * LANES, (y + 1) * LANES)
            by_slot[j, :N_SLOTS, lanes] = got_own[:, y, j * CAP : (j + 1) * CAP, :].reshape(
                N_SLOTS, LANES
            )
            k = 1 - j
            by_slot[j, N_SLOTS:, lanes] = got_other[:, y, k * CAP : (k + 1) * CAP, :].reshape(
                N_SLOTS, LANES
            )
    bias_acc[...] = jnp.zeros_like(bias_acc)
    gain_acc[...] = jnp.zeros_like(gain_acc)
    gain = gain_ref[...]
    bias = bias_ref[:, own_half]
    chunk = CHUNK
    nt = (((1,), (1,)), ((), ()))
    tn = (((0,), (0,)), ((), ()))
    slot_ids = lax.broadcasted_iota(i32, (chunk, N_SLOTS), 1)

    for i in range(2 * TOK // chunk):
        rows = slice(i * chunk, (i + 1) * chunk)
        hit_own = (slot_own[rows, :] == slot_ids).astype(f32).astype(bf16)
        hit_other = (slot_other[rows, :] == slot_ids).astype(f32).astype(bf16)
        j = i // (TOK // chunk)
        emb = jnp.dot(hit_own, by_slot[j, :N_SLOTS, :], preferred_element_type=f32) + jnp.dot(
            hit_other, by_slot[j, N_SLOTS:, :], preferred_element_type=f32
        )
        emb_ref[rows, :] = emb.astype(bf16)
        inv_rms = lax.rsqrt(jnp.mean(emb * emb, axis=-1, keepdims=True) + norm_eps)
        x_hat = emb * inv_rms
        normed = (x_hat * gain).astype(bf16)
        normed_s[rows, :] = normed
        if i == 0:
            w_in_copy.wait()
        pre = jnp.dot(normed, w_in[...], preferred_element_type=f32) + bias
        square = pre * pre
        tanh_part = jnp.tanh(gelu_coef * (pre + 0.044715 * (square * pre)))
        gate = 0.5 * (1.0 + tanh_part)
        hidden_s[rows, :] = (pre * gate).astype(bf16)
        slope = gate + 0.5 * pre * (1.0 - tanh_part * tanh_part) * (
            gelu_coef + (gelu_coef * 3.0 * 0.044715) * square
        )
        if i == 0:
            for copy in late_copies:
                copy.wait()
        d_act = lax.dot_general(d_out_s[rows, :], w_out[...], nt, preferred_element_type=f32)
        d_pre = d_act * slope
        d_pre_bf = d_pre.astype(bf16)
        d_pre_s[rows, :] = d_pre_bf
        bias_acc[...] += jnp.sum(d_pre.reshape(chunk // 8, 8, HALF), axis=0)
        part = lax.dot_general(d_pre_bf, w_in[...], nt, preferred_element_type=f32)
        send_ref[rows, :] = part.astype(bf16)
        gain_acc[...] += jnp.sum((part * x_hat).reshape(chunk // 8, 8, D), axis=0)

    def one_tile(i, carry):
        cols = pl.ds(pl.multiple_of(i * GIN, GIN), GIN)
        gin_s[:, cols] = lax.dot_general(
            normed_s[...], d_pre_s[:, cols], tn, preferred_element_type=f32
        ).astype(bf16)
        return carry

    lax.fori_loop(0, HALF // GIN, one_tile, 0)
    g_bias = jnp.sum(bias_acc[...], axis=0, keepdims=True)
    g_gain = jnp.sum(gain_acc[...], axis=0, keepdims=True)
    for r in range(HALF // LANES):
        vec_s[r : r + 1, :] = g_bias[:, r * LANES : (r + 1) * LANES]
    for r in range(D // LANES):
        vec_s[8 + r : 9 + r, :] = g_gain[:, r * LANES : (r + 1) * LANES]
    for shift, ref in enumerate(ring_refs):
        to = lax.rem(place[1] + shift, 4)
        cols = pl.ds(pl.multiple_of(to * 256, 256), 256)
        g_out = lax.dot_general(
            hidden_s[:, cols], d_out_s[...], tn, preferred_element_type=f32
        ).astype(bf16)
        for b in range(4):
            rows = pl.ds(pl.multiple_of(to * 128 + b * 32, 32), 32)
            for y in range(N_Y):
                at = b * N_BLOCK + y * 128
                ref[at : at + 64, :] = g_out[b * 64 : b * 64 + 64, y * LANES : (y + 1) * LANES]
                for p in range(2):
                    lane = (y * 2 + p) * LANES
                    ref[at + 64 + p * 32 : at + 96 + p * 32, :] = gin_s[rows, lane : lane + LANES]
        vec = [vec_s[pl.ds(to * 3 + r, 1), :] for r in range(3)] + [jnp.zeros((13, LANES), f32)]
        ref[4 * N_BLOCK :, :] = jnp.concatenate(vec, axis=0).astype(bf16)


def block(place, slot_own, slot_other, got_own, got_other, cot_own, cot_other, gain, w_in, bias, w_out):
    return pl.pallas_call(
        block_kernel,
        in_specs=[SCALARS] + [NEAR] * 4 + [FAR] * 2 + [NEAR, FAR, NEAR, FAR],
        out_specs=[NEAR] * 6,
        scratch_shapes=[
            pltpu.VMEM((2, 2 * N_SLOTS, D), bf16),
            pltpu.VMEM((2 * TOK, D), bf16),
            pltpu.VMEM((2 * TOK, HALF), bf16),
            pltpu.VMEM((2 * TOK, HALF), bf16),
            pltpu.VMEM((8, HALF), f32),
            pltpu.VMEM((8, D), f32),
            pltpu.VMEM((2 * TOK, D), bf16),
            pltpu.VMEM((D, HALF), bf16),
            pltpu.VMEM((16, LANES), f32),
            pltpu.VMEM((D, HALF), bf16),
            pltpu.VMEM((HALF, D), bf16),
            pltpu.SemaphoreType.DMA((4,)),
        ],
        out_shape=[jax.ShapeDtypeStruct((2 * TOK, D), bf16)] * 2
        + [jax.ShapeDtypeStruct((N_RING, LANES), bf16)] * 4,
        compiler_params=params(BLOCK_MIB),
        name="block",
    )(place, slot_own, slot_other, got_own, got_other, cot_own, cot_other, gain, w_in, bias, w_out)


def pack_kernel(slot_ref, part_ref, other_ref, emb_ref, gain_ref, cot_own, cot_other, out_ref):
    gain = gain_ref[...]
    slot_ids = lax.broadcasted_iota(i32, (N_SLOTS, TOK), 0)
    for j in range(2):
        rows = slice(j * TOK, (j + 1) * TOK)
        theirs = slice((1 - j) * TOK, (2 - j) * TOK)
        emb = emb_ref[rows, :].astype(f32)
        inv_rms = lax.rsqrt(jnp.mean(emb * emb, axis=-1, keepdims=True) + norm_eps)
        x_hat = emb * inv_rms
        scaled = (part_ref[rows, :].astype(f32) + other_ref[theirs, :].astype(f32)) * gain
        d_out = (cot_own if j == 0 else cot_other)[...].astype(f32)
        d_embed = (
            inv_rms * (scaled - x_hat * jnp.mean(scaled * x_hat, axis=-1, keepdims=True)) + d_out
        ).astype(bf16)
        hit = (slot_ids == slot_ref[j : j + 1, :]).astype(f32).astype(bf16)
        grads = jnp.dot(hit, d_embed, preferred_element_type=f32).astype(bf16)
        for y in range(N_Y):
            out_ref[:, y, j * CAP : (j + 1) * CAP, :] = grads[
                :, y * LANES : (y + 1) * LANES
            ].reshape(N_XZ, CAP, LANES)


def pack(slot_row, part, other, emb, gain, cot_own, cot_other):
    return pl.pallas_call(
        pack_kernel,
        out_shape=jax.ShapeDtypeStruct((N_XZ, N_Y, PAIR_CAP, LANES), bf16),
        compiler_params=params(32),
        cost_estimate=pl.CostEstimate(flops=2 * 10**9, bytes_accessed=10**7, transcendentals=0),
        name="pack",
    )(slot_row, part, other, emb, gain, cot_own, cot_other)


N_ACC = 8
SCATTER_MIB = 48


def scatter_kernel(asked, arrived_ref, far_ref, sems, grads, out_ref, *accs):
    zero = jnp.zeros((512, LANES), f32)

    def clear(i, carry):
        rows = pl.ds(pl.multiple_of(i * 512, 512), 512)
        for acc in (out_ref,) + accs:
            acc[rows, :] = zero
        return carry

    lax.fori_loop(0, ROWS // 512, clear, 0)

    def widen(i, carry):
        rows = pl.ds(pl.multiple_of(i * 512, 512), 512)
        grads[rows, :] = arrived_ref[pl.ds(i * 8, 8)].astype(f32).reshape(512, LANES)
        return carry

    lax.fori_loop(0, N_REQ // 512, widen, 0)
    unroll = 8
    share = N_REQ // N_ACC

    def add(i, carry):
        base = pl.multiple_of(i * unroll, unroll)
        for u in range(unroll):
            for a, acc in enumerate((out_ref,) + accs):
                row = base + (a * share + u)
                at = pl.ds(asked[request_at(base) + (a * share * LANES // PAIR_CAP + u)], 1)
                acc[at, :] = acc[at, :] + grads[pl.ds(row, 1), :]
        return carry

    lax.fori_loop(0, share // unroll, add, 0)

    def merge(i, carry):
        rows = pl.ds(pl.multiple_of(i * 512, 512), 512)
        total = out_ref[rows, :]
        for acc in accs:
            total = total + acc[rows, :]
        out_ref[rows, :] = total
        pltpu.make_async_copy(out_ref.at[rows], far_ref.at[rows], sems.at[i]).start()
        return carry

    lax.fori_loop(0, ROWS // 512, merge, 0)

    def finished(i, carry):
        rows = pl.ds(pl.multiple_of(i * 512, 512), 512)
        pltpu.make_async_copy(out_ref.at[rows], far_ref.at[rows], sems.at[i]).wait()
        return carry

    lax.fori_loop(0, ROWS // 512, finished, 0)


def scatter_rows(asked, arrived):
    return pl.pallas_call(
        scatter_kernel,
        in_specs=[SCALARS, NEAR],
        out_specs=FAR,
        scratch_shapes=[pltpu.SemaphoreType.DMA((ROWS // 512,)), pltpu.VMEM((N_REQ, LANES), f32)]
        + [pltpu.VMEM((ROWS, LANES), f32)] * N_ACC,
        out_shape=jax.ShapeDtypeStruct((ROWS, LANES), f32),
        compiler_params=params(SCATTER_MIB),
        cost_estimate=pl.CostEstimate(flops=10**10, bytes_accessed=10**7, transcendentals=0),
        name="scatter_rows",
    )(asked, arrived)


def ring_add(here, back_1, back_2, back_3, rows):
    first = here[rows, :].astype(f32) + back_2[rows, :].astype(f32)
    return first + (back_1[rows, :].astype(f32) + back_3[rows, :].astype(f32))


def sum_split_kernel(place, here, back_1, back_2, back_3, *outs):
    vec = ring_add(here, back_1, back_2, back_3, slice(4 * N_BLOCK, N_RING)).astype(bf16)
    for shift, out in enumerate(outs):
        to = lax.rem(place[2] + shift, 4)
        for part in range(4):
            step = N_BLOCK // 4
            rows = pl.ds(pl.multiple_of(to * N_BLOCK + part * step, step), step)
            out[part * step : (part + 1) * step, :] = ring_add(
                here, back_1, back_2, back_3, rows
            ).astype(bf16)
        out[N_BLOCK:, :] = vec


def sum_split(place, pieces):
    return pl.pallas_call(
        sum_split_kernel,
        in_specs=[SCALARS] + [NEAR] * 4,
        out_specs=[NEAR] * 4,
        out_shape=[jax.ShapeDtypeStruct((N_BLOCK + N_VEC, LANES), bf16)] * 4,
        compiler_params=params(8),
        cost_estimate=pl.CostEstimate(flops=6 * 10**9, bytes_accessed=10**6, transcendentals=0),
        name="sum_split",
    )(place, *pieces)


def sum_kernel(here, back_1, back_2, back_3, out):
    n = N_BLOCK + N_VEC
    for at in range(0, n, 88):
        rows = slice(at, min(at + 88, n))
        out[rows, :] = ring_add(here, back_1, back_2, back_3, rows).astype(bf16)


def sum_four(pieces):
    return pl.pallas_call(
        sum_kernel,
        out_shape=jax.ShapeDtypeStruct((N_BLOCK + N_VEC, LANES), bf16),
        compiler_params=params(4),
        cost_estimate=pl.CostEstimate(flops=6 * 10**9, bytes_accessed=10**6, transcendentals=0),
        name="sum_four",
    )(*pieces)


def join_kernel(here, back_1, back_2, back_3, out):
    for i, ref in enumerate((here, back_1, back_2, back_3)):
        out[i * N_BLOCK : (i + 1) * N_BLOCK, :] = ref[:N_BLOCK, :]
    out[4 * N_BLOCK :, :] = here[N_BLOCK:, :]


def join_four(pieces):
    return pl.pallas_call(
        join_kernel,
        out_shape=jax.ShapeDtypeStruct((N_RING, LANES), bf16),
        compiler_params=params(4),
        cost_estimate=pl.CostEstimate(flops=6 * 10**9, bytes_accessed=10**6, transcendentals=0),
        name="join_four",
    )(*pieces)


def write_pieces(scale, place, a_at, b_at, shifts, pieces, out_ref, in_ref, vec_s):
    for step, s in enumerate(shifts):

        @pl.when(pl.program_id(0) == step)
        def _(ref=pieces[step], s=s):
            a = lax.rem(place[a_at] + (4 - s), 4)
            for j in range(4):
                b = lax.rem(place[b_at] + (4 - j), 4)
                rows_out = pl.ds(pl.multiple_of(b * 64, 64), 64)
                rows_in = pl.ds(pl.multiple_of(b * 32, 32), 32)
                for y in range(N_Y):
                    at = j * N_BLOCK + y * 128
                    out_ref[rows_out, y * LANES : (y + 1) * LANES] = (
                        ref[at : at + 64, :].astype(f32) * scale
                    )
                    for p in range(2):
                        lane = (y * 2 + p) * LANES
                        in_ref[rows_in, lane : lane + LANES] = (
                            ref[at + 64 + p * 32 : at + 96 + p * 32, :].astype(f32) * scale
                        )
            vec = ref[4 * N_BLOCK :, :].astype(f32) * scale
            for r in range(3):
                vec_s[pl.ds(a * 3 + r, 1), :] = vec[r : r + 1, :]


def finish_first_kernel(scale, place, piece, out_ref, in_ref, vec_ref):
    vec_ref[...] = jnp.zeros_like(vec_ref)
    write_pieces(scale, place, 1, 2, (0,), [piece], out_ref, in_ref, vec_ref)


def finish_own_kernel(scale, place, *refs):
    vec_before, out_ref, in_ref, vec_ref = refs[3:4] + refs[6:]

    @pl.when(pl.program_id(0) == 0)
    def _():
        vec_ref[...] = vec_before[...]

    write_pieces(scale, place, 1, 2, (1, 2, 3), refs[:3], out_ref, in_ref, vec_ref)


def finish_other_kernel(scale, place, *refs):
    own_vec, out_ref, in_ref, bias_ref, gain_ref, vec_s = refs[4:5] + refs[7:]
    write_pieces(scale, place, 3, 4, (0, 1, 2, 3), refs[:4], out_ref, in_ref, vec_s)

    @pl.when(pl.program_id(0) == 3)
    def _():
        bias_ref[pl.ds(pl.multiple_of(place[0] * 8, 8), 8), :] = own_vec[:8, :]
        bias_ref[pl.ds(pl.multiple_of((1 - place[0]) * 8, 8), 8), :] = vec_s[:8, :]
        gain_ref[...] = own_vec[8:12, :] + vec_s[8:12, :]


RESULTS = [
    jax.ShapeDtypeStruct((2 * HALF, D), f32),
    jax.ShapeDtypeStruct((D, 2 * HALF), f32),
]
VECTORS = [jax.ShapeDtypeStruct((16, LANES), f32), jax.ShapeDtypeStruct((4, LANES), f32)]


def finish_part(kernel, name, scale, place, half_of, a_at, first, pieces, before, n_vectors, scratch):
    n = len(pieces)

    def row_of(s, c):
        return lax.rem(c[a_at] + 4 - first - s, 4)

    in_specs = [whole((N_RING, LANES))] * n
    aliases = {}
    if before:
        in_specs += [whole((16, LANES))] + [pl.BlockSpec(memory_space=pl.ANY)] * 2
        aliases = {n + 2: 0, n + 3: 1}
    return pl.pallas_call(
        lambda *refs: kernel(scale, *refs),
        grid_spec=pltpu.PrefetchScalarGridSpec(
            num_scalar_prefetch=1,
            grid=(n,),
            in_specs=in_specs,
            out_specs=[
                pl.BlockSpec((256, D), lambda s, c: (half_of(c) * 4 + row_of(s, c), 0)),
                pl.BlockSpec((128, HALF), lambda s, c: (row_of(s, c), half_of(c))),
            ]
            + [whole(v.shape) for v in VECTORS[:n_vectors]],
            scratch_shapes=scratch,
        ),
        out_shape=RESULTS + VECTORS[:n_vectors],
        input_output_aliases=aliases,
        compiler_params=params(12),
        cost_estimate=pl.CostEstimate(
            flops=n * 15 * 10**8, bytes_accessed=n * 10**6, transcendentals=0
        ),
        name=name,
    )(place, *pieces, *before)


def local(table, item_ids, cotangent, norm_gain, w_in, bias_in, w_out):
    core = lax.axis_index("core").astype(i32)
    x, y, z = (lax.axis_index(name).astype(i32) for name in "xyz")
    is_first = core == 0
    place = jnp.stack(
        [
            core,
            jnp.where(is_first, x, y),
            jnp.where(is_first, y, z),
            jnp.where(is_first, y, x),
            jnp.where(is_first, z, y),
        ]
    )
    own_ids = item_ids.reshape(-1)
    cot_own = cotangent.reshape(TOK, D)
    cot_other = swap(cot_own)
    ids = jnp.stack([own_ids, swap(own_ids)])

    owners = ids // ROWS
    offsets = ids - owners * ROWS
    range_ids = jnp.arange(N_XZ * N_CORE, dtype=i32)
    onehot = (owners[:, :, None] == range_ids).astype(bf16)
    tok_ids = jnp.arange(TOK, dtype=i32)
    lower = (tok_ids[:, None] >= tok_ids[None, :]).astype(bf16)
    running = jnp.einsum("ts,jsr->jtr", lower, onehot, preferred_element_type=f32)
    rank = (jnp.sum(running * onehot.astype(f32), axis=2) - 1.0).astype(i32)
    slot = (owners // 2) * CAP + rank
    is_own = owners % 2 == core
    slot_own = jnp.where(is_own, slot, -1)
    slot_other = jnp.where(is_own, -1, slot)
    slot_ids = jnp.arange(N_SLOTS, dtype=i32)
    wanted = jnp.sum(
        jnp.where(slot_own[:, :, None] == slot_ids, offsets[:, :, None], 0), axis=1
    )
    wanted = jnp.transpose(wanted.reshape(2, N_XZ, CAP), (1, 0, 2))
    wanted = jnp.pad(wanted.reshape(N_XZ, 1, PAIR_CAP), ((0, 0), (0, 0), (0, LANES - PAIR_CAP)))
    requests = jnp.broadcast_to(wanted, (N_XZ, N_Y, LANES)).reshape(N_PEERS, 1, LANES)
    requests, cot_other, slot_own, slot_other = lax.optimization_barrier(
        (requests, cot_other, slot_own, slot_other)
    )
    asked = exchange(requests).reshape(-1)
    fetched = exchange(gather_rows(asked, table)).reshape(N_XZ, N_Y, PAIR_CAP, LANES)
    gain_row = norm_gain.reshape(1, D)
    emb, send, *ring = block(
        place,
        slot_own.reshape(2 * TOK, 1),
        slot_other.reshape(2 * TOK, 1),
        fetched,
        swap(fetched),
        cot_own,
        cot_other,
        gain_row,
        w_in,
        bias_in.reshape(1, 2 * HALF),
        w_out,
    )
    other = swap(send)
    ring_got = [along(0, ring[s], s) for s in (1, 2, 3)]
    payload = pack(slot_own, send, other, emb, gain_row, cot_own, cot_other)
    place_late, payload = lax.optimization_barrier((place, payload))
    split = list(sum_split(place_late, ring[:1] + ring_got))
    arrived = exchange(payload.reshape(N_PEERS, PAIR_CAP, LANES))
    mine = sum_four(split[:1] + [along(1, split[s], s) for s in (1, 2, 3)])
    total = sum_four([mine] + [along(2, mine, s) for s in (1, 2, 3)])
    joined = join_four([total] + [along(1, total, s) for s in (1, 2, 3)])
    pieces = [joined] + [along(0, joined, s) for s in (1, 2, 3)]
    table_grad = scatter_rows(asked, arrived)
    scale = 1.0 / math.sqrt(TOK * N_PEERS * N_CORE)
    other_first = swap(joined)
    g_out, g_in, vec = finish_part(
        finish_first_kernel, "finish_first", scale, place, lambda c: c[0], 1, 0, [joined], (), 1, []
    )
    *late, table_grad, g_out, g_in, vec = lax.optimization_barrier(
        (*pieces[1:], table_grad, g_out, g_in, vec)
    )
    others = [other_first] + [swap(p) for p in late]
    g_out, g_in, vec = finish_part(
        finish_own_kernel, "finish_own", scale, place, lambda c: c[0], 1, 1, late, (vec, g_out, g_in), 1, []
    )
    g_out, g_in, g_bias, g_gain = finish_part(
        finish_other_kernel,
        "finish_other",
        scale,
        place,
        lambda c: 1 - c[0],
        3,
        0,
        others,
        (vec, g_out, g_in),
        2,
        [pltpu.VMEM((16, LANES), f32)],
    )
    return (table_grad, g_in, g_bias.reshape(-1), g_out, g_gain.reshape(-1))


def solution(mesh):
    pairs = Mesh(mesh.devices.reshape(N_X, N_Z, N_CORE, N_Y), EVERY)
    rows = ("x", "z", "core")
    return jax.shard_map(
        local,
        mesh=pairs,
        in_specs=(
            P(rows, "y"),
            P(EVERY, None),
            P(EVERY, None, None),
            P(),
            P(),
            P(),
            P(),
        ),
        out_specs=(P(rows, "y"), P(), P(), P(), P()),
        check_vma=False,
    )
```
